256 devices in a mesh: src: 4 (over x), space: 64 (over z, y, core).
Axes of the slice: x: 4, y: 4, z: 8, core: 2. Of those that a mesh axis runs over, the one named last changes fastest.
Arguments:
- contrast: float32 [2, 64, 256, 256], P(None, None, 'space'), may hold values from -0.4 to 0.45
- measured: float32 [4, 2, 256, 256], P('src', None, 'space'), may hold values from -7 to 7
- positions: int32 [4, 2], P('src'), may hold values from 0 to 255
Outputs:
- contrast_sources: float32 [4, 2, 64, 256, 256], P('src', None, None, 'space')
- contrast_new: float32 [2, 64, 256, 256], P(None, None, 'space')
The draws below stay inside these ranges and needn't reach their ends.
All inputs are finite; a program needn't handle non-finite values.
Results may differ from the reference program's by a relative error of at most 0.0003.
Values sent between devices are 32-bit elements; how exact they have to be, the bound alone decides.
A program may use at most 64 MiB of HBM per device.

```python
import math
import jax
import jax.numpy as jnp
from jax import lax

NX = 256
NY = 256
NZ = 64
OUTER = 2
SRCS = 4


def draw_contrast(key, part):
    key_real, key_imag = jax.random.split(jax.random.fold_in(key, 11))
    across = jnp.arange(NX).astype(jnp.float32)
    growth = jnp.sqrt(1.0 + 2.0 * across / (NX - 1))[None, :, None]
    shape = (NZ, NX, NY)
    real_part = growth * jax.random.uniform(key_real, shape, jnp.float32, -0.2, 0.25)
    imag_part = growth * jax.random.uniform(key_imag, shape, jnp.float32, -0.02, 0.07)
    return jnp.stack([real_part, imag_part], axis=0)


def draw_measured(key, part):
    shape = (SRCS, 2, NX, NY)
    across = jnp.arange(NX).astype(jnp.float32)
    growth = jnp.sqrt(1.0 + 2.0 * across / (NX - 1))[None, None, :, None]
    values = jnp.clip(jax.random.normal(jax.random.fold_in(key, 23), shape, jnp.float32), -4.0, 4.0)
    return values * growth


def set_ends(values, own_key, low, high):
    shape = values.shape
    spot = [jax.random.randint(jax.random.fold_in(own_key, axis), (), 0, shape[axis]) for axis in range(len(shape))]
    values = values.at[tuple(spot)].set(low)
    longest = shape.index(max(shape))
    spot[longest] = (spot[longest] + 1) % shape[longest]
    return values.at[tuple(spot)].set(high)


def setup_inputs(seed: int = 0) -> dict:
    splits = jax.random.split(jax.random.key(seed), 4)
    contrast = draw_contrast(jax.random.fold_in(splits[3], 71), 0)
    measured = draw_measured(jax.random.fold_in(splits[3], 71), 0)
    positions = set_ends(jax.random.randint(splits[2], (SRCS, 2), 0, NX), jax.random.fold_in(splits[2], 1), 0, NX - 1).astype(jnp.int32)
    return {"contrast": contrast, "measured": measured, "positions": positions}


WAVENUMBER = 2.0 * math.pi / 6.0
DAMPING = 0.3
SOURCE_GAP = 8.0
FLOOR_SHARE = 0.75
REAL_LOW = -0.25
REAL_HIGH = 0.35
IMAG_HIGH = 0.1

def laplace_modes(start_mode, length, total):
    mode_index = (start_mode + jnp.arange(length)).astype(jnp.float32)
    half_sine = jnp.sin(math.pi * mode_index / total)
    return 4.0 * half_sine * half_sine

def green_spectrum(depth_modes, first_modes, second_modes):
    eigen = depth_modes[:, None, None] + first_modes[None, :, None] + second_modes[None, None, :]
    wave_sq = WAVENUMBER * WAVENUMBER
    real_den = eigen - wave_sq
    imag_den = wave_sq * DAMPING
    factor = wave_sq / (real_den * real_den + imag_den * imag_den)
    return (factor * real_den, factor * imag_den)

def incident(positions, start_row, row_count):
    heights = jnp.arange(NZ).astype(jnp.float32) + SOURCE_GAP
    across = (start_row + jnp.arange(row_count)).astype(jnp.float32)
    along_y = jnp.arange(NY).astype(jnp.float32)
    source_x = positions[:, 0].astype(jnp.float32)
    source_y = positions[:, 1].astype(jnp.float32)
    offset_x = across[None, :] - source_x[:, None]
    offset_y = along_y[None, :] - source_y[:, None]
    dist_sq = heights[None, :, None, None] * heights[None, :, None, None] + offset_x[:, None, :, None] * offset_x[:, None, :, None]
    dist_sq = dist_sq + offset_y[:, None, None, :] * offset_y[:, None, None, :]
    phases = WAVENUMBER * jnp.sqrt(dist_sq)
    return (jnp.cos(phases), jnp.sin(phases))

def squared_magnitude(values):
    return values.real * values.real + values.imag * values.imag

def reference(contrast, measured, positions):
    chi = contrast[0] + 1j * contrast[1]
    inc_real, inc_imag = incident(positions, 0, NX)
    incident_field = inc_real + 1j * inc_imag
    data_field = measured[:, 0] + 1j * measured[:, 1]
    green_real, green_imag = green_spectrum(laplace_modes(0, NZ, NZ), laplace_modes(0, NX, NX), laplace_modes(0, NY, NY))
    green = green_real + 1j * green_imag

    def convolve(field, kernel):
        return jnp.fft.ifftn(kernel[None] * jnp.fft.fftn(field, axes=(1, 2, 3)), axes=(1, 2, 3))
    sources_field = chi[None] * incident_field
    scattered = convolve(sources_field, green)
    data_total = jnp.sum(squared_magnitude(data_field))
    for outer_step in range(OUTER):
        object_total = jnp.sum(squared_magnitude(chi[None] * incident_field))
        data_weight = 1.0 / data_total
        object_weight = 1.0 / object_total
        total_field = incident_field + scattered
        residual = chi[None] * total_field - sources_field
        data_residual = data_field - scattered[:, 0]
        adjoint_input = -object_weight * jnp.conj(chi)[None] * residual
        adjoint_input = adjoint_input.at[:, 0].add(data_weight * data_residual)
        descent = object_weight * residual + convolve(adjoint_input, jnp.conj(green))
        descent_image = convolve(descent, green)
        change = descent - chi[None] * descent_image
        step_length = jnp.sum(squared_magnitude(descent)) / (data_weight * jnp.sum(squared_magnitude(descent_image[:, 0])) + object_weight * jnp.sum(squared_magnitude(change)))
        sources_field = sources_field + step_length * descent
        scattered = scattered + step_length * descent_image
        total_field = incident_field + scattered
        numerator = lax.optimization_barrier(jnp.sum(sources_field * jnp.conj(total_field), axis=0))
        power_sum = lax.optimization_barrier(jnp.sum(squared_magnitude(total_field), axis=0))
        floored = jnp.maximum(power_sum, FLOOR_SHARE * SRCS)
        chi_real = jnp.clip(numerator.real / floored, REAL_LOW, REAL_HIGH)
        chi_imag = jnp.clip(numerator.imag / floored, 0.0, IMAG_HIGH)
        chi = chi_real + 1j * chi_imag
    return (jnp.stack([sources_field.real, sources_field.imag], axis=1), jnp.stack([chi.real, chi.imag], axis=0))
```

```python
import functools
import math

import jax
import jax.numpy as jnp
import ml_dtypes
import numpy as np
from jax import lax
from jax.experimental import pallas as pl
from jax.experimental.pallas import tpu as pltpu
from jax.sharding import PartitionSpec as P

OUTER = 2
WAVENUMBER = 2.0 * math.pi / 6.0
DAMPING = 0.3
SOURCE_GAP = 8.0
FLOOR_SHARE = 0.75
REAL_LOW = -0.25
REAL_HIGH = 0.35
IMAG_HIGH = 0.1
F32 = jnp.float32
BF16 = jnp.bfloat16
MESH = pl.DeviceIdType.MESH


def hartley(length):
    turn = np.outer(np.arange(length), np.arange(length)) % length
    angle = 2.0 * np.pi / length * turn
    return (np.cos(angle) + np.sin(angle)) / np.sqrt(length)


def high_low(table):
    high = table.astype(ml_dtypes.bfloat16)
    low = (table - high.astype(np.float64)).astype(ml_dtypes.bfloat16)
    return np.stack([high, low])


def modes(length):
    return 4.0 * np.sin(np.pi * np.arange(length) / length) ** 2


def decay_tables(depth, across):
    wave_sq = WAVENUMBER * WAVENUMBER
    trace = 2.0 + modes(depth)[:, None] + modes(across)[None, :] - wave_sq * (1.0 + 1j * DAMPING)
    root = np.sqrt(trace * trace - 4.0)
    first = (trace - root) / 2.0
    second = (trace + root) / 2.0
    small = np.where(np.abs(first) < np.abs(second), first, second)
    large = np.where(np.abs(first) < np.abs(second), second, first)
    small = 1.0 / large
    kappa = wave_sq / (large - small)
    tables = np.stack([small.real, small.imag, kappa.real, kappa.imag])
    return tables.astype(np.float32)


def cmul(a, b):
    return (a[0] * b[0] - a[1] * b[1], a[0] * b[1] + a[1] * b[0])


def cmadd(a, b, c):
    return (a[0] * b[0] - a[1] * b[1] + c[0], a[0] * b[1] + a[1] * b[0] + c[1])


def half_turn(fraction):
    angle = fraction * math.pi
    sq = angle * angle
    sine = jnp.full_like(sq, -1.0 / math.factorial(11))
    for order in (9, 7, 5, 3, 1):
        sine = sine * sq + (1.0 if order % 4 == 1 else -1.0) / math.factorial(order)
    cosine = jnp.full_like(sq, 1.0 / math.factorial(12))
    for order in (10, 8, 6, 4, 2, 0):
        cosine = cosine * sq + (1.0 if order % 4 == 0 else -1.0) / math.factorial(order)
    return sine * angle, cosine


def kernel(
    cfg,
    pos_ref, chi0_ref, meas_ref, tab_ref, hy_ref, hz_ref,
    w_ref, chi_out_ref,
    chi1_ref, e_ref, s_ref, r_ref, d_ref, v_ref, sp_ref, np_ref, np_recv,
    send1, send3, recv1, recv2, recv3, red1, red2,
    ex_send, ex_recv, red_send, red_recv, x_send, x_recv,
):
    ns, g1, g2, nz, ny, rows = cfg
    halves = ny // 128
    nx = g1 * g2 * rows
    zgroups = nz // 8
    src = lax.axis_index("src")
    space = lax.axis_index("space")
    m = lax.rem(space, g1)
    grp = space // g1
    base = grp * g1

    barrier = pltpu.get_barrier_semaphore()

    def greet_group(k, carry):
        pl.semaphore_signal(barrier, inc=1, device_id=(src, base + lax.rem(m + k, g1)), device_id_type=MESH)
        return carry

    def cross_peer(k):
        return lax.rem(src + k // g2, ns), lax.rem(grp + lax.rem(k, g2), g2) * g1 + m

    def greet_cross(k, carry):
        pl.semaphore_signal(barrier, inc=1, device_id=cross_peer(k), device_id_type=MESH)
        return carry

    lax.fori_loop(1, g1, greet_group, 0)
    lax.fori_loop(1, ns * g2, greet_cross, 0)

    def remote(src_ref, dst_ref, send_sem, recv_sem, device):
        return pltpu.make_async_remote_copy(
            src_ref=src_ref, dst_ref=dst_ref, send_sem=send_sem, recv_sem=recv_sem,
            device_id=device, device_id_type=MESH,
        )

    def take(ref, sem):
        pltpu.make_async_copy(ref, ref, sem).wait()

    def reduce_start(a, parts):
        red1[a, 0] = jnp.concatenate(parts + [jnp.zeros((8 - len(parts), 128), F32)], axis=0)

        def send(k, carry):
            remote(red1.at[a, 0], red1.at[a, k], red_send.at[a, 0], red_recv.at[a, 0],
                   (src, base + lax.rem(m + k, g1))).start()
            return carry

        lax.fori_loop(1, g1, send, 0)

    def reduce_middle(a):
        take(red1.at[a, pl.ds(1, g1 - 1)], red_recv.at[a, 0])

        def add(j, total):
            return total + red1[a, lax.rem(m - j + g1, g1)]

        red2[a, 0] = lax.fori_loop(0, g1, add, jnp.zeros((8, 128), F32), unroll=True)
        take(red1.at[a, pl.ds(1, g1 - 1)], red_send.at[a, 0])

        def send(k, carry):
            remote(red2.at[a, 0], red2.at[a, k], red_send.at[a, 1], red_recv.at[a, 1], cross_peer(k)).start()
            return carry

        lax.fori_loop(1, ns * g2, send, 0)

    def reduce_end(a):
        count = ns * g2
        take(red2.at[a, pl.ds(1, count - 1)], red_recv.at[a, 1])

        def add(j, total):
            slot = lax.rem(src - j // g2 + ns, ns) * g2 + lax.rem(grp - lax.rem(j, g2) + g2, g2)
            return total + red2[a, slot]

        total = lax.fori_loop(0, count, add, jnp.zeros((8, 128), F32), unroll=True)
        take(red2.at[a, pl.ds(1, count - 1)], red_send.at[a, 1])
        return jnp.sum(total, axis=1, keepdims=True)

    def fold(acc):
        part = acc[:, :128]
        for h in range(1, halves):
            part = part + acc[:, h * 128:(h + 1) * 128]
        return jnp.sum(part, axis=0, keepdims=True)

    def split(a):
        high = a.astype(BF16)
        return high, (a - high.astype(F32)).astype(BF16)

    def dot3(a, b):
        mm = functools.partial(jnp.dot, preferred_element_type=F32)
        return mm(a[0], b[0]) + (mm(a[1], b[0]) + mm(a[0], b[1]))

    def local(src_ref, dst_ref):
        hz = (hz_ref[0], hz_ref[1])
        hy = (hy_ref[0], hy_ref[1])
        for pair in range(rows // 2):
            block = src_ref[pl.ds(2 * pair, 2)].reshape(4 * nz, ny)
            depth_done = dot3(hz, split(block))
            done = dot3(split(depth_done), hy)
            dst_ref[pl.ds(2 * pair, 2)] = done.reshape(2, 2 * nz, ny)

    def tile(ref, lead, part, comp):
        z = pl.multiple_of(part // halves * 8, 8)
        y = pl.multiple_of(lax.rem(part, halves) * 128, 128)
        return ref.at[lead, pl.ds(comp * nz + z, 8), pl.ds(y, 128)]

    def ctable(part, which):
        z = pl.multiple_of(part // halves * 8, 8)
        y = pl.multiple_of(lax.rem(part, halves) * 128, 128)
        return tuple(tab_ref[2 * which + c, pl.ds(z, 8), pl.ds(y, 128)] for c in range(2))

    def spectral(lead, part):
        return (tile(sp_ref, lead, part, 0)[...], tile(sp_ref, lead, part, 1)[...])

    def sweep_out(t):
        def summarise(part):
            root = ctable(part, 0)
            rowv = [spectral(i, part) for i in range(rows)]
            ahead = rowv[0]
            for i in range(1, rows):
                ahead = cmadd(ahead, root, rowv[i])
            behind = rowv[rows - 1]
            for i in range(rows - 2, -1, -1):
                behind = cmadd(behind, root, rowv[i])
            return ahead + behind

        def step(k, carry):
            peer = lax.rem(m + k, g1)
            vals = summarise(peer)
            for c in range(4):
                send1[peer, c] = vals[c]
            remote(send1.at[peer], recv1.at[t, k], ex_send.at[t, 0], ex_recv.at[t, 0], (src, base + peer)).start()
            return carry

        lax.fori_loop(1, g1, step, 0)
        vals = summarise(m)
        for c in range(4):
            recv1[t, 0, c] = vals[c]

    def power(value, doublings):
        for _ in range(doublings):
            value = cmul(value, value)
        return value

    def own_root():
        return ctable(m, 0)

    def middle_out(t):
        take(recv1.at[t, pl.ds(1, g1 - 1)], ex_recv.at[t, 0])
        block_root = power(own_root(), int(math.log2(rows)))

        def gather(j, carry):
            ahead, behind = carry
            slot_a = lax.rem(m - j + g1, g1)
            slot_b = lax.rem(m - (g1 - 1 - j) + g1, g1)
            ahead = cmadd(ahead, block_root, (recv1[t, slot_a, 0], recv1[t, slot_a, 1]))
            behind = cmadd(behind, block_root, (recv1[t, slot_b, 2], recv1[t, slot_b, 3]))
            return ahead, behind

        zero = jnp.zeros((8, 128), F32)
        ahead, behind = lax.fori_loop(0, g1, gather, ((zero, zero), (zero, zero)), unroll=True)
        for c, value in enumerate(ahead + behind):
            recv2[t, 0, c] = value

        def send(k, carry):
            peer = lax.rem(grp + k, g2) * g1 + m
            remote(recv2.at[t, 0], recv2.at[t, k], ex_send.at[t, 1], ex_recv.at[t, 1], (src, peer)).start()
            return carry

        lax.fori_loop(1, g2, send, 0)
        take(recv1.at[t, pl.ds(1, g1 - 1)], ex_send.at[t, 0])

    def middle_back(t):
        block_root = power(own_root(), int(math.log2(rows)))
        group_root = power(block_root, int(math.log2(g1)))
        turn = power(group_root, int(math.log2(g2)))
        real, imag = 1.0 - turn[0], turn[1]
        norm = 1.0 / (real * real + imag * imag)
        inverse = (real * norm, imag * norm)
        take(recv2.at[t, pl.ds(1, g2 - 1)], ex_recv.at[t, 1])
        left = (recv2[t, 0, 0], recv2[t, 0, 1])
        right = (recv2[t, 0, 2], recv2[t, 0, 3])
        for k in range(g2 - 1, 0, -1):
            left = cmadd(left, group_root, (recv2[t, k, 0], recv2[t, k, 1]))
            right = cmadd(right, group_root, (recv2[t, g2 - k, 2], recv2[t, g2 - k, 3]))
        left = cmul(left, inverse)
        right = cmul(right, inverse)

        def spread(j, carry):
            left, right = carry
            back = g1 - 1 - j
            for c in range(2):
                send3[j, c] = left[c]
                send3[back, 2 + c] = right[c]
            slot_a = lax.rem(m - j + g1, g1)
            slot_b = lax.rem(m - back + g1, g1)
            left = cmadd(left, block_root, (recv1[t, slot_a, 0], recv1[t, slot_a, 1]))
            right = cmadd(right, block_root, (recv1[t, slot_b, 2], recv1[t, slot_b, 3]))
            return left, right

        lax.fori_loop(0, g1, spread, (left, right), unroll=True)

        def send(k, carry):
            peer = lax.rem(m + k, g1)
            remote(send3.at[peer], recv3.at[t, k], ex_send.at[t, 2], ex_recv.at[t, 2], (src, base + peer)).start()
            return carry

        lax.fori_loop(1, g1, send, 0)
        for c in range(4):
            recv3[t, 0, c] = send3[m, c]
        take(recv2.at[t, pl.ds(1, g2 - 1)], ex_send.at[t, 1])

    def sweep_back(t):
        take(recv3.at[t, pl.ds(1, g1 - 1)], ex_recv.at[t, 2])

        def step(k, carry):
            part = lax.rem(m - k + g1, g1)
            root = ctable(part, 0)
            kappa = ctable(part, 1)
            rowv = [spectral(i, part) for i in range(rows)]
            state = (recv3[t, k, 0], recv3[t, k, 1])
            ahead = []
            for i in range(rows):
                state = cmadd(state, root, rowv[i])
                ahead.append(state)
            state = cmul((recv3[t, k, 2], recv3[t, k, 3]), root)
            for i in range(rows - 1, -1, -1):
                total = cmul((ahead[i][0] + state[0], ahead[i][1] + state[1]), kappa)
                tile(sp_ref, i, part, 0)[...] = total[0]
                tile(sp_ref, i, part, 1)[...] = total[1]
                if i:
                    state = cmul((state[0] + rowv[i][0], state[1] + rowv[i][1]), root)
            return carry

        lax.fori_loop(0, g1, step, 0)
        take(recv3.at[t, pl.ds(1, g1 - 1)], ex_send.at[t, 2])

    def convolve(t, src_ref, dst_ref, between=()):
        hooks = list(between) + [lambda: None] * 3
        local(src_ref, sp_ref)
        hooks[0]()
        sweep_out(t)
        middle_out(t)
        hooks[1]()
        middle_back(t)
        sweep_back(t)
        hooks[2]()
        local(sp_ref, dst_ref)

    def pair(ref, x, z):
        return (ref[x, pl.ds(z, 8), :], ref[x, pl.ds(nz + z, 8), :])

    def put(ref, x, z, value):
        ref[x, pl.ds(z, 8), :] = value[0]
        ref[x, pl.ds(nz + z, 8), :] = value[1]

    def each_block(body, init):
        def outer(n, carry):
            return body(n // zgroups, pl.multiple_of(lax.rem(n, zgroups) * 8, 8), carry)

        return lax.fori_loop(0, rows * zgroups, outer, init, unroll=2)

    def square(value):
        return value[0] * value[0] + value[1] * value[1]

    zero = jnp.zeros((8, ny), F32)
    source_x = pos_ref[0, 0].astype(F32)
    source_y = pos_ref[0, 1].astype(F32)
    offset_y = lax.broadcasted_iota(jnp.int32, (8, ny), 1).astype(F32) - source_y
    offset_y_sq = offset_y * offset_y
    level = lax.broadcasted_iota(jnp.int32, (8, ny), 0).astype(F32) + SOURCE_GAP

    def begin(x, z, total):
        height = level + z.astype(F32)
        offset_x = (space * rows + x).astype(F32) - source_x
        dist = jnp.sqrt(height * height + offset_x * offset_x + offset_y_sq)
        turns = dist * (1.0 / 6.0)
        sine, cosine = half_turn(turns - jnp.floor(turns + 0.5))
        wave = (1.0 - 2.0 * sine * sine, 2.0 * sine * cosine)
        put(e_ref, x, z, wave)
        field = cmul(pair(chi0_ref, x, z), wave)
        put(w_ref, x, z, field)
        return total + square(field)

    object_part = each_block(begin, zero)
    data_part = jnp.zeros((1, ny), F32)
    for x in range(rows):
        for c in range(2):
            data_part = data_part + meas_ref[x, pl.ds(c, 1), :] * meas_ref[x, pl.ds(c, 1), :]
    data_fold = data_part[:, :128]
    for h in range(1, halves):
        data_fold = data_fold + data_part[:, h * 128:(h + 1) * 128]

    pl.semaphore_wait(barrier, (g1 - 1) + (ns * g2 - 1))
    reduce_start(0, [data_fold, fold(object_part)])
    convolve(0, w_ref, s_ref, (lambda: reduce_middle(0),))
    sums = reduce_end(0)
    data_weight = 1.0 / sums[0:1]
    object_weight = 1.0 / sums[1:2]
    chi_ref = chi0_ref
    for update in range(OUTER):
        t = 1 + 2 * update
        chi_next = chi1_ref if update < OUTER - 1 else chi_out_ref

        def residual(x, z, carry, chi_ref=chi_ref, object_weight=object_weight):
            chi = pair(chi_ref, x, z)
            e, s, w = pair(e_ref, x, z), pair(s_ref, x, z), pair(w_ref, x, z)
            field = cmul(chi, (e[0] + s[0], e[1] + s[1]))
            res = (object_weight * (field[0] - w[0]), object_weight * (field[1] - w[1]))
            put(r_ref, x, z, res)
            flipped = cmul(chi, (res[0], -res[1]))
            put(v_ref, x, z, (-flipped[0], -flipped[1]))
            return carry

        each_block(residual, 0)
        for x in range(rows):
            v_ref[x, pl.ds(0, 1), :] += data_weight * (meas_ref[x, pl.ds(0, 1), :] - s_ref[x, pl.ds(0, 1), :])
            v_ref[x, pl.ds(nz, 1), :] -= data_weight * (meas_ref[x, pl.ds(1, 1), :] - s_ref[x, pl.ds(nz, 1), :])
        convolve(t, v_ref, d_ref)

        def descend(x, z, total):
            res, image = pair(r_ref, x, z), pair(d_ref, x, z)
            d = (res[0] + image[0], res[1] - image[1])
            put(d_ref, x, z, d)
            return total + square(d)

        descent_part = each_block(descend, zero)
        convolve(t + 1, d_ref, v_ref)

        def changes(x, z, total, chi_ref=chi_ref):
            chi, d, h = pair(chi_ref, x, z), pair(d_ref, x, z), pair(v_ref, x, z)
            moved = cmul(chi, h)
            return total + square((d[0] - moved[0], d[1] - moved[1]))

        change_part = each_block(changes, zero)
        image_part = jnp.zeros((1, ny), F32)
        for x in range(rows):
            image_part = image_part + square((v_ref[x, pl.ds(0, 1), :], v_ref[x, pl.ds(nz, 1), :]))
        image_fold = image_part[:, :128]
        for h in range(1, halves):
            image_fold = image_fold + image_part[:, h * 128:(h + 1) * 128]
        a = 1 + 2 * update
        reduce_start(a, [fold(descent_part), image_fold, fold(change_part)])
        reduce_middle(a)
        sums = reduce_end(a)
        length = sums[0:1] / (data_weight * sums[1:2] + object_weight * sums[2:3])

        for k in range(1, ns + 1):
            x = lax.rem(src + k, ns)

            def advance(n, carry, x=x, length=length):
                z = pl.multiple_of(n * 8, 8)
                w, s, d, h, e = (pair(ref, x, z) for ref in (w_ref, s_ref, d_ref, v_ref, e_ref))
                w = (w[0] + length * d[0], w[1] + length * d[1])
                s = (s[0] + length * h[0], s[1] + length * h[1])
                put(w_ref, x, z, w)
                put(s_ref, x, z, s)
                u = (e[0] + s[0], e[1] + s[1])
                np_ref[x, pl.ds(z, 8), :] = w[0] * u[0] + w[1] * u[1]
                np_ref[x, pl.ds(nz + z, 8), :] = w[1] * u[0] - w[0] * u[1]
                np_ref[x, pl.ds(2 * nz + z, 8), :] = square(u)
                return carry

            lax.fori_loop(0, zgroups, advance, 0, unroll=2)
            if k < ns:
                remote(np_ref.at[x], np_recv.at[update, k], x_send.at[update, 0], x_recv.at[update, 0],
                       (x, space)).start()
        take(np_recv.at[update, pl.ds(1, ns - 1)], x_recv.at[update, 0])

        def contrast(n, total):
            z = pl.multiple_of(n * 8, 8)
            parts = [np_ref[src, pl.ds(c * nz + z, 8), :] for c in range(3)]
            for k in range(1, ns):
                parts = [parts[c] + np_recv[update, k, pl.ds(c * nz + z, 8), :] for c in range(3)]
            scale = 1.0 / jnp.maximum(parts[2], FLOOR_SHARE * ns)
            chi = (jnp.clip(parts[0] * scale, REAL_LOW, REAL_HIGH), jnp.clip(parts[1] * scale, 0.0, IMAG_HIGH))
            put(chi_next, src, z, chi)
            return total + square(chi)

        chi_part = lax.fori_loop(0, zgroups, contrast, zero, unroll=2)
        for k in range(1, ns):
            remote(chi_next.at[src], chi_next.at[src], x_send.at[update, 1], x_recv.at[update, 1],
                   (lax.rem(src + k, ns), space)).start()
        if update < OUTER - 1:
            reduce_start(a + 1, [fold(chi_part) * float(ns)])
            reduce_middle(a + 1)
            sums = reduce_end(a + 1)
            object_weight = 1.0 / sums[0:1]
        take(chi_next.at[pl.ds(0, ns - 1)], x_recv.at[update, 1])
        take(np_recv.at[update, pl.ds(1, ns - 1)], x_send.at[update, 0])
        take(chi_next.at[pl.ds(0, ns - 1)], x_send.at[update, 1])
        chi_ref = chi_next


def on_device(ns, g1, g2, contrast, measured, positions):
    _, nz, rows, ny = contrast.shape
    cfg = (ns, g1, g2, nz, ny, rows)
    transforms = 1 + 2 * OUTER
    reductions = 2 * OUTER
    chi0 = contrast.transpose(2, 0, 1, 3).reshape(rows, 2 * nz, ny)
    meas = measured[0].transpose(1, 0, 2)
    tables = decay_tables(nz, ny)
    hy = high_low(hartley(ny))
    hz = high_low(np.kron(np.eye(4), hartley(nz)))
    field = (rows, 2 * nz, ny)
    vmem = pl.BlockSpec(memory_space=pltpu.VMEM)
    w, chi = pl.pallas_call(
        functools.partial(kernel, cfg),
        out_shape=(jax.ShapeDtypeStruct(field, F32), jax.ShapeDtypeStruct(field, F32)),
        in_specs=[pl.BlockSpec(memory_space=pltpu.SMEM)] + [vmem] * 5,
        out_specs=(vmem, vmem),
        scratch_shapes=[pltpu.VMEM(field, F32)] * 7 + [
            pltpu.VMEM((rows, 3 * nz, ny), F32),
            pltpu.VMEM((OUTER, ns, 3 * nz, ny), F32),
            pltpu.VMEM((g1, 4, 8, 128), F32),
            pltpu.VMEM((g1, 4, 8, 128), F32),
            pltpu.VMEM((transforms, g1, 4, 8, 128), F32),
            pltpu.VMEM((transforms, g2, 4, 8, 128), F32),
            pltpu.VMEM((transforms, g1, 4, 8, 128), F32),
            pltpu.VMEM((reductions, g1, 8, 128), F32),
            pltpu.VMEM((reductions, ns * g2, 8, 128), F32),
            pltpu.SemaphoreType.DMA((transforms, 3)),
            pltpu.SemaphoreType.DMA((transforms, 3)),
            pltpu.SemaphoreType.DMA((reductions, 2)),
            pltpu.SemaphoreType.DMA((reductions, 2)),
            pltpu.SemaphoreType.DMA((OUTER, 2)),
            pltpu.SemaphoreType.DMA((OUTER, 2)),
        ],
        compiler_params=pltpu.CompilerParams(
            collective_id=0, has_side_effects=True, vmem_limit_bytes=40 * 1024 * 1024
        ),
    )(positions, chi0, meas, tables, hy, hz)
    sources = w.reshape(rows, 2, nz, ny).transpose(1, 2, 0, 3)[None]
    return sources, chi.reshape(rows, 2, nz, ny).transpose(1, 2, 0, 3)


def solution(mesh, g2=4):
    placed = (P(None, None, "space", None), P("src", None, "space", None), P("src", None))
    return jax.shard_map(
        functools.partial(on_device, mesh.shape["src"], mesh.shape["space"] // g2, g2),
        mesh=mesh,
        in_specs=placed,
        out_specs=(P("src", None, None, "space", None), P(None, None, "space", None)),
        check_vma=False,
    )
```

```python
import functools
import math

import jax
import jax.numpy as jnp
import ml_dtypes
import numpy as np
from jax import lax
from jax.experimental import pallas as pl
from jax.experimental.pallas import tpu as pltpu
from jax.sharding import PartitionSpec as P

OUTER = 2
WAVENUMBER = 2.0 * math.pi / 6.0
DAMPING = 0.3
SOURCE_GAP = 8.0
FLOOR_SHARE = 0.75
REAL_LOW = -0.25
REAL_HIGH = 0.35
IMAG_HIGH = 0.1
F32 = jnp.float32
BF16 = jnp.bfloat16
MESH = pl.DeviceIdType.MESH


def hartley(length):
    turn = np.outer(np.arange(length), np.arange(length)) % length
    angle = 2.0 * np.pi / length * turn
    return (np.cos(angle) + np.sin(angle)) / np.sqrt(length)


def high_low(table):
    high = table.astype(ml_dtypes.bfloat16)
    low = (table - high.astype(np.float64)).astype(ml_dtypes.bfloat16)
    return np.stack([high, low])


def modes(length):
    return 4.0 * np.sin(np.pi * np.arange(length) / length) ** 2


def decay_tables(depth, across):
    wave_sq = WAVENUMBER * WAVENUMBER
    trace = 2.0 + modes(depth)[:, None] + modes(across)[None, :] - wave_sq * (1.0 + 1j * DAMPING)
    root = np.sqrt(trace * trace - 4.0)
    first = (trace - root) / 2.0
    second = (trace + root) / 2.0
    small = np.where(np.abs(first) < np.abs(second), first, second)
    large = np.where(np.abs(first) < np.abs(second), second, first)
    small = 1.0 / large
    kappa = wave_sq / (large - small)
    tables = np.stack([small.real, small.imag, kappa.real, kappa.imag])
    return tables.astype(np.float32)


def cmul(a, b):
    return (a[0] * b[0] - a[1] * b[1], a[0] * b[1] + a[1] * b[0])


def cmadd(a, b, c):
    return (a[0] * b[0] - a[1] * b[1] + c[0], a[0] * b[1] + a[1] * b[0] + c[1])


def half_turn(fraction):
    angle = fraction * math.pi
    sq = angle * angle
    sine = jnp.full_like(sq, -1.0 / math.factorial(11))
    for order in (9, 7, 5, 3, 1):
        sine = sine * sq + (1.0 if order % 4 == 1 else -1.0) / math.factorial(order)
    cosine = jnp.full_like(sq, 1.0 / math.factorial(12))
    for order in (10, 8, 6, 4, 2, 0):
        cosine = cosine * sq + (1.0 if order % 4 == 0 else -1.0) / math.factorial(order)
    return sine * angle, cosine


def kernel(
    cfg,
    pos_ref, chi0_ref, meas_ref, tab_ref, hy_ref, hz_ref,
    w_ref, chi_out_ref,
    chi1_ref, e_ref, s_ref, r_ref, d_ref, v_ref, b_ref, sp_all, np_ref, np_recv,
    send1_all, send3_all, recv1, recv2, recv3, red1, red2,
    ex_send, ex_recv, red_send, red_recv, x_send, x_recv,
):
    ns, g1, g2, nz, ny, rows = cfg
    halves = ny // 128
    nx = g1 * g2 * rows
    zgroups = nz // 8
    src = lax.axis_index("src")
    space = lax.axis_index("space")
    m = lax.rem(space, g1)
    grp = space // g1
    base = grp * g1

    barrier = pltpu.get_barrier_semaphore()

    def greet_group(k, carry):
        pl.semaphore_signal(barrier, inc=1, device_id=(src, base + lax.rem(m + k, g1)), device_id_type=MESH)
        return carry

    def cross_peer(k):
        return lax.rem(src + k // g2, ns), lax.rem(grp + lax.rem(k, g2), g2) * g1 + m

    def greet_cross(k, carry):
        pl.semaphore_signal(barrier, inc=1, device_id=cross_peer(k), device_id_type=MESH)
        return carry

    lax.fori_loop(1, g1, greet_group, 0)
    lax.fori_loop(1, ns * g2, greet_cross, 0)

    def remote(src_ref, dst_ref, send_sem, recv_sem, device):
        return pltpu.make_async_remote_copy(
            src_ref=src_ref, dst_ref=dst_ref, send_sem=send_sem, recv_sem=recv_sem,
            device_id=device, device_id_type=MESH,
        )

    def take(ref, sem):
        pltpu.make_async_copy(ref, ref, sem).wait()

    def reduce_start(a, parts):
        red1[a, 0] = jnp.concatenate(parts + [jnp.zeros((8 - len(parts), 128), F32)], axis=0)

        def send(k, carry):
            remote(red1.at[a, 0], red1.at[a, k], red_send.at[a, 0], red_recv.at[a, 0],
                   (src, base + lax.rem(m + k, g1))).start()
            return carry

        lax.fori_loop(1, g1, send, 0)

    def reduce_middle(a):
        take(red1.at[a, pl.ds(1, g1 - 1)], red_recv.at[a, 0])

        def add(j, total):
            return total + red1[a, lax.rem(m - j + g1, g1)]

        red2[a, 0] = lax.fori_loop(0, g1, add, jnp.zeros((8, 128), F32), unroll=True)
        take(red1.at[a, pl.ds(1, g1 - 1)], red_send.at[a, 0])

        def send(k, carry):
            remote(red2.at[a, 0], red2.at[a, k], red_send.at[a, 1], red_recv.at[a, 1], cross_peer(k)).start()
            return carry

        lax.fori_loop(1, ns * g2, send, 0)

    def reduce_end(a):
        count = ns * g2
        take(red2.at[a, pl.ds(1, count - 1)], red_recv.at[a, 1])

        def add(j, total):
            slot = lax.rem(src - j // g2 + ns, ns) * g2 + lax.rem(grp - lax.rem(j, g2) + g2, g2)
            return total + red2[a, slot]

        total = lax.fori_loop(0, count, add, jnp.zeros((8, 128), F32), unroll=True)
        take(red2.at[a, pl.ds(1, count - 1)], red_send.at[a, 1])
        return jnp.sum(total, axis=1, keepdims=True)

    def fold(acc):
        part = acc[:, :128]
        for h in range(1, halves):
            part = part + acc[:, h * 128:(h + 1) * 128]
        return jnp.sum(part, axis=0, keepdims=True)

    def split(a):
        high = a.astype(BF16)
        return high, (a - high.astype(F32)).astype(BF16)

    def dot3(a, b):
        mm = functools.partial(jnp.dot, preferred_element_type=F32)
        return mm(a[0], b[0]) + (mm(a[1], b[0]) + mm(a[0], b[1]))

    def local(src_ref, dst_ref):
        hz = (hz_ref[0], hz_ref[1])
        hy = (hy_ref[0], hy_ref[1])
        for pair in range(rows // 2):
            block = src_ref[pl.ds(2 * pair, 2)].reshape(4 * nz, ny)
            depth_done = dot3(hz, split(block))
            done = dot3(split(depth_done), hy)
            dst_ref[pl.ds(2 * pair, 2)] = done.reshape(2, 2 * nz, ny)

    def tile(ref, lead, part, comp):
        z = pl.multiple_of(part // halves * 8, 8)
        y = pl.multiple_of(lax.rem(part, halves) * 128, 128)
        return ref.at[lead, pl.ds(comp * nz + z, 8), pl.ds(y, 128)]

    def ctable(part, which):
        z = pl.multiple_of(part // halves * 8, 8)
        y = pl.multiple_of(lax.rem(part, halves) * 128, 128)
        return tuple(tab_ref[2 * which + c, pl.ds(z, 8), pl.ds(y, 128)] for c in range(2))

    def spectral(sp_ref, lead, part):
        return (tile(sp_ref, lead, part, 0)[...], tile(sp_ref, lead, part, 1)[...])

    def sweep_out(t):
        sp_ref, send1 = sp_all.at[t % 2], send1_all.at[t % 2]

        def summarise(part):
            root = ctable(part, 0)
            rowv = [spectral(sp_ref, i, part) for i in range(rows)]
            ahead = rowv[0]
            for i in range(1, rows):
                ahead = cmadd(ahead, root, rowv[i])
            behind = rowv[rows - 1]
            for i in range(rows - 2, -1, -1):
                behind = cmadd(behind, root, rowv[i])
            return ahead + behind

        def step(k, carry):
            peer = lax.rem(m + k, g1)
            vals = summarise(peer)
            for c in range(4):
                send1[peer, c] = vals[c]
            remote(send1.at[peer], recv1.at[t, k], ex_send.at[t, 0], ex_recv.at[t, 0], (src, base + peer)).start()
            return carry

        lax.fori_loop(1, g1, step, 0)
        vals = summarise(m)
        for c in range(4):
            recv1[t, 0, c] = vals[c]

    def power(value, doublings):
        for _ in range(doublings):
            value = cmul(value, value)
        return value

    def own_root():
        return ctable(m, 0)

    def middle_out(t):
        take(recv1.at[t, pl.ds(1, g1 - 1)], ex_recv.at[t, 0])
        block_root = power(own_root(), int(math.log2(rows)))

        def gather(j, carry):
            ahead, behind = carry
            slot_a = lax.rem(m - j + g1, g1)
            slot_b = lax.rem(m - (g1 - 1 - j) + g1, g1)
            ahead = cmadd(ahead, block_root, (recv1[t, slot_a, 0], recv1[t, slot_a, 1]))
            behind = cmadd(behind, block_root, (recv1[t, slot_b, 2], recv1[t, slot_b, 3]))
            return ahead, behind

        zero = jnp.zeros((8, 128), F32)
        ahead, behind = lax.fori_loop(0, g1, gather, ((zero, zero), (zero, zero)), unroll=True)
        for c, value in enumerate(ahead + behind):
            recv2[t, 0, c] = value

        def send(k, carry):
            peer = lax.rem(grp + k, g2) * g1 + m
            remote(recv2.at[t, 0], recv2.at[t, k], ex_send.at[t, 1], ex_recv.at[t, 1], (src, peer)).start()
            return carry

        lax.fori_loop(1, g2, send, 0)
        take(recv1.at[t, pl.ds(1, g1 - 1)], ex_send.at[t, 0])

    def middle_back(t):
        send3 = send3_all.at[t % 2]
        block_root = power(own_root(), int(math.log2(rows)))
        group_root = power(block_root, int(math.log2(g1)))
        turn = power(group_root, int(math.log2(g2)))
        real, imag = 1.0 - turn[0], turn[1]
        norm = 1.0 / (real * real + imag * imag)
        inverse = (real * norm, imag * norm)
        take(recv2.at[t, pl.ds(1, g2 - 1)], ex_recv.at[t, 1])
        left = (recv2[t, 0, 0], recv2[t, 0, 1])
        right = (recv2[t, 0, 2], recv2[t, 0, 3])
        for k in range(g2 - 1, 0, -1):
            left = cmadd(left, group_root, (recv2[t, k, 0], recv2[t, k, 1]))
            right = cmadd(right, group_root, (recv2[t, g2 - k, 2], recv2[t, g2 - k, 3]))
        left = cmul(left, inverse)
        right = cmul(right, inverse)

        def spread(j, carry):
            left, right = carry
            back = g1 - 1 - j
            for c in range(2):
                send3[j, c] = left[c]
                send3[back, 2 + c] = right[c]
            slot_a = lax.rem(m - j + g1, g1)
            slot_b = lax.rem(m - back + g1, g1)
            left = cmadd(left, block_root, (recv1[t, slot_a, 0], recv1[t, slot_a, 1]))
            right = cmadd(right, block_root, (recv1[t, slot_b, 2], recv1[t, slot_b, 3]))
            return left, right

        lax.fori_loop(0, g1, spread, (left, right), unroll=True)

        def send(k, carry):
            peer = lax.rem(m + k, g1)
            remote(send3.at[peer], recv3.at[t, k], ex_send.at[t, 2], ex_recv.at[t, 2], (src, base + peer)).start()
            return carry

        lax.fori_loop(1, g1, send, 0)
        for c in range(4):
            recv3[t, 0, c] = send3[m, c]
        take(recv2.at[t, pl.ds(1, g2 - 1)], ex_send.at[t, 1])

    def sweep_back(t):
        sp_ref = sp_all.at[t % 2]
        take(recv3.at[t, pl.ds(1, g1 - 1)], ex_recv.at[t, 2])

        def step(k, carry):
            part = lax.rem(m - k + g1, g1)
            root = ctable(part, 0)
            kappa = ctable(part, 1)
            rowv = [spectral(sp_ref, i, part) for i in range(rows)]
            state = (recv3[t, k, 0], recv3[t, k, 1])
            ahead = []
            for i in range(rows):
                state = cmadd(state, root, rowv[i])
                ahead.append(state)
            state = cmul((recv3[t, k, 2], recv3[t, k, 3]), root)
            for i in range(rows - 1, -1, -1):
                total = cmul((ahead[i][0] + state[0], ahead[i][1] + state[1]), kappa)
                tile(sp_ref, i, part, 0)[...] = total[0]
                tile(sp_ref, i, part, 1)[...] = total[1]
                if i:
                    state = cmul((state[0] + rowv[i][0], state[1] + rowv[i][1]), root)
            return carry

        lax.fori_loop(0, g1, step, 0)
        take(recv3.at[t, pl.ds(1, g1 - 1)], ex_send.at[t, 2])

    def pair(ref, x, z):
        return (ref[x, pl.ds(z, 8), :], ref[x, pl.ds(nz + z, 8), :])

    def put(ref, x, z, value):
        ref[x, pl.ds(z, 8), :] = value[0]
        ref[x, pl.ds(nz + z, 8), :] = value[1]

    def each_block(body, init):
        def outer(n, carry):
            return body(n // zgroups, pl.multiple_of(lax.rem(n, zgroups) * 8, 8), carry)

        return lax.fori_loop(0, rows * zgroups, outer, init, unroll=4)

    def square(value):
        return value[0] * value[0] + value[1] * value[1]

    zero = jnp.zeros((8, ny), F32)
    source_x = pos_ref[0, 0].astype(F32)
    source_y = pos_ref[0, 1].astype(F32)
    offset_y = lax.broadcasted_iota(jnp.int32, (8, ny), 1).astype(F32) - source_y
    offset_y_sq = offset_y * offset_y
    level = lax.broadcasted_iota(jnp.int32, (8, ny), 0).astype(F32) + SOURCE_GAP

    def begin(x, z, total):
        height = level + z.astype(F32)
        offset_x = (space * rows + x).astype(F32) - source_x
        dist = jnp.sqrt(height * height + offset_x * offset_x + offset_y_sq)
        turns = dist * (1.0 / 6.0)
        sine, cosine = half_turn(turns - jnp.floor(turns + 0.5))
        wave = (1.0 - 2.0 * sine * sine, 2.0 * sine * cosine)
        put(e_ref, x, z, wave)
        field = cmul(pair(chi0_ref, x, z), wave)
        put(w_ref, x, z, field)
        return total + square(field)

    object_part = each_block(begin, zero)
    data_part = jnp.zeros((1, ny), F32)
    for x in range(rows):
        for c in range(2):
            data_part = data_part + meas_ref[x, pl.ds(c, 1), :] * meas_ref[x, pl.ds(c, 1), :]
    data_fold = data_part[:, :128]
    for h in range(1, halves):
        data_fold = data_fold + data_part[:, h * 128:(h + 1) * 128]

    local(w_ref, sp_all.at[0])
    pl.semaphore_wait(barrier, (g1 - 1) + (ns * g2 - 1))
    sweep_out(0)
    reduce_start(0, [data_fold, fold(object_part)])
    middle_out(0)
    reduce_middle(0)
    middle_back(0)
    sums = reduce_end(0)
    sweep_back(0)
    local(sp_all.at[0], s_ref)
    data_weight = 1.0 / sums[0:1]
    object_weight = 1.0 / sums[1:2]
    ratio = 0.5 / DAMPING
    chi_ref = chi0_ref
    for update in range(OUTER):
        t = 1 + 2 * update
        chi_next = chi1_ref if update < OUTER - 1 else chi_out_ref

        def residual(x, z, carry, chi_ref=chi_ref, object_weight=object_weight):
            chi = pair(chi_ref, x, z)
            e, s, w = pair(e_ref, x, z), pair(s_ref, x, z), pair(w_ref, x, z)
            field = cmul(chi, (e[0] + s[0], e[1] + s[1]))
            res = (object_weight * (field[0] - w[0]), object_weight * (field[1] - w[1]))
            put(r_ref, x, z, res)
            flipped = cmul(chi, (res[0], -res[1]))
            put(v_ref, x, z, (-flipped[0], -flipped[1]))
            put(b_ref, x, z, (res[0] + ratio * flipped[1], res[1] + ratio * flipped[0]))
            return carry

        each_block(residual, 0)
        for x in range(rows):
            top = data_weight * (meas_ref[x, pl.ds(0, 1), :] - s_ref[x, pl.ds(0, 1), :])
            bottom = data_weight * (meas_ref[x, pl.ds(1, 1), :] - s_ref[x, pl.ds(nz, 1), :])
            v_ref[x, pl.ds(0, 1), :] += top
            v_ref[x, pl.ds(nz, 1), :] -= bottom
            b_ref[x, pl.ds(0, 1), :] += ratio * bottom
            b_ref[x, pl.ds(nz, 1), :] -= ratio * top
        first, second = sp_all.at[t % 2], sp_all.at[(t + 1) % 2]
        local(v_ref, first)
        sweep_out(t)
        local(b_ref, second)
        sweep_out(t + 1)
        middle_out(t)
        middle_out(t + 1)
        middle_back(t)
        middle_back(t + 1)
        sweep_back(t)
        local(first, d_ref)
        sweep_back(t + 1)
        local(second, v_ref)

        def descend(x, z, totals, chi_ref=chi_ref):
            res, image, other = pair(r_ref, x, z), pair(d_ref, x, z), pair(v_ref, x, z)
            d = (res[0] + image[0], res[1] - image[1])
            h = (other[0] + ratio * image[1], other[1] + ratio * image[0])
            put(d_ref, x, z, d)
            put(v_ref, x, z, h)
            moved = cmul(pair(chi_ref, x, z), h)
            return totals[0] + square(d), totals[1] + square((d[0] - moved[0], d[1] - moved[1]))

        descent_part, change_part = each_block(descend, (zero, zero))
        image_part = jnp.zeros((1, ny), F32)
        for x in range(rows):
            image_part = image_part + square((v_ref[x, pl.ds(0, 1), :], v_ref[x, pl.ds(nz, 1), :]))
        image_fold = image_part[:, :128]
        for h in range(1, halves):
            image_fold = image_fold + image_part[:, h * 128:(h + 1) * 128]
        a = 1 + 2 * update
        reduce_start(a, [fold(descent_part), image_fold, fold(change_part)])
        reduce_middle(a)
        sums = reduce_end(a)
        length = sums[0:1] / (data_weight * sums[1:2] + object_weight * sums[2:3])

        for k in range(1, ns + 1):
            x = lax.rem(src + k, ns)

            def advance(n, carry, x=x, length=length):
                z = pl.multiple_of(n * 8, 8)
                w, s, d, h, e = (pair(ref, x, z) for ref in (w_ref, s_ref, d_ref, v_ref, e_ref))
                w = (w[0] + length * d[0], w[1] + length * d[1])
                s = (s[0] + length * h[0], s[1] + length * h[1])
                put(w_ref, x, z, w)
                put(s_ref, x, z, s)
                u = (e[0] + s[0], e[1] + s[1])
                np_ref[x, pl.ds(z, 8), :] = w[0] * u[0] + w[1] * u[1]
                np_ref[x, pl.ds(nz + z, 8), :] = w[1] * u[0] - w[0] * u[1]
                np_ref[x, pl.ds(2 * nz + z, 8), :] = square(u)
                return carry

            lax.fori_loop(0, zgroups, advance, 0, unroll=2)
            if k < ns:
                remote(np_ref.at[x], np_recv.at[update, k], x_send.at[update, 0], x_recv.at[update, 0],
                       (x, space)).start()
        take(np_recv.at[update, pl.ds(1, ns - 1)], x_recv.at[update, 0])

        def contrast(n, total):
            z = pl.multiple_of(n * 8, 8)
            parts = [np_ref[src, pl.ds(c * nz + z, 8), :] for c in range(3)]
            for k in range(1, ns):
                parts = [parts[c] + np_recv[update, k, pl.ds(c * nz + z, 8), :] for c in range(3)]
            scale = 1.0 / jnp.maximum(parts[2], FLOOR_SHARE * ns)
            chi = (jnp.clip(parts[0] * scale, REAL_LOW, REAL_HIGH), jnp.clip(parts[1] * scale, 0.0, IMAG_HIGH))
            put(chi_next, src, z, chi)
            return total + square(chi)

        chi_part = lax.fori_loop(0, zgroups, contrast, zero, unroll=2)
        for k in range(1, ns):
            remote(chi_next.at[src], chi_next.at[src], x_send.at[update, 1], x_recv.at[update, 1],
                   (lax.rem(src + k, ns), space)).start()
        if update < OUTER - 1:
            reduce_start(a + 1, [fold(chi_part) * float(ns)])
            reduce_middle(a + 1)
            sums = reduce_end(a + 1)
            object_weight = 1.0 / sums[0:1]
        take(chi_next.at[pl.ds(0, ns - 1)], x_recv.at[update, 1])
        take(np_recv.at[update, pl.ds(1, ns - 1)], x_send.at[update, 0])
        take(chi_next.at[pl.ds(0, ns - 1)], x_send.at[update, 1])
        chi_ref = chi_next


def on_device(ns, g1, g2, contrast, measured, positions):
    _, nz, rows, ny = contrast.shape
    cfg = (ns, g1, g2, nz, ny, rows)
    transforms = 1 + 2 * OUTER
    reductions = 2 * OUTER
    chi0 = contrast.transpose(2, 0, 1, 3).reshape(rows, 2 * nz, ny)
    meas = measured[0].transpose(1, 0, 2)
    tables = decay_tables(nz, ny)
    hy = high_low(hartley(ny))
    hz = high_low(np.kron(np.eye(4), hartley(nz)))
    field = (rows, 2 * nz, ny)
    vmem = pl.BlockSpec(memory_space=pltpu.VMEM)
    w, chi = pl.pallas_call(
        functools.partial(kernel, cfg),
        out_shape=(jax.ShapeDtypeStruct(field, F32), jax.ShapeDtypeStruct(field, F32)),
        in_specs=[pl.BlockSpec(memory_space=pltpu.SMEM)] + [vmem] * 5,
        out_specs=(vmem, vmem),
        scratch_shapes=[pltpu.VMEM(field, F32)] * 7 + [
            pltpu.VMEM((2,) + field, F32),
            pltpu.VMEM((rows, 3 * nz, ny), F32),
            pltpu.VMEM((OUTER, ns, 3 * nz, ny), F32),
            pltpu.VMEM((2, g1, 4, 8, 128), F32),
            pltpu.VMEM((2, g1, 4, 8, 128), F32),
            pltpu.VMEM((transforms, g1, 4, 8, 128), F32),
            pltpu.VMEM((transforms, g2, 4, 8, 128), F32),
            pltpu.VMEM((transforms, g1, 4, 8, 128), F32),
            pltpu.VMEM((reductions, g1, 8, 128), F32),
            pltpu.VMEM((reductions, ns * g2, 8, 128), F32),
            pltpu.SemaphoreType.DMA((transforms, 3)),
            pltpu.SemaphoreType.DMA((transforms, 3)),
            pltpu.SemaphoreType.DMA((reductions, 2)),
            pltpu.SemaphoreType.DMA((reductions, 2)),
            pltpu.SemaphoreType.DMA((OUTER, 2)),
            pltpu.SemaphoreType.DMA((OUTER, 2)),
        ],
        compiler_params=pltpu.CompilerParams(
            collective_id=0, has_side_effects=True, vmem_limit_bytes=40 * 1024 * 1024
        ),
    )(positions, chi0, meas, tables, hy, hz)
    sources = w.reshape(rows, 2, nz, ny).transpose(1, 2, 0, 3)[None]
    return sources, chi.reshape(rows, 2, nz, ny).transpose(1, 2, 0, 3)


def solution(mesh, g2=4):
    placed = (P(None, None, "space", None), P("src", None, "space", None), P("src", None))
    return jax.shard_map(
        functools.partial(on_device, mesh.shape["src"], mesh.shape["space"] // g2, g2),
        mesh=mesh,
        in_specs=placed,
        out_specs=(P("src", None, None, "space", None), P(None, None, "space", None)),
        check_vma=False,
    )
```

```python
import functools
import math

import jax
import jax.numpy as jnp
import ml_dtypes
import numpy as np
from jax import lax
from jax.experimental import pallas as pl
from jax.experimental.pallas import tpu as pltpu
from jax.sharding import PartitionSpec as P

OUTER = 2
WAVENUMBER = 2.0 * math.pi / 6.0
DAMPING = 0.3
SOURCE_GAP = 8.0
FLOOR_SHARE = 0.75
REAL_LOW = -0.25
REAL_HIGH = 0.35
IMAG_HIGH = 0.1
F32 = jnp.float32
BF16 = jnp.bfloat16
MESH = pl.DeviceIdType.MESH


def hartley(length):
    turn = np.outer(np.arange(length), np.arange(length)) % length
    angle = 2.0 * np.pi / length * turn
    return (np.cos(angle) + np.sin(angle)) / np.sqrt(length)


def high_low(table):
    high = table.astype(ml_dtypes.bfloat16)
    low = (table - high.astype(np.float64)).astype(ml_dtypes.bfloat16)
    return np.stack([high, low])


def modes(length):
    return 4.0 * np.sin(np.pi * np.arange(length) / length) ** 2


def decay_tables(depth, across):
    wave_sq = WAVENUMBER * WAVENUMBER
    trace = 2.0 + modes(depth)[:, None] + modes(across)[None, :] - wave_sq * (1.0 + 1j * DAMPING)
    root = np.sqrt(trace * trace - 4.0)
    first = (trace - root) / 2.0
    second = (trace + root) / 2.0
    small = np.where(np.abs(first) < np.abs(second), first, second)
    large = np.where(np.abs(first) < np.abs(second), second, first)
    small = 1.0 / large
    kappa = wave_sq / (large - small)
    tables = np.stack([small.real, small.imag, kappa.real, kappa.imag])
    return tables.astype(np.float32)


def cmul(a, b):
    return (a[0] * b[0] - a[1] * b[1], a[0] * b[1] + a[1] * b[0])


def cmadd(a, b, c):
    return (a[0] * b[0] - a[1] * b[1] + c[0], a[0] * b[1] + a[1] * b[0] + c[1])


def half_turn(fraction):
    angle = fraction * math.pi
    sq = angle * angle
    sine = jnp.full_like(sq, -1.0 / math.factorial(11))
    for order in (9, 7, 5, 3, 1):
        sine = sine * sq + (1.0 if order % 4 == 1 else -1.0) / math.factorial(order)
    cosine = jnp.full_like(sq, 1.0 / math.factorial(12))
    for order in (10, 8, 6, 4, 2, 0):
        cosine = cosine * sq + (1.0 if order % 4 == 0 else -1.0) / math.factorial(order)
    return sine * angle, cosine


def kernel(
    cfg,
    pos_ref, chi0_ref, meas_ref, tab_ref, hy_ref, hz_ref,
    w_ref, chi_out_ref,
    chi1_ref, e_ref, s_ref, r_ref, d_ref, v_ref, b_ref, sp_all, rho_ref, early_ref, early_recv, late_ref, late_recv,
    send1_all, send3_all, recv1, recv2, recv3, red1, red2,
    ex_send, ex_recv, red_send, red_recv, x_send, x_recv,
):
    ns, g1, g2, nz, ny, rows = cfg
    halves = ny // 128
    nx = g1 * g2 * rows
    zgroups = nz // 8
    src = lax.axis_index("src")
    space = lax.axis_index("space")
    m = lax.rem(space, g1)
    grp = space // g1
    base = grp * g1

    barrier = pltpu.get_barrier_semaphore()

    def greet_group(k, carry):
        pl.semaphore_signal(barrier, inc=1, device_id=(src, base + lax.rem(m + k, g1)), device_id_type=MESH)
        return carry

    def cross_peer(k):
        return lax.rem(src + k // g2, ns), lax.rem(grp + lax.rem(k, g2), g2) * g1 + m

    def greet_cross(k, carry):
        pl.semaphore_signal(barrier, inc=1, device_id=cross_peer(k), device_id_type=MESH)
        return carry

    lax.fori_loop(1, g1, greet_group, 0)
    lax.fori_loop(1, ns * g2, greet_cross, 0)

    def remote(src_ref, dst_ref, send_sem, recv_sem, device):
        return pltpu.make_async_remote_copy(
            src_ref=src_ref, dst_ref=dst_ref, send_sem=send_sem, recv_sem=recv_sem,
            device_id=device, device_id_type=MESH,
        )

    def take(ref, sem):
        pltpu.make_async_copy(ref, ref, sem).wait()

    def reduce_start(a, parts):
        red1[a, 0] = jnp.concatenate(parts + [jnp.zeros((8 - len(parts), 128), F32)], axis=0)

        def send(k, carry):
            remote(red1.at[a, 0], red1.at[a, k], red_send.at[a, 0], red_recv.at[a, 0],
                   (src, base + lax.rem(m + k, g1))).start()
            return carry

        lax.fori_loop(1, g1, send, 0)

    def reduce_middle(a):
        take(red1.at[a, pl.ds(1, g1 - 1)], red_recv.at[a, 0])

        def add(j, total):
            return total + red1[a, lax.rem(m - j + g1, g1)]

        red2[a, 0] = lax.fori_loop(0, g1, add, jnp.zeros((8, 128), F32), unroll=True)
        take(red1.at[a, pl.ds(1, g1 - 1)], red_send.at[a, 0])

        def send(k, carry):
            remote(red2.at[a, 0], red2.at[a, k], red_send.at[a, 1], red_recv.at[a, 1], cross_peer(k)).start()
            return carry

        lax.fori_loop(1, ns * g2, send, 0)

    def reduce_end(a):
        count = ns * g2
        take(red2.at[a, pl.ds(1, count - 1)], red_recv.at[a, 1])

        def add(j, total):
            slot = lax.rem(src - j // g2 + ns, ns) * g2 + lax.rem(grp - lax.rem(j, g2) + g2, g2)
            return total + red2[a, slot]

        total = lax.fori_loop(0, count, add, jnp.zeros((8, 128), F32), unroll=True)
        take(red2.at[a, pl.ds(1, count - 1)], red_send.at[a, 1])
        return jnp.sum(total, axis=1, keepdims=True)

    def fold(acc):
        part = acc[:, :128]
        for h in range(1, halves):
            part = part + acc[:, h * 128:(h + 1) * 128]
        return jnp.sum(part, axis=0, keepdims=True)

    def split(a):
        high = a.astype(BF16)
        return high, (a - high.astype(F32)).astype(BF16)

    def dot3(a, b):
        mm = functools.partial(jnp.dot, preferred_element_type=F32)
        return mm(a[0], b[0]) + (mm(a[1], b[0]) + mm(a[0], b[1]))

    def local(src_ref, dst_ref):
        hz = (hz_ref[0], hz_ref[1])
        hy = (hy_ref[0], hy_ref[1])
        for pair in range(rows // 2):
            block = src_ref[pl.ds(2 * pair, 2)].reshape(4 * nz, ny)
            depth_done = dot3(hz, split(block))
            done = dot3(split(depth_done), hy)
            dst_ref[pl.ds(2 * pair, 2)] = done.reshape(2, 2 * nz, ny)

    def tile(ref, lead, part, comp):
        z = pl.multiple_of(part // halves * 8, 8)
        y = pl.multiple_of(lax.rem(part, halves) * 128, 128)
        return ref.at[lead, pl.ds(comp * nz + z, 8), pl.ds(y, 128)]

    def ctable(part, which):
        z = pl.multiple_of(part // halves * 8, 8)
        y = pl.multiple_of(lax.rem(part, halves) * 128, 128)
        return tuple(tab_ref[2 * which + c, pl.ds(z, 8), pl.ds(y, 128)] for c in range(2))

    def spectral(sp_ref, lead, part):
        return (tile(sp_ref, lead, part, 0)[...], tile(sp_ref, lead, part, 1)[...])

    def sweep_out(t, extra=None):
        sp_ref, send1 = sp_all.at[t % 2], send1_all.at[t % 2]

        def summarise(part):
            root = ctable(part, 0)
            rowv = [spectral(sp_ref, i, part) for i in range(rows)]
            if extra is not None:
                rowv = [extra(i, part, value) for i, value in enumerate(rowv)]
                for i in range(rows):
                    tile(sp_ref, i, part, 0)[...] = rowv[i][0]
                    tile(sp_ref, i, part, 1)[...] = rowv[i][1]
            ahead = rowv[0]
            for i in range(1, rows):
                ahead = cmadd(ahead, root, rowv[i])
            behind = rowv[rows - 1]
            for i in range(rows - 2, -1, -1):
                behind = cmadd(behind, root, rowv[i])
            return ahead + behind

        def step(k, carry):
            peer = lax.rem(m + k, g1)
            vals = summarise(peer)
            for c in range(4):
                send1[peer, c] = vals[c]
            remote(send1.at[peer], recv1.at[t, k], ex_send.at[t, 0], ex_recv.at[t, 0], (src, base + peer)).start()
            return carry

        lax.fori_loop(1, g1, step, 0)
        vals = summarise(m)
        for c in range(4):
            recv1[t, 0, c] = vals[c]

    def power(value, doublings):
        for _ in range(doublings):
            value = cmul(value, value)
        return value

    def own_root():
        return ctable(m, 0)

    def middle_out(t):
        take(recv1.at[t, pl.ds(1, g1 - 1)], ex_recv.at[t, 0])
        block_root = power(own_root(), int(math.log2(rows)))

        def gather(j, carry):
            ahead, behind = carry
            slot_a = lax.rem(m - j + g1, g1)
            slot_b = lax.rem(m - (g1 - 1 - j) + g1, g1)
            ahead = cmadd(ahead, block_root, (recv1[t, slot_a, 0], recv1[t, slot_a, 1]))
            behind = cmadd(behind, block_root, (recv1[t, slot_b, 2], recv1[t, slot_b, 3]))
            return ahead, behind

        zero = jnp.zeros((8, 128), F32)
        ahead, behind = lax.fori_loop(0, g1, gather, ((zero, zero), (zero, zero)), unroll=True)
        for c, value in enumerate(ahead + behind):
            recv2[t, 0, c] = value

        def send(k, carry):
            peer = lax.rem(grp + k, g2) * g1 + m
            remote(recv2.at[t, 0], recv2.at[t, k], ex_send.at[t, 1], ex_recv.at[t, 1], (src, peer)).start()
            return carry

        lax.fori_loop(1, g2, send, 0)
        take(recv1.at[t, pl.ds(1, g1 - 1)], ex_send.at[t, 0])

    def middle_back(t):
        send3 = send3_all.at[t % 2]
        block_root = power(own_root(), int(math.log2(rows)))
        group_root = power(block_root, int(math.log2(g1)))
        turn = power(group_root, int(math.log2(g2)))
        real, imag = 1.0 - turn[0], turn[1]
        norm = 1.0 / (real * real + imag * imag)
        inverse = (real * norm, imag * norm)
        take(recv2.at[t, pl.ds(1, g2 - 1)], ex_recv.at[t, 1])
        left = (recv2[t, 0, 0], recv2[t, 0, 1])
        right = (recv2[t, 0, 2], recv2[t, 0, 3])
        for k in range(g2 - 1, 0, -1):
            left = cmadd(left, group_root, (recv2[t, k, 0], recv2[t, k, 1]))
            right = cmadd(right, group_root, (recv2[t, g2 - k, 2], recv2[t, g2 - k, 3]))
        left = cmul(left, inverse)
        right = cmul(right, inverse)

        def spread(j, carry):
            left, right = carry
            back = g1 - 1 - j
            for c in range(2):
                send3[j, c] = left[c]
                send3[back, 2 + c] = right[c]
            slot_a = lax.rem(m - j + g1, g1)
            slot_b = lax.rem(m - back + g1, g1)
            left = cmadd(left, block_root, (recv1[t, slot_a, 0], recv1[t, slot_a, 1]))
            right = cmadd(right, block_root, (recv1[t, slot_b, 2], recv1[t, slot_b, 3]))
            return left, right

        lax.fori_loop(0, g1, spread, (left, right), unroll=True)

        def send(k, carry):
            peer = lax.rem(m + k, g1)
            remote(send3.at[peer], recv3.at[t, k], ex_send.at[t, 2], ex_recv.at[t, 2], (src, base + peer)).start()
            return carry

        lax.fori_loop(1, g1, send, 0)
        for c in range(4):
            recv3[t, 0, c] = send3[m, c]
        take(recv2.at[t, pl.ds(1, g2 - 1)], ex_send.at[t, 1])

    def sweep_back(t):
        sp_ref = sp_all.at[t % 2]
        take(recv3.at[t, pl.ds(1, g1 - 1)], ex_recv.at[t, 2])

        def step(k, carry):
            part = lax.rem(m - k + g1, g1)
            root = ctable(part, 0)
            kappa = ctable(part, 1)
            rowv = [spectral(sp_ref, i, part) for i in range(rows)]
            state = (recv3[t, k, 0], recv3[t, k, 1])
            ahead = []
            for i in range(rows):
                state = cmadd(state, root, rowv[i])
                ahead.append(state)
            state = cmul((recv3[t, k, 2], recv3[t, k, 3]), root)
            for i in range(rows - 1, -1, -1):
                total = cmul((ahead[i][0] + state[0], ahead[i][1] + state[1]), kappa)
                tile(sp_ref, i, part, 0)[...] = total[0]
                tile(sp_ref, i, part, 1)[...] = total[1]
                if i:
                    state = cmul((state[0] + rowv[i][0], state[1] + rowv[i][1]), root)
            return carry

        lax.fori_loop(0, g1, step, 0)
        take(recv3.at[t, pl.ds(1, g1 - 1)], ex_send.at[t, 2])

    def pair(ref, x, z):
        return (ref[x, pl.ds(z, 8), :], ref[x, pl.ds(nz + z, 8), :])

    def put(ref, x, z, value):
        ref[x, pl.ds(z, 8), :] = value[0]
        ref[x, pl.ds(nz + z, 8), :] = value[1]

    def each_block(body, init):
        def outer(n, carry):
            return body(n // zgroups, pl.multiple_of(lax.rem(n, zgroups) * 8, 8), carry)

        return lax.fori_loop(0, rows * zgroups, outer, init, unroll=4)

    def square(value):
        return value[0] * value[0] + value[1] * value[1]

    zero = jnp.zeros((8, ny), F32)
    source_x = pos_ref[0, 0].astype(F32)
    source_y = pos_ref[0, 1].astype(F32)
    offset_y = lax.broadcasted_iota(jnp.int32, (8, ny), 1).astype(F32) - source_y
    offset_y_sq = offset_y * offset_y
    level = lax.broadcasted_iota(jnp.int32, (8, ny), 0).astype(F32) + SOURCE_GAP

    def begin(x, z, total):
        height = level + z.astype(F32)
        offset_x = (space * rows + x).astype(F32) - source_x
        dist = jnp.sqrt(height * height + offset_x * offset_x + offset_y_sq)
        turns = dist * (1.0 / 6.0)
        sine, cosine = half_turn(turns - jnp.floor(turns + 0.5))
        wave = (1.0 - 2.0 * sine * sine, 2.0 * sine * cosine)
        put(e_ref, x, z, wave)
        field = cmul(pair(chi0_ref, x, z), wave)
        put(w_ref, x, z, field)
        return total + square(field)

    object_part = each_block(begin, zero)
    data_part = jnp.zeros((1, ny), F32)
    for x in range(rows):
        for c in range(2):
            data_part = data_part + meas_ref[x, pl.ds(c, 1), :] * meas_ref[x, pl.ds(c, 1), :]
    data_fold = data_part[:, :128]
    for h in range(1, halves):
        data_fold = data_fold + data_part[:, h * 128:(h + 1) * 128]

    local(w_ref, sp_all.at[0])
    pl.semaphore_wait(barrier, (g1 - 1) + (ns * g2 - 1))
    sweep_out(0)
    reduce_start(0, [data_fold, fold(object_part)])
    middle_out(0)
    reduce_middle(0)
    middle_back(0)
    sums = reduce_end(0)
    sweep_back(0)
    local(sp_all.at[0], s_ref)
    data_total = sums[0:1]
    object_share = sums[1:2] / data_total
    ratio = 0.5 / DAMPING
    level_zero = 1.0 / math.sqrt(nz)
    chi_ref = chi0_ref
    for update in range(OUTER):
        t = 1 + 2 * update
        a = 1 + 2 * update
        last = update == OUTER - 1
        chi_next = chi_out_ref if last else chi1_ref
        early, late = early_recv.at[update], late_recv.at[update]

        for k in (2, 1, 3, 0):
            x = lax.rem(src + k, ns)

            def residual(n, carry, x=x, chi_ref=chi_ref):
                z = pl.multiple_of(n * 8, 8)
                chi = pair(chi_ref, x, z)
                e, s, w = pair(e_ref, x, z), pair(s_ref, x, z), pair(w_ref, x, z)
                u = (e[0] + s[0], e[1] + s[1])
                field = cmul(chi, u)
                res = (field[0] - w[0], field[1] - w[1])
                put(r_ref, x, z, res)
                flipped = cmul(chi, (res[0], -res[1]))
                put(v_ref, x, z, (-flipped[0], -flipped[1]))
                put(b_ref, x, z, (res[0] + ratio * flipped[1], res[1] + ratio * flipped[0]))
                early_ref[x, pl.ds(z, 8), :] = w[0] * u[0] + w[1] * u[1]
                early_ref[x, pl.ds(nz + z, 8), :] = w[1] * u[0] - w[0] * u[1]
                early_ref[x, pl.ds(2 * nz + z, 8), :] = square(u)
                return carry

            lax.fori_loop(0, zgroups, residual, 0, unroll=4)
            if k:
                remote(early_ref.at[x], early.at[k], x_send.at[update, 0], x_recv.at[update, 0], (x, space)).start()
        rho = jnp.concatenate(
            [
                meas_ref[x, pl.ds(c, 1), :] - s_ref[x, pl.ds(c * nz, 1), :]
                for x in range(rows) for c in range(2)
            ],
            axis=0,
        )
        rho_ref[...] = level_zero * dot3(split(rho), (hy_ref[0], hy_ref[1]))

        first, second = sp_all.at[t % 2], sp_all.at[(t + 1) % 2]
        local(v_ref, first)
        local(b_ref, second)
        if update:
            object_share = float(ns) * reduce_end(2)[0:1] / data_total

        def rho_tile(i, part, c, object_share=object_share):
            y = pl.multiple_of(lax.rem(part, halves) * 128, 128)
            return object_share * rho_ref[pl.ds(2 * i + c, 1), pl.ds(y, 128)]

        def add_first(i, part, value, rho_tile=rho_tile):
            return value[0] + rho_tile(i, part, 0), value[1] - rho_tile(i, part, 1)

        def add_second(i, part, value, rho_tile=rho_tile):
            return value[0] + ratio * rho_tile(i, part, 1), value[1] - ratio * rho_tile(i, part, 0)

        sweep_out(t, add_first)
        sweep_out(t + 1, add_second)
        middle_out(t)
        middle_out(t + 1)
        middle_back(t)
        middle_back(t + 1)
        sweep_back(t)
        local(first, d_ref)
        sweep_back(t + 1)
        local(second, v_ref)

        totals = (zero, zero)
        for k in (2, 1, 3, 0):
            x = lax.rem(src + k, ns)

            def descend(n, totals, x=x, chi_ref=chi_ref):
                z = pl.multiple_of(n * 8, 8)
                res, image, other = pair(r_ref, x, z), pair(d_ref, x, z), pair(v_ref, x, z)
                d = (res[0] + image[0], res[1] - image[1])
                h = (other[0] + ratio * image[1], other[1] + ratio * image[0])
                put(d_ref, x, z, d)
                put(v_ref, x, z, h)
                moved = cmul(pair(chi_ref, x, z), h)
                e, s, w = pair(e_ref, x, z), pair(s_ref, x, z), pair(w_ref, x, z)
                u = (e[0] + s[0], e[1] + s[1])
                late_parts = (
                    d[0] * u[0] + d[1] * u[1] + (w[0] * h[0] + w[1] * h[1]),
                    d[1] * u[0] - d[0] * u[1] + (w[1] * h[0] - w[0] * h[1]),
                    2.0 * (u[0] * h[0] + u[1] * h[1]),
                    d[0] * h[0] + d[1] * h[1],
                    d[1] * h[0] - d[0] * h[1],
                    square(h),
                )
                for c, value in enumerate(late_parts):
                    late_ref[x, pl.ds(c * nz + z, 8), :] = value
                return totals[0] + square(d), totals[1] + square((d[0] - moved[0], d[1] - moved[1]))

            totals = lax.fori_loop(0, zgroups, descend, totals, unroll=4)
            if k:
                remote(late_ref.at[x], late.at[k], x_send.at[update, 1], x_recv.at[update, 1], (x, space)).start()
        image_part = jnp.zeros((1, ny), F32)
        for x in range(rows):
            image_part = image_part + square((v_ref[x, pl.ds(0, 1), :], v_ref[x, pl.ds(nz, 1), :]))
        image_fold = image_part[:, :128]
        for h in range(1, halves):
            image_fold = image_fold + image_part[:, h * 128:(h + 1) * 128]
        reduce_start(a, [fold(totals[0]), image_fold, fold(totals[1])])
        take(early.at[pl.ds(1, ns - 1)], x_recv.at[update, 0])

        def gather_early(n, carry, early=early):
            at = pl.ds(pl.multiple_of(n * 8, 8), 8)
            early_ref[src, at, :] = early_ref[src, at, :] + early[1, at, :] + early[2, at, :] + early[3, at, :]
            return carry

        lax.fori_loop(0, 3 * zgroups, gather_early, 0, unroll=4)
        reduce_middle(a)
        sums = reduce_end(a)
        length = sums[0:1] / (object_share * sums[1:2] + sums[2:3])

        def advance(x, z, carry, length=length, last=last):
            w, d = pair(w_ref, x, z), pair(d_ref, x, z)
            put(w_ref, x, z, (w[0] + length * d[0], w[1] + length * d[1]))
            if not last:
                s, h = pair(s_ref, x, z), pair(v_ref, x, z)
                put(s_ref, x, z, (s[0] + length * h[0], s[1] + length * h[1]))
            return carry

        each_block(advance, 0)
        take(late.at[pl.ds(1, ns - 1)], x_recv.at[update, 1])

        def contrast(n, total, length=length, late=late, chi_next=chi_next):
            z = pl.multiple_of(n * 8, 8)
            sums = []
            for c in range(6):
                at = pl.ds(c * nz + z, 8)
                sums.append(late_ref[src, at, :] + late[1, at, :] + late[2, at, :] + late[3, at, :])
            parts = [
                early_ref[src, pl.ds(c * nz + z, 8), :] + length * (sums[c] + length * sums[3 + c]) for c in range(3)
            ]
            scale = 1.0 / jnp.maximum(parts[2], FLOOR_SHARE * ns)
            chi = (jnp.clip(parts[0] * scale, REAL_LOW, REAL_HIGH), jnp.clip(parts[1] * scale, 0.0, IMAG_HIGH))
            put(chi_next, src, z, chi)
            return total + square(chi)

        chi_part = lax.fori_loop(0, zgroups, contrast, zero, unroll=2)
        for k in (2, 1, 3):
            remote(chi_next.at[src], chi_next.at[src], x_send.at[update, 2], x_recv.at[update, 2],
                   (lax.rem(src + k, ns), space)).start()
        if not last:
            reduce_start(2, [fold(chi_part)])
            reduce_middle(2)
        take(chi_next.at[pl.ds(0, ns - 1)], x_recv.at[update, 2])
        take(early.at[pl.ds(1, ns - 1)], x_send.at[update, 0])
        take(late.at[pl.ds(1, ns - 1)], x_send.at[update, 1])
        take(chi_next.at[pl.ds(0, ns - 1)], x_send.at[update, 2])
        chi_ref = chi_next


def on_device(ns, g1, g2, contrast, measured, positions):
    _, nz, rows, ny = contrast.shape
    cfg = (ns, g1, g2, nz, ny, rows)
    transforms = 1 + 2 * OUTER
    reductions = 2 * OUTER
    chi0 = contrast.transpose(2, 0, 1, 3).reshape(rows, 2 * nz, ny)
    meas = measured[0].transpose(1, 0, 2)
    tables = decay_tables(nz, ny)
    hy = high_low(hartley(ny))
    hz = high_low(np.kron(np.eye(4), hartley(nz)))
    field = (rows, 2 * nz, ny)
    vmem = pl.BlockSpec(memory_space=pltpu.VMEM)
    w, chi = pl.pallas_call(
        functools.partial(kernel, cfg),
        out_shape=(jax.ShapeDtypeStruct(field, F32), jax.ShapeDtypeStruct(field, F32)),
        in_specs=[pl.BlockSpec(memory_space=pltpu.SMEM)] + [vmem] * 5,
        out_specs=(vmem, vmem),
        scratch_shapes=[pltpu.VMEM(field, F32)] * 7 + [
            pltpu.VMEM((2,) + field, F32),
            pltpu.VMEM((2 * rows, ny), F32),
            pltpu.VMEM((rows, 3 * nz, ny), F32),
            pltpu.VMEM((OUTER, ns, 3 * nz, ny), F32),
            pltpu.VMEM((rows, 6 * nz, ny), F32),
            pltpu.VMEM((OUTER, ns, 6 * nz, ny), F32),
            pltpu.VMEM((2, g1, 4, 8, 128), F32),
            pltpu.VMEM((2, g1, 4, 8, 128), F32),
            pltpu.VMEM((transforms, g1, 4, 8, 128), F32),
            pltpu.VMEM((transforms, g2, 4, 8, 128), F32),
            pltpu.VMEM((transforms, g1, 4, 8, 128), F32),
            pltpu.VMEM((reductions, g1, 8, 128), F32),
            pltpu.VMEM((reductions, ns * g2, 8, 128), F32),
            pltpu.SemaphoreType.DMA((transforms, 3)),
            pltpu.SemaphoreType.DMA((transforms, 3)),
            pltpu.SemaphoreType.DMA((reductions, 2)),
            pltpu.SemaphoreType.DMA((reductions, 2)),
            pltpu.SemaphoreType.DMA((OUTER, 3)),
            pltpu.SemaphoreType.DMA((OUTER, 3)),
        ],
        compiler_params=pltpu.CompilerParams(
            collective_id=0, has_side_effects=True, vmem_limit_bytes=40 * 1024 * 1024
        ),
    )(positions, chi0, meas, tables, hy, hz)
    sources = w.reshape(rows, 2, nz, ny).transpose(1, 2, 0, 3)[None]
    return sources, chi.reshape(rows, 2, nz, ny).transpose(1, 2, 0, 3)


def solution(mesh, g2=4):
    placed = (P(None, None, "space", None), P("src", None, "space", None), P("src", None))
    return jax.shard_map(
        functools.partial(on_device, mesh.shape["src"], mesh.shape["space"] // g2, g2),
        mesh=mesh,
        in_specs=placed,
        out_specs=(P("src", None, None, "space", None), P(None, None, "space", None)),
        check_vma=False,
    )
```

```python
import functools
import math

import jax
import jax.numpy as jnp
import ml_dtypes
import numpy as np
from jax import lax
from jax.experimental import pallas as pl
from jax.experimental.pallas import tpu as pltpu
from jax.sharding import PartitionSpec as P

OUTER = 2
WAVENUMBER = 2.0 * math.pi / 6.0
DAMPING = 0.3
SOURCE_GAP = 8.0
FLOOR_SHARE = 0.75
REAL_LOW = -0.25
REAL_HIGH = 0.35
IMAG_HIGH = 0.1
F32 = jnp.float32
BF16 = jnp.bfloat16
MESH = pl.DeviceIdType.MESH


def hartley(length):
    turn = np.outer(np.arange(length), np.arange(length)) % length
    angle = 2.0 * np.pi / length * turn
    return (np.cos(angle) + np.sin(angle)) / np.sqrt(length)


def high_low(table):
    high = table.astype(ml_dtypes.bfloat16)
    low = (table - high.astype(np.float64)).astype(ml_dtypes.bfloat16)
    return np.stack([high, low])


def modes(length):
    return 4.0 * np.sin(np.pi * np.arange(length) / length) ** 2


def decay_tables(depth, across):
    wave_sq = WAVENUMBER * WAVENUMBER
    trace = 2.0 + modes(depth)[:, None] + modes(across)[None, :] - wave_sq * (1.0 + 1j * DAMPING)
    root = np.sqrt(trace * trace - 4.0)
    first = (trace - root) / 2.0
    second = (trace + root) / 2.0
    small = np.where(np.abs(first) < np.abs(second), first, second)
    large = np.where(np.abs(first) < np.abs(second), second, first)
    small = 1.0 / large
    kappa = wave_sq / (large - small)
    tables = np.stack([small.real, small.imag, kappa.real, kappa.imag])
    return tables.astype(np.float32)


def cmul(a, b):
    return (a[0] * b[0] - a[1] * b[1], a[0] * b[1] + a[1] * b[0])


def cmadd(a, b, c):
    return (a[0] * b[0] - a[1] * b[1] + c[0], a[0] * b[1] + a[1] * b[0] + c[1])


def half_turn(fraction):
    angle = fraction * math.pi
    sq = angle * angle
    sine = jnp.full_like(sq, -1.0 / math.factorial(11))
    for order in (9, 7, 5, 3, 1):
        sine = sine * sq + (1.0 if order % 4 == 1 else -1.0) / math.factorial(order)
    cosine = jnp.full_like(sq, 1.0 / math.factorial(12))
    for order in (10, 8, 6, 4, 2, 0):
        cosine = cosine * sq + (1.0 if order % 4 == 0 else -1.0) / math.factorial(order)
    return sine * angle, cosine


def kernel(
    cfg,
    pos_ref, chi0_ref, meas_ref, tab_ref, hy_ref, hz_ref,
    w_ref, chi_out_ref,
    chi1_ref, e_ref, s_ref, r_ref, d_ref, v_ref, b_ref, sp_all, rho_ref, early_ref, early_recv, late_ref, late_recv,
    send0_all, send1_all, send3_all, states_all, sums, recv1, recv2, recv3, recv4, red1, red2,
    ex_send, ex_recv, red_send, red_recv, x_send, x_recv,
):
    ns, g1, g2, nz, ny, rows = cfg
    halves = ny // 128
    nx = g1 * g2 * rows
    zgroups = nz // 8
    src = lax.axis_index("src")
    space = lax.axis_index("space")
    m = lax.rem(space, g1)
    chips = g1 // 2
    core = lax.rem(m, 2)
    chip = m // 2
    grp = space // g1
    base = grp * g1

    partner = (src, space + 1 - 2 * core)

    barrier = pltpu.get_barrier_semaphore()

    def greet_group(k, carry):
        pl.semaphore_signal(barrier, inc=1, device_id=(src, base + lax.rem(m + k, g1)), device_id_type=MESH)
        return carry

    def cross_peer(k):
        return lax.rem(src + k // g2, ns), lax.rem(grp + lax.rem(k, g2), g2) * g1 + m

    def greet_cross(k, carry):
        pl.semaphore_signal(barrier, inc=1, device_id=cross_peer(k), device_id_type=MESH)
        return carry

    lax.fori_loop(1, g1, greet_group, 0)
    lax.fori_loop(1, ns * g2, greet_cross, 0)

    def remote(src_ref, dst_ref, send_sem, recv_sem, device):
        return pltpu.make_async_remote_copy(
            src_ref=src_ref, dst_ref=dst_ref, send_sem=send_sem, recv_sem=recv_sem,
            device_id=device, device_id_type=MESH,
        )

    def take(ref, sem):
        pltpu.make_async_copy(ref, ref, sem).wait()

    def reduce_start(a, parts):
        red1[a, 0] = jnp.concatenate(parts + [jnp.zeros((8 - len(parts), 128), F32)], axis=0)

        def send(k, carry):
            remote(red1.at[a, 0], red1.at[a, k], red_send.at[a, 0], red_recv.at[a, 0],
                   (src, base + lax.rem(m + k, g1))).start()
            return carry

        lax.fori_loop(1, g1, send, 0)

    def reduce_middle(a):
        take(red1.at[a, pl.ds(1, g1 - 1)], red_recv.at[a, 0])

        def add(j, total):
            return total + red1[a, lax.rem(m - j + g1, g1)]

        red2[a, 0] = lax.fori_loop(0, g1, add, jnp.zeros((8, 128), F32), unroll=True)
        take(red1.at[a, pl.ds(1, g1 - 1)], red_send.at[a, 0])

        def send(k, carry):
            remote(red2.at[a, 0], red2.at[a, k], red_send.at[a, 1], red_recv.at[a, 1], cross_peer(k)).start()
            return carry

        lax.fori_loop(1, ns * g2, send, 0)

    def reduce_end(a):
        count = ns * g2
        take(red2.at[a, pl.ds(1, count - 1)], red_recv.at[a, 1])

        def add(j, total):
            slot = lax.rem(src - j // g2 + ns, ns) * g2 + lax.rem(grp - lax.rem(j, g2) + g2, g2)
            return total + red2[a, slot]

        total = lax.fori_loop(0, count, add, jnp.zeros((8, 128), F32), unroll=True)
        take(red2.at[a, pl.ds(1, count - 1)], red_send.at[a, 1])
        return jnp.sum(total, axis=1, keepdims=True)

    def fold(acc):
        part = acc[:, :128]
        for h in range(1, halves):
            part = part + acc[:, h * 128:(h + 1) * 128]
        return jnp.sum(part, axis=0, keepdims=True)

    def split(a):
        high = a.astype(BF16)
        return high, (a - high.astype(F32)).astype(BF16)

    def dot3(a, b):
        mm = functools.partial(jnp.dot, preferred_element_type=F32)
        return mm(a[0], b[0]) + (mm(a[1], b[0]) + mm(a[0], b[1]))

    def local(src_ref, dst_ref):
        hz = (hz_ref[0], hz_ref[1])
        hy = (hy_ref[0], hy_ref[1])
        for pair in range(rows // 2):
            block = src_ref[pl.ds(2 * pair, 2)].reshape(4 * nz, ny)
            depth_done = dot3(hz, split(block))
            done = dot3(split(depth_done), hy)
            dst_ref[pl.ds(2 * pair, 2)] = done.reshape(2, 2 * nz, ny)

    def tile(ref, lead, part, comp):
        z = pl.multiple_of(part // halves * 8, 8)
        y = pl.multiple_of(lax.rem(part, halves) * 128, 128)
        return ref.at[lead, pl.ds(comp * nz + z, 8), pl.ds(y, 128)]

    def ctable(part, which):
        z = pl.multiple_of(part // halves * 8, 8)
        y = pl.multiple_of(lax.rem(part, halves) * 128, 128)
        return tuple(tab_ref[2 * which + c, pl.ds(z, 8), pl.ds(y, 128)] for c in range(2))

    def spectral(sp_ref, lead, part):
        return (tile(sp_ref, lead, part, 0)[...], tile(sp_ref, lead, part, 1)[...])

    def sweep_out(t, extra=None):
        sp_ref, send0, send1 = sp_all.at[t % 2], send0_all.at[t % 2], send1_all.at[t % 2]

        def summarise(part):
            root = ctable(part, 0)
            rowv = [spectral(sp_ref, i, part) for i in range(rows)]
            if extra is not None:
                rowv = [extra(i, part, value) for i, value in enumerate(rowv)]
                for i in range(rows):
                    tile(sp_ref, i, part, 0)[...] = rowv[i][0]
                    tile(sp_ref, i, part, 1)[...] = rowv[i][1]
            ahead = rowv[0]
            for i in range(1, rows):
                ahead = cmadd(ahead, root, rowv[i])
            behind = rowv[rows - 1]
            for i in range(rows - 2, -1, -1):
                behind = cmadd(behind, root, rowv[i])
            return ahead + behind

        def other_half(k, carry):
            g = lax.rem(chip + k, chips)
            vals = summarise(2 * g + 1 - core)
            for c in range(4):
                send0[g, c] = vals[c]
            remote(send0.at[g], sums.at[t, core, g], ex_send.at[t, 0], ex_recv.at[t, 0], partner).start()
            return carry

        def own_half(k, carry):
            g = lax.rem(chip + k, chips)
            vals = summarise(2 * g + core)
            for c in range(4):
                sums[t, core, g, c] = vals[c]
            return carry

        lax.fori_loop(1, chips + 1, other_half, 0, unroll=2)
        lax.fori_loop(1, chips + 1, own_half, 0, unroll=2)
        take(sums.at[t, 1 - core], ex_recv.at[t, 0])

        def combine(g):
            block_root = power(ctable(2 * g + core, 0), int(math.log2(rows)))
            first = [sums[t, 0, g, c] for c in range(4)]
            second = [sums[t, 1, g, c] for c in range(4)]
            return cmadd(first[:2], block_root, second[:2]) + cmadd(second[2:], block_root, first[2:])

        def step(k, carry):
            g = lax.rem(chip + k, chips)
            vals = combine(g)
            for c in range(4):
                send1[g, c] = vals[c]
            remote(send1.at[g], recv1.at[t, k], ex_send.at[t, 1], ex_recv.at[t, 1],
                   (src, base + 2 * g + core)).start()
            return carry

        lax.fori_loop(1, chips, step, 0)
        vals = combine(chip)
        for c in range(4):
            recv1[t, 0, c] = vals[c]

    def power(value, doublings):
        for _ in range(doublings):
            value = cmul(value, value)
        return value

    def own_root():
        return ctable(m, 0)

    def chip_root():
        return power(own_root(), int(math.log2(2 * rows)))

    def middle_out(t):
        take(recv1.at[t, pl.ds(1, chips - 1)], ex_recv.at[t, 1])
        root = chip_root()

        def gather(j, carry):
            ahead, behind = carry
            slot_a = lax.rem(chip - j + chips, chips)
            slot_b = lax.rem(chip + 1 + j, chips)
            ahead = cmadd(ahead, root, (recv1[t, slot_a, 0], recv1[t, slot_a, 1]))
            behind = cmadd(behind, root, (recv1[t, slot_b, 2], recv1[t, slot_b, 3]))
            return ahead, behind

        zero = jnp.zeros((8, 128), F32)
        ahead, behind = lax.fori_loop(0, chips, gather, ((zero, zero), (zero, zero)), unroll=True)
        for c, value in enumerate(ahead + behind):
            recv2[t, 0, c] = value

        def send(k, carry):
            peer = lax.rem(grp + k, g2) * g1 + m
            remote(recv2.at[t, 0], recv2.at[t, k], ex_send.at[t, 2], ex_recv.at[t, 2], (src, peer)).start()
            return carry

        lax.fori_loop(1, g2, send, 0)

    def middle_back(t):
        send3 = send3_all.at[t % 2]
        root = chip_root()
        group_root = power(root, int(math.log2(chips)))
        turn = power(group_root, int(math.log2(g2)))
        real, imag = 1.0 - turn[0], turn[1]
        norm = 1.0 / (real * real + imag * imag)
        inverse = (real * norm, imag * norm)
        take(recv2.at[t, pl.ds(1, g2 - 1)], ex_recv.at[t, 2])
        left = (recv2[t, 0, 0], recv2[t, 0, 1])
        right = (recv2[t, 0, 2], recv2[t, 0, 3])
        for k in range(g2 - 1, 0, -1):
            left = cmadd(left, group_root, (recv2[t, k, 0], recv2[t, k, 1]))
            right = cmadd(right, group_root, (recv2[t, g2 - k, 2], recv2[t, g2 - k, 3]))
        left = cmul(left, inverse)
        right = cmul(right, inverse)

        def spread(j, carry):
            left, right = carry
            back = chips - 1 - j
            for c in range(2):
                send3[j, c] = left[c]
                send3[back, 2 + c] = right[c]
            slot_a = lax.rem(chip - j + chips, chips)
            slot_b = lax.rem(chip + 1 + j, chips)
            left = cmadd(left, root, (recv1[t, slot_a, 0], recv1[t, slot_a, 1]))
            right = cmadd(right, root, (recv1[t, slot_b, 2], recv1[t, slot_b, 3]))
            return left, right

        lax.fori_loop(0, chips, spread, (left, right), unroll=True)

        def send(k, carry):
            g = lax.rem(chip + k, chips)
            remote(send3.at[g], recv3.at[t, k], ex_send.at[t, 3], ex_recv.at[t, 3],
                   (src, base + 2 * g + core)).start()
            return carry

        lax.fori_loop(1, chips, send, 0)
        for c in range(4):
            recv3[t, 0, c] = send3[chip, c]

    def sweep_back(t):
        sp_ref, states = sp_all.at[t % 2], states_all.at[t % 2]
        take(recv3.at[t, pl.ds(1, chips - 1)], ex_recv.at[t, 3])

        def pass_on(k, carry):
            g = lax.rem(chip - k + chips, chips)
            block_root = power(ctable(2 * g + core, 0), int(math.log2(rows)))
            left = (recv3[t, k, 0], recv3[t, k, 1])
            right = (recv3[t, k, 2], recv3[t, k, 3])
            inner_left = cmadd(left, block_root, (sums[t, 0, g, 0], sums[t, 0, g, 1]))
            inner_right = cmadd(right, block_root, (sums[t, 1, g, 2], sums[t, 1, g, 3]))
            for c in range(2):
                states[0, g, c] = left[c]
                states[0, g, 2 + c] = inner_right[c]
                states[1, g, c] = inner_left[c]
                states[1, g, 2 + c] = right[c]
            remote(states.at[1 - core, g], recv4.at[t, g], ex_send.at[t, 4], ex_recv.at[t, 4], partner).start()
            return carry

        lax.fori_loop(0, chips, pass_on, 0, unroll=2)

        def apply(part, ends):
            root = ctable(part, 0)
            kappa = ctable(part, 1)
            rowv = [spectral(sp_ref, i, part) for i in range(rows)]
            state = ends[:2]
            ahead = []
            for i in range(rows):
                state = cmadd(state, root, rowv[i])
                ahead.append(state)
            state = cmul(ends[2:], root)
            for i in range(rows - 1, -1, -1):
                total = cmul((ahead[i][0] + state[0], ahead[i][1] + state[1]), kappa)
                tile(sp_ref, i, part, 0)[...] = total[0]
                tile(sp_ref, i, part, 1)[...] = total[1]
                if i:
                    state = cmul((state[0] + rowv[i][0], state[1] + rowv[i][1]), root)

        def own_half(g, carry):
            apply(2 * g + core, tuple(states[core, g, c] for c in range(4)))
            return carry

        def other_half(g, carry):
            apply(2 * g + 1 - core, tuple(recv4[t, g, c] for c in range(4)))
            return carry

        lax.fori_loop(0, chips, own_half, 0, unroll=2)
        take(recv4.at[t], ex_recv.at[t, 4])
        lax.fori_loop(0, chips, other_half, 0, unroll=2)

    def finish(t):
        take(recv4.at[t], ex_send.at[t, 0])
        take(recv1.at[t, pl.ds(1, chips - 1)], ex_send.at[t, 1])
        take(recv2.at[t, pl.ds(1, g2 - 1)], ex_send.at[t, 2])
        take(recv3.at[t, pl.ds(1, chips - 1)], ex_send.at[t, 3])
        take(recv4.at[t], ex_send.at[t, 4])

    def pair(ref, x, z):
        return (ref[x, pl.ds(z, 8), :], ref[x, pl.ds(nz + z, 8), :])

    def put(ref, x, z, value):
        ref[x, pl.ds(z, 8), :] = value[0]
        ref[x, pl.ds(nz + z, 8), :] = value[1]

    def each_block(body, init):
        def outer(n, carry):
            return body(n // zgroups, pl.multiple_of(lax.rem(n, zgroups) * 8, 8), carry)

        return lax.fori_loop(0, rows * zgroups, outer, init, unroll=4)

    def square(value):
        return value[0] * value[0] + value[1] * value[1]

    zero = jnp.zeros((8, ny), F32)
    source_x = pos_ref[0, 0].astype(F32)
    source_y = pos_ref[0, 1].astype(F32)
    offset_y = lax.broadcasted_iota(jnp.int32, (8, ny), 1).astype(F32) - source_y
    offset_y_sq = offset_y * offset_y
    level = lax.broadcasted_iota(jnp.int32, (8, ny), 0).astype(F32) + SOURCE_GAP

    def begin(x, z, total):
        height = level + z.astype(F32)
        offset_x = (space * rows + x).astype(F32) - source_x
        dist = jnp.sqrt(height * height + offset_x * offset_x + offset_y_sq)
        turns = dist * (1.0 / 6.0)
        sine, cosine = half_turn(turns - jnp.floor(turns + 0.5))
        wave = (1.0 - 2.0 * sine * sine, 2.0 * sine * cosine)
        put(e_ref, x, z, wave)
        field = cmul(pair(chi0_ref, x, z), wave)
        put(w_ref, x, z, field)
        return total + square(field)

    object_part = each_block(begin, zero)
    data_part = jnp.zeros((1, ny), F32)
    for x in range(rows):
        for c in range(2):
            data_part = data_part + meas_ref[x, pl.ds(c, 1), :] * meas_ref[x, pl.ds(c, 1), :]
    data_fold = data_part[:, :128]
    for h in range(1, halves):
        data_fold = data_fold + data_part[:, h * 128:(h + 1) * 128]

    local(w_ref, sp_all.at[0])
    pl.semaphore_wait(barrier, (g1 - 1) + (ns * g2 - 1))
    sweep_out(0)
    reduce_start(0, [data_fold, fold(object_part)])
    middle_out(0)
    reduce_middle(0)
    middle_back(0)
    totals = reduce_end(0)
    sweep_back(0)
    finish(0)
    local(sp_all.at[0], s_ref)
    data_total = totals[0:1]
    object_share = totals[1:2] / data_total
    ratio = 0.5 / DAMPING
    level_zero = 1.0 / math.sqrt(nz)
    chi_ref = chi0_ref
    for update in range(OUTER):
        t = 1 + 2 * update
        a = 1 + 2 * update
        last = update == OUTER - 1
        chi_next = chi_out_ref if last else chi1_ref
        early, late = early_recv.at[update], late_recv.at[update]

        for k in (2, 1, 3, 0):
            x = lax.rem(src + k, ns)

            def residual(n, carry, x=x, chi_ref=chi_ref):
                z = pl.multiple_of(n * 8, 8)
                chi = pair(chi_ref, x, z)
                e, s, w = pair(e_ref, x, z), pair(s_ref, x, z), pair(w_ref, x, z)
                u = (e[0] + s[0], e[1] + s[1])
                field = cmul(chi, u)
                res = (field[0] - w[0], field[1] - w[1])
                put(r_ref, x, z, res)
                flipped = cmul(chi, (res[0], -res[1]))
                put(v_ref, x, z, (-flipped[0], -flipped[1]))
                put(b_ref, x, z, (res[0] + ratio * flipped[1], res[1] + ratio * flipped[0]))
                early_ref[x, pl.ds(z, 8), :] = w[0] * u[0] + w[1] * u[1]
                early_ref[x, pl.ds(nz + z, 8), :] = w[1] * u[0] - w[0] * u[1]
                early_ref[x, pl.ds(2 * nz + z, 8), :] = square(u)
                return carry

            lax.fori_loop(0, zgroups, residual, 0, unroll=4)
            if k:
                remote(early_ref.at[x], early.at[k], x_send.at[update, 0], x_recv.at[update, 0], (x, space)).start()
        rho = jnp.concatenate(
            [
                meas_ref[x, pl.ds(c, 1), :] - s_ref[x, pl.ds(c * nz, 1), :]
                for x in range(rows) for c in range(2)
            ],
            axis=0,
        )
        rho_ref[...] = level_zero * dot3(split(rho), (hy_ref[0], hy_ref[1]))

        first, second = sp_all.at[t % 2], sp_all.at[(t + 1) % 2]
        local(v_ref, first)
        local(b_ref, second)
        if update:
            object_share = float(ns) * reduce_end(2)[0:1] / data_total

        def rho_tile(i, part, c, object_share=object_share):
            y = pl.multiple_of(lax.rem(part, halves) * 128, 128)
            return object_share * rho_ref[pl.ds(2 * i + c, 1), pl.ds(y, 128)]

        def add_first(i, part, value, rho_tile=rho_tile):
            return value[0] + rho_tile(i, part, 0), value[1] - rho_tile(i, part, 1)

        def add_second(i, part, value, rho_tile=rho_tile):
            return value[0] + ratio * rho_tile(i, part, 1), value[1] - ratio * rho_tile(i, part, 0)

        sweep_out(t, add_first)
        sweep_out(t + 1, add_second)
        middle_out(t)
        middle_out(t + 1)
        middle_back(t)
        middle_back(t + 1)
        sweep_back(t)
        local(first, d_ref)
        sweep_back(t + 1)
        local(second, v_ref)
        finish(t)
        finish(t + 1)

        totals = (zero, zero)
        for k in (2, 1, 3, 0):
            x = lax.rem(src + k, ns)

            def descend(n, totals, x=x, chi_ref=chi_ref):
                z = pl.multiple_of(n * 8, 8)
                res, image, other = pair(r_ref, x, z), pair(d_ref, x, z), pair(v_ref, x, z)
                d = (res[0] + image[0], res[1] - image[1])
                h = (other[0] + ratio * image[1], other[1] + ratio * image[0])
                put(d_ref, x, z, d)
                put(v_ref, x, z, h)
                moved = cmul(pair(chi_ref, x, z), h)
                e, s, w = pair(e_ref, x, z), pair(s_ref, x, z), pair(w_ref, x, z)
                u = (e[0] + s[0], e[1] + s[1])
                late_parts = (
                    d[0] * u[0] + d[1] * u[1] + (w[0] * h[0] + w[1] * h[1]),
                    d[1] * u[0] - d[0] * u[1] + (w[1] * h[0] - w[0] * h[1]),
                    2.0 * (u[0] * h[0] + u[1] * h[1]),
                    d[0] * h[0] + d[1] * h[1],
                    d[1] * h[0] - d[0] * h[1],
                    square(h),
                )
                for c, value in enumerate(late_parts):
                    late_ref[x, pl.ds(c * nz + z, 8), :] = value
                return totals[0] + square(d), totals[1] + square((d[0] - moved[0], d[1] - moved[1]))

            totals = lax.fori_loop(0, zgroups, descend, totals, unroll=4)
            if k:
                remote(late_ref.at[x], late.at[k], x_send.at[update, 1], x_recv.at[update, 1], (x, space)).start()
        image_part = jnp.zeros((1, ny), F32)
        for x in range(rows):
            image_part = image_part + square((v_ref[x, pl.ds(0, 1), :], v_ref[x, pl.ds(nz, 1), :]))
        image_fold = image_part[:, :128]
        for h in range(1, halves):
            image_fold = image_fold + image_part[:, h * 128:(h + 1) * 128]
        reduce_start(a, [fold(totals[0]), image_fold, fold(totals[1])])
        take(early.at[pl.ds(1, ns - 1)], x_recv.at[update, 0])

        def gather_early(n, carry, early=early):
            at = pl.ds(pl.multiple_of(n * 8, 8), 8)
            early_ref[src, at, :] = early_ref[src, at, :] + early[1, at, :] + early[2, at, :] + early[3, at, :]
            return carry

        lax.fori_loop(0, 3 * zgroups, gather_early, 0, unroll=4)
        reduce_middle(a)
        totals = reduce_end(a)
        length = totals[0:1] / (object_share * totals[1:2] + totals[2:3])

        def advance(x, z, carry, length=length, last=last):
            w, d = pair(w_ref, x, z), pair(d_ref, x, z)
            put(w_ref, x, z, (w[0] + length * d[0], w[1] + length * d[1]))
            if not last:
                s, h = pair(s_ref, x, z), pair(v_ref, x, z)
                put(s_ref, x, z, (s[0] + length * h[0], s[1] + length * h[1]))
            return carry

        each_block(advance, 0)
        take(late.at[pl.ds(1, ns - 1)], x_recv.at[update, 1])

        def contrast(n, total, length=length, late=late, chi_next=chi_next):
            z = pl.multiple_of(n * 8, 8)
            terms = []
            for c in range(6):
                at = pl.ds(c * nz + z, 8)
                terms.append(late_ref[src, at, :] + late[1, at, :] + late[2, at, :] + late[3, at, :])
            parts = [
                early_ref[src, pl.ds(c * nz + z, 8), :] + length * (terms[c] + length * terms[3 + c]) for c in range(3)
            ]
            scale = 1.0 / jnp.maximum(parts[2], FLOOR_SHARE * ns)
            chi = (jnp.clip(parts[0] * scale, REAL_LOW, REAL_HIGH), jnp.clip(parts[1] * scale, 0.0, IMAG_HIGH))
            put(chi_next, src, z, chi)
            return total + square(chi)

        chi_part = lax.fori_loop(0, zgroups, contrast, zero, unroll=2)
        for k in (2, 1, 3):
            remote(chi_next.at[src], chi_next.at[src], x_send.at[update, 2], x_recv.at[update, 2],
                   (lax.rem(src + k, ns), space)).start()
        if not last:
            reduce_start(2, [fold(chi_part)])
            reduce_middle(2)
        take(chi_next.at[pl.ds(0, ns - 1)], x_recv.at[update, 2])
        take(early.at[pl.ds(1, ns - 1)], x_send.at[update, 0])
        take(late.at[pl.ds(1, ns - 1)], x_send.at[update, 1])
        take(chi_next.at[pl.ds(0, ns - 1)], x_send.at[update, 2])
        chi_ref = chi_next


def on_device(ns, g1, g2, contrast, measured, positions):
    _, nz, rows, ny = contrast.shape
    cfg = (ns, g1, g2, nz, ny, rows)
    transforms = 1 + 2 * OUTER
    reductions = 2 * OUTER
    chi0 = contrast.transpose(2, 0, 1, 3).reshape(rows, 2 * nz, ny)
    meas = measured[0].transpose(1, 0, 2)
    tables = decay_tables(nz, ny)
    hy = high_low(hartley(ny))
    hz = high_low(np.kron(np.eye(4), hartley(nz)))
    field = (rows, 2 * nz, ny)
    vmem = pl.BlockSpec(memory_space=pltpu.VMEM)
    w, chi = pl.pallas_call(
        functools.partial(kernel, cfg),
        out_shape=(jax.ShapeDtypeStruct(field, F32), jax.ShapeDtypeStruct(field, F32)),
        in_specs=[pl.BlockSpec(memory_space=pltpu.SMEM)] + [vmem] * 5,
        out_specs=(vmem, vmem),
        scratch_shapes=[pltpu.VMEM(field, F32)] * 7 + [
            pltpu.VMEM((2,) + field, F32),
            pltpu.VMEM((2 * rows, ny), F32),
            pltpu.VMEM((rows, 3 * nz, ny), F32),
            pltpu.VMEM((OUTER, ns, 3 * nz, ny), F32),
            pltpu.VMEM((rows, 6 * nz, ny), F32),
            pltpu.VMEM((OUTER, ns, 6 * nz, ny), F32),
            pltpu.VMEM((2, g1 // 2, 4, 8, 128), F32),
            pltpu.VMEM((2, g1 // 2, 4, 8, 128), F32),
            pltpu.VMEM((2, g1 // 2, 4, 8, 128), F32),
            pltpu.VMEM((2, 2, g1 // 2, 4, 8, 128), F32),
            pltpu.VMEM((transforms, 2, g1 // 2, 4, 8, 128), F32),
            pltpu.VMEM((transforms, g1 // 2, 4, 8, 128), F32),
            pltpu.VMEM((transforms, g2, 4, 8, 128), F32),
            pltpu.VMEM((transforms, g1 // 2, 4, 8, 128), F32),
            pltpu.VMEM((transforms, g1 // 2, 4, 8, 128), F32),
            pltpu.VMEM((reductions, g1, 8, 128), F32),
            pltpu.VMEM((reductions, ns * g2, 8, 128), F32),
            pltpu.SemaphoreType.DMA((transforms, 5)),
            pltpu.SemaphoreType.DMA((transforms, 5)),
            pltpu.SemaphoreType.DMA((reductions, 2)),
            pltpu.SemaphoreType.DMA((reductions, 2)),
            pltpu.SemaphoreType.DMA((OUTER, 3)),
            pltpu.SemaphoreType.DMA((OUTER, 3)),
        ],
        compiler_params=pltpu.CompilerParams(
            collective_id=0, has_side_effects=True, vmem_limit_bytes=40 * 1024 * 1024
        ),
    )(positions, chi0, meas, tables, hy, hz)
    sources = w.reshape(rows, 2, nz, ny).transpose(1, 2, 0, 3)[None]
    return sources, chi.reshape(rows, 2, nz, ny).transpose(1, 2, 0, 3)


def solution(mesh, g2=4):
    placed = (P(None, None, "space", None), P("src", None, "space", None), P("src", None))
    return jax.shard_map(
        functools.partial(on_device, mesh.shape["src"], mesh.shape["space"] // g2, g2),
        mesh=mesh,
        in_specs=placed,
        out_specs=(P("src", None, None, "space", None), P(None, None, "space", None)),
        check_vma=False,
    )
```

```python
import functools
import math

import jax
import jax.numpy as jnp
import ml_dtypes
import numpy as np
from jax import lax
from jax.experimental import pallas as pl
from jax.experimental.pallas import tpu as pltpu
from jax.sharding import PartitionSpec as P

OUTER = 2
WAVENUMBER = 2.0 * math.pi / 6.0
DAMPING = 0.3
SOURCE_GAP = 8.0
FLOOR_SHARE = 0.75
REAL_LOW = -0.25
REAL_HIGH = 0.35
IMAG_HIGH = 0.1
F32 = jnp.float32
BF16 = jnp.bfloat16
MESH = pl.DeviceIdType.MESH


def hartley(length):
    turn = np.outer(np.arange(length), np.arange(length)) % length
    angle = 2.0 * np.pi / length * turn
    return (np.cos(angle) + np.sin(angle)) / np.sqrt(length)


def high_low(table):
    high = table.astype(ml_dtypes.bfloat16)
    low = (table - high.astype(np.float64)).astype(ml_dtypes.bfloat16)
    return np.stack([high, low])


def modes(length):
    return 4.0 * np.sin(np.pi * np.arange(length) / length) ** 2


def decay_tables(depth, across):
    wave_sq = WAVENUMBER * WAVENUMBER
    trace = 2.0 + modes(depth)[:, None] + modes(across)[None, :] - wave_sq * (1.0 + 1j * DAMPING)
    root = np.sqrt(trace * trace - 4.0)
    first = (trace - root) / 2.0
    second = (trace + root) / 2.0
    small = np.where(np.abs(first) < np.abs(second), first, second)
    large = np.where(np.abs(first) < np.abs(second), second, first)
    small = 1.0 / large
    kappa = wave_sq / (large - small)
    tables = np.stack([small.real, small.imag, kappa.real, kappa.imag])
    return tables.astype(np.float32)


def cmul(a, b):
    return (a[0] * b[0] - a[1] * b[1], a[0] * b[1] + a[1] * b[0])


def cmadd(a, b, c):
    return (a[0] * b[0] - a[1] * b[1] + c[0], a[0] * b[1] + a[1] * b[0] + c[1])


def half_turn(fraction):
    angle = fraction * math.pi
    sq = angle * angle
    sine = jnp.full_like(sq, -1.0 / math.factorial(11))
    for order in (9, 7, 5, 3, 1):
        sine = sine * sq + (1.0 if order % 4 == 1 else -1.0) / math.factorial(order)
    cosine = jnp.full_like(sq, 1.0 / math.factorial(12))
    for order in (10, 8, 6, 4, 2, 0):
        cosine = cosine * sq + (1.0 if order % 4 == 0 else -1.0) / math.factorial(order)
    return sine * angle, cosine


def kernel(
    cfg,
    pos_ref, chi0_ref, meas_ref, tab_ref, hy_ref, hz_ref,
    w_ref, chi_out_ref,
    chi1_ref, e_ref, s_ref, r_ref, d_ref, v_ref, b_ref, sp_all, rho_ref, early_ref, early_recv, late_ref, late_recv,
    send0_all, send1_all, send3_all, states_all, sums, recv1, recv2, recv3, recv4, red1, red2,
    ex_send, ex_recv, red_send, red_recv, x_send, x_recv, late_send, late_took, chi_took,
):
    ns, g1, g2, nz, ny, rows = cfg
    halves = ny // 128
    nx = g1 * g2 * rows
    zgroups = nz // 8
    src = lax.axis_index("src")
    space = lax.axis_index("space")
    m = lax.rem(space, g1)
    chips = g1 // 2
    core = lax.rem(m, 2)
    chip = m // 2
    grp = space // g1
    base = grp * g1

    partner = (src, space + 1 - 2 * core)

    barrier = pltpu.get_barrier_semaphore()

    def greet_group(k, carry):
        pl.semaphore_signal(barrier, inc=1, device_id=(src, base + lax.rem(m + k, g1)), device_id_type=MESH)
        return carry

    def cross_peer(k):
        return lax.rem(src + k // g2, ns), lax.rem(grp + lax.rem(k, g2), g2) * g1 + m

    def greet_cross(k, carry):
        pl.semaphore_signal(barrier, inc=1, device_id=cross_peer(k), device_id_type=MESH)
        return carry

    lax.fori_loop(1, g1, greet_group, 0)
    lax.fori_loop(1, ns * g2, greet_cross, 0)

    def remote(src_ref, dst_ref, send_sem, recv_sem, device):
        return pltpu.make_async_remote_copy(
            src_ref=src_ref, dst_ref=dst_ref, send_sem=send_sem, recv_sem=recv_sem,
            device_id=device, device_id_type=MESH,
        )

    def take(ref, sem):
        pltpu.make_async_copy(ref, ref, sem).wait()

    def reduce_start(a, parts):
        red1[a, 0] = jnp.concatenate(parts + [jnp.zeros((8 - len(parts), 128), F32)], axis=0)

        def send(k, carry):
            remote(red1.at[a, 0], red1.at[a, k], red_send.at[a, 0], red_recv.at[a, 0],
                   (src, base + lax.rem(m + k, g1))).start()
            return carry

        lax.fori_loop(1, g1, send, 0)

    def reduce_middle(a):
        take(red1.at[a, pl.ds(1, g1 - 1)], red_recv.at[a, 0])

        def add(j, total):
            return total + red1[a, lax.rem(m - j + g1, g1)]

        red2[a, 0] = lax.fori_loop(0, g1, add, jnp.zeros((8, 128), F32), unroll=True)
        take(red1.at[a, pl.ds(1, g1 - 1)], red_send.at[a, 0])

        def send(k, carry):
            remote(red2.at[a, 0], red2.at[a, k], red_send.at[a, 1], red_recv.at[a, 1], cross_peer(k)).start()
            return carry

        lax.fori_loop(1, ns * g2, send, 0)

    def reduce_end(a):
        count = ns * g2
        take(red2.at[a, pl.ds(1, count - 1)], red_recv.at[a, 1])

        def add(j, total):
            slot = lax.rem(src - j // g2 + ns, ns) * g2 + lax.rem(grp - lax.rem(j, g2) + g2, g2)
            return total + red2[a, slot]

        total = lax.fori_loop(0, count, add, jnp.zeros((8, 128), F32), unroll=True)
        take(red2.at[a, pl.ds(1, count - 1)], red_send.at[a, 1])
        return jnp.sum(total, axis=1, keepdims=True)

    def fold(acc):
        part = acc[:, :128]
        for h in range(1, halves):
            part = part + acc[:, h * 128:(h + 1) * 128]
        return jnp.sum(part, axis=0, keepdims=True)

    def split(a):
        high = a.astype(BF16)
        return high, (a - high.astype(F32)).astype(BF16)

    def dot3(a, b):
        mm = functools.partial(jnp.dot, preferred_element_type=F32)
        return mm(a[0], b[0]) + (mm(a[1], b[0]) + mm(a[0], b[1]))

    def local(src_ref, dst_ref):
        hz = (hz_ref[0], hz_ref[1])
        hy = (hy_ref[0], hy_ref[1])
        for pair in range(rows // 2):
            block = src_ref[pl.ds(2 * pair, 2)].reshape(4 * nz, ny)
            depth_done = dot3(hz, split(block))
            done = dot3(split(depth_done), hy)
            dst_ref[pl.ds(2 * pair, 2)] = done.reshape(2, 2 * nz, ny)

    def tile(ref, lead, part, comp):
        z = pl.multiple_of(part // halves * 8, 8)
        y = pl.multiple_of(lax.rem(part, halves) * 128, 128)
        return ref.at[lead, pl.ds(comp * nz + z, 8), pl.ds(y, 128)]

    def ctable(part, which):
        z = pl.multiple_of(part // halves * 8, 8)
        y = pl.multiple_of(lax.rem(part, halves) * 128, 128)
        return tuple(tab_ref[2 * which + c, pl.ds(z, 8), pl.ds(y, 128)] for c in range(2))

    def spectral(sp_ref, lead, part):
        return (tile(sp_ref, lead, part, 0)[...], tile(sp_ref, lead, part, 1)[...])

    def sweep_out(t, extra=None):
        sp_ref, send0, send1 = sp_all.at[t % 2], send0_all.at[t % 2], send1_all.at[t % 2]

        def summarise(part):
            root = ctable(part, 0)
            rowv = [spectral(sp_ref, i, part) for i in range(rows)]
            if extra is not None:
                rowv = [extra(i, part, value) for i, value in enumerate(rowv)]
                for i in range(rows):
                    tile(sp_ref, i, part, 0)[...] = rowv[i][0]
                    tile(sp_ref, i, part, 1)[...] = rowv[i][1]
            ahead = rowv[0]
            for i in range(1, rows):
                ahead = cmadd(ahead, root, rowv[i])
            behind = rowv[rows - 1]
            for i in range(rows - 2, -1, -1):
                behind = cmadd(behind, root, rowv[i])
            return ahead + behind

        def other_half(k, carry):
            g = lax.rem(chip + k, chips)
            vals = summarise(2 * g + 1 - core)
            for c in range(4):
                send0[g, c] = vals[c]
            remote(send0.at[g], sums.at[t, core, g], ex_send.at[t, 0], ex_recv.at[t, 0], partner).start()
            return carry

        def own_half(k, carry):
            g = lax.rem(chip + k, chips)
            vals = summarise(2 * g + core)
            for c in range(4):
                sums[t, core, g, c] = vals[c]
            return carry

        lax.fori_loop(1, chips + 1, other_half, 0, unroll=2)
        lax.fori_loop(1, chips + 1, own_half, 0, unroll=2)
        take(sums.at[t, 1 - core], ex_recv.at[t, 0])

        def combine(g):
            block_root = power(ctable(2 * g + core, 0), int(math.log2(rows)))
            first = [sums[t, 0, g, c] for c in range(4)]
            second = [sums[t, 1, g, c] for c in range(4)]
            return cmadd(first[:2], block_root, second[:2]) + cmadd(second[2:], block_root, first[2:])

        def step(k, carry):
            g = lax.rem(chip + k, chips)
            vals = combine(g)
            for c in range(4):
                send1[g, c] = vals[c]
            remote(send1.at[g], recv1.at[t, k], ex_send.at[t, 1], ex_recv.at[t, 1],
                   (src, base + 2 * g + core)).start()
            return carry

        lax.fori_loop(1, chips, step, 0)
        vals = combine(chip)
        for c in range(4):
            recv1[t, 0, c] = vals[c]

    def power(value, doublings):
        for _ in range(doublings):
            value = cmul(value, value)
        return value

    def own_root():
        return ctable(m, 0)

    def chip_root():
        return power(own_root(), int(math.log2(2 * rows)))

    def middle_out(t):
        take(recv1.at[t, pl.ds(1, chips - 1)], ex_recv.at[t, 1])
        root = chip_root()

        def gather(j, carry):
            ahead, behind = carry
            slot_a = lax.rem(chip - j + chips, chips)
            slot_b = lax.rem(chip + 1 + j, chips)
            ahead = cmadd(ahead, root, (recv1[t, slot_a, 0], recv1[t, slot_a, 1]))
            behind = cmadd(behind, root, (recv1[t, slot_b, 2], recv1[t, slot_b, 3]))
            return ahead, behind

        zero = jnp.zeros((8, 128), F32)
        ahead, behind = lax.fori_loop(0, chips, gather, ((zero, zero), (zero, zero)), unroll=True)
        for c, value in enumerate(ahead + behind):
            recv2[t, 0, c] = value

        def send(k, carry):
            peer = lax.rem(grp + k, g2) * g1 + m
            remote(recv2.at[t, 0], recv2.at[t, k], ex_send.at[t, 2], ex_recv.at[t, 2], (src, peer)).start()
            return carry

        lax.fori_loop(1, g2, send, 0)

    def middle_back(t):
        send3 = send3_all.at[t % 2]
        root = chip_root()
        group_root = power(root, int(math.log2(chips)))
        turn = power(group_root, int(math.log2(g2)))
        real, imag = 1.0 - turn[0], turn[1]
        norm = 1.0 / (real * real + imag * imag)
        inverse = (real * norm, imag * norm)
        take(recv2.at[t, pl.ds(1, g2 - 1)], ex_recv.at[t, 2])
        left = (recv2[t, 0, 0], recv2[t, 0, 1])
        right = (recv2[t, 0, 2], recv2[t, 0, 3])
        for k in range(g2 - 1, 0, -1):
            left = cmadd(left, group_root, (recv2[t, k, 0], recv2[t, k, 1]))
            right = cmadd(right, group_root, (recv2[t, g2 - k, 2], recv2[t, g2 - k, 3]))
        left = cmul(left, inverse)
        right = cmul(right, inverse)

        def spread(j, carry):
            left, right = carry
            back = chips - 1 - j
            for c in range(2):
                send3[j, c] = left[c]
                send3[back, 2 + c] = right[c]
            slot_a = lax.rem(chip - j + chips, chips)
            slot_b = lax.rem(chip + 1 + j, chips)
            left = cmadd(left, root, (recv1[t, slot_a, 0], recv1[t, slot_a, 1]))
            right = cmadd(right, root, (recv1[t, slot_b, 2], recv1[t, slot_b, 3]))
            return left, right

        lax.fori_loop(0, chips, spread, (left, right), unroll=True)

        def send(k, carry):
            g = lax.rem(chip + k, chips)
            remote(send3.at[g], recv3.at[t, k], ex_send.at[t, 3], ex_recv.at[t, 3],
                   (src, base + 2 * g + core)).start()
            return carry

        lax.fori_loop(1, chips, send, 0)
        for c in range(4):
            recv3[t, 0, c] = send3[chip, c]

    def sweep_back(t):
        sp_ref, states = sp_all.at[t % 2], states_all.at[t % 2]
        take(recv3.at[t, pl.ds(1, chips - 1)], ex_recv.at[t, 3])

        def pass_on(k, carry):
            g = lax.rem(chip - k + chips, chips)
            block_root = power(ctable(2 * g + core, 0), int(math.log2(rows)))
            left = (recv3[t, k, 0], recv3[t, k, 1])
            right = (recv3[t, k, 2], recv3[t, k, 3])
            inner_left = cmadd(left, block_root, (sums[t, 0, g, 0], sums[t, 0, g, 1]))
            inner_right = cmadd(right, block_root, (sums[t, 1, g, 2], sums[t, 1, g, 3]))
            for c in range(2):
                states[0, g, c] = left[c]
                states[0, g, 2 + c] = inner_right[c]
                states[1, g, c] = inner_left[c]
                states[1, g, 2 + c] = right[c]
            remote(states.at[1 - core, g], recv4.at[t, g], ex_send.at[t, 4], ex_recv.at[t, 4], partner).start()
            return carry

        lax.fori_loop(0, chips, pass_on, 0, unroll=2)

        def apply(part, ends):
            root = ctable(part, 0)
            kappa = ctable(part, 1)
            rowv = [spectral(sp_ref, i, part) for i in range(rows)]
            state = ends[:2]
            ahead = []
            for i in range(rows):
                state = cmadd(state, root, rowv[i])
                ahead.append(state)
            state = cmul(ends[2:], root)
            for i in range(rows - 1, -1, -1):
                total = cmul((ahead[i][0] + state[0], ahead[i][1] + state[1]), kappa)
                tile(sp_ref, i, part, 0)[...] = total[0]
                tile(sp_ref, i, part, 1)[...] = total[1]
                if i:
                    state = cmul((state[0] + rowv[i][0], state[1] + rowv[i][1]), root)

        def own_half(g, carry):
            apply(2 * g + core, tuple(states[core, g, c] for c in range(4)))
            return carry

        def other_half(g, carry):
            apply(2 * g + 1 - core, tuple(recv4[t, g, c] for c in range(4)))
            return carry

        lax.fori_loop(0, chips, own_half, 0, unroll=2)
        take(recv4.at[t], ex_recv.at[t, 4])
        lax.fori_loop(0, chips, other_half, 0, unroll=2)

    def finish(t):
        take(recv4.at[t], ex_send.at[t, 0])
        take(recv1.at[t, pl.ds(1, chips - 1)], ex_send.at[t, 1])
        take(recv2.at[t, pl.ds(1, g2 - 1)], ex_send.at[t, 2])
        take(recv3.at[t, pl.ds(1, chips - 1)], ex_send.at[t, 3])
        take(recv4.at[t], ex_send.at[t, 4])

    def pair(ref, x, z):
        return (ref[x, pl.ds(z, 8), :], ref[x, pl.ds(nz + z, 8), :])

    def put(ref, x, z, value):
        ref[x, pl.ds(z, 8), :] = value[0]
        ref[x, pl.ds(nz + z, 8), :] = value[1]

    def each_block(body, init):
        def outer(n, carry):
            return body(n // zgroups, pl.multiple_of(lax.rem(n, zgroups) * 8, 8), carry)

        return lax.fori_loop(0, rows * zgroups, outer, init, unroll=4)

    def square(value):
        return value[0] * value[0] + value[1] * value[1]

    zero = jnp.zeros((8, ny), F32)
    source_x = pos_ref[0, 0].astype(F32)
    source_y = pos_ref[0, 1].astype(F32)
    offset_y = lax.broadcasted_iota(jnp.int32, (8, ny), 1).astype(F32) - source_y
    offset_y_sq = offset_y * offset_y
    level = lax.broadcasted_iota(jnp.int32, (8, ny), 0).astype(F32) + SOURCE_GAP

    def begin(x, z, total):
        height = level + z.astype(F32)
        offset_x = (space * rows + x).astype(F32) - source_x
        dist = jnp.sqrt(height * height + offset_x * offset_x + offset_y_sq)
        turns = dist * (1.0 / 6.0)
        sine, cosine = half_turn(turns - jnp.floor(turns + 0.5))
        wave = (1.0 - 2.0 * sine * sine, 2.0 * sine * cosine)
        put(e_ref, x, z, wave)
        field = cmul(pair(chi0_ref, x, z), wave)
        put(w_ref, x, z, field)
        return total + square(field)

    object_part = each_block(begin, zero)
    data_part = jnp.zeros((1, ny), F32)
    for x in range(rows):
        for c in range(2):
            data_part = data_part + meas_ref[x, pl.ds(c, 1), :] * meas_ref[x, pl.ds(c, 1), :]
    data_fold = data_part[:, :128]
    for h in range(1, halves):
        data_fold = data_fold + data_part[:, h * 128:(h + 1) * 128]

    local(w_ref, sp_all.at[0])
    pl.semaphore_wait(barrier, (g1 - 1) + (ns * g2 - 1))
    sweep_out(0)
    reduce_start(0, [data_fold, fold(object_part)])
    middle_out(0)
    reduce_middle(0)
    middle_back(0)
    totals = reduce_end(0)
    sweep_back(0)
    finish(0)
    local(sp_all.at[0], s_ref)
    data_total = totals[0:1]
    object_share = totals[1:2] / data_total
    ratio = 0.5 / DAMPING
    level_zero = 1.0 / math.sqrt(nz)
    chi_ref = chi0_ref
    for update in range(OUTER):
        t = 1 + 2 * update
        a = 1 + 2 * update
        last = update == OUTER - 1
        chi_next = chi_out_ref if last else chi1_ref
        early, late = early_recv.at[update], late_recv.at[update]
        right, left, across = (lax.rem(src + k, ns) for k in (1, 3, 2))

        for k in (0, 3, 1, 2):
            x = lax.rem(src + k, ns)
            if update and k:
                take(chi_ref.at[0], chi_took.at[update - 1, ns - k])

            def residual(n, carry, x=x, chi_ref=chi_ref):
                z = pl.multiple_of(n * 8, 8)
                chi = pair(chi_ref, x, z)
                e, s, w = pair(e_ref, x, z), pair(s_ref, x, z), pair(w_ref, x, z)
                u = (e[0] + s[0], e[1] + s[1])
                field = cmul(chi, u)
                res = (field[0] - w[0], field[1] - w[1])
                put(r_ref, x, z, res)
                flipped = cmul(chi, (res[0], -res[1]))
                put(v_ref, x, z, (-flipped[0], -flipped[1]))
                put(b_ref, x, z, (res[0] + ratio * flipped[1], res[1] + ratio * flipped[0]))
                early_ref[x, pl.ds(z, 8), :] = w[0] * u[0] + w[1] * u[1]
                early_ref[x, pl.ds(nz + z, 8), :] = w[1] * u[0] - w[0] * u[1]
                early_ref[x, pl.ds(2 * nz + z, 8), :] = square(u)
                return carry

            lax.fori_loop(0, zgroups, residual, 0, unroll=4)
            if k:
                remote(early_ref.at[x], early.at[k], x_send.at[update, 0], x_recv.at[update, 0], (x, space)).start()
        rho = jnp.concatenate(
            [
                meas_ref[x, pl.ds(c, 1), :] - s_ref[x, pl.ds(c * nz, 1), :]
                for x in range(rows) for c in range(2)
            ],
            axis=0,
        )
        rho_ref[...] = level_zero * dot3(split(rho), (hy_ref[0], hy_ref[1]))

        first, second = sp_all.at[t % 2], sp_all.at[(t + 1) % 2]
        local(v_ref, first)
        local(b_ref, second)
        if update:
            object_share = float(ns) * reduce_end(2)[0:1] / data_total

        def rho_tile(i, part, c, object_share=object_share):
            y = pl.multiple_of(lax.rem(part, halves) * 128, 128)
            return object_share * rho_ref[pl.ds(2 * i + c, 1), pl.ds(y, 128)]

        def add_first(i, part, value, rho_tile=rho_tile):
            return value[0] + rho_tile(i, part, 0), value[1] - rho_tile(i, part, 1)

        def add_second(i, part, value, rho_tile=rho_tile):
            return value[0] + ratio * rho_tile(i, part, 1), value[1] - ratio * rho_tile(i, part, 0)

        sweep_out(t, add_first)
        sweep_out(t + 1, add_second)
        middle_out(t)
        middle_out(t + 1)
        middle_back(t)
        middle_back(t + 1)
        sweep_back(t)
        local(first, d_ref)
        sweep_back(t + 1)
        local(second, v_ref)
        finish(t)
        finish(t + 1)

        def pass_late(row, half, place, device, update=update, late=late):
            remote(late_ref.at[row, half], late.at[place, half], late_send.at[update, place, half],
                   late_took.at[update, place, half], (device, space)).start()

        def add_late(row, half, update=update, late=late):
            take(late.at[0, half], late_took.at[update, 0, half])

            def add(n, carry):
                at = pl.ds(pl.multiple_of(n * 8, 8), 8)
                late_ref[row, half, at, :] = late_ref[row, half, at, :] + late[0, half, at, :]
                return carry

            lax.fori_loop(0, 3 * zgroups, add, 0, unroll=8)

        totals = (zero, zero)
        for k in (2, 1, 3, 0):
            x = lax.rem(src + k, ns)

            def descend(n, totals, x=x, chi_ref=chi_ref):
                z = pl.multiple_of(n * 8, 8)
                res, image, other = pair(r_ref, x, z), pair(d_ref, x, z), pair(v_ref, x, z)
                d = (res[0] + image[0], res[1] - image[1])
                h = (other[0] + ratio * image[1], other[1] + ratio * image[0])
                put(d_ref, x, z, d)
                put(v_ref, x, z, h)
                moved = cmul(pair(chi_ref, x, z), h)
                e, s, w = pair(e_ref, x, z), pair(s_ref, x, z), pair(w_ref, x, z)
                u = (e[0] + s[0], e[1] + s[1])
                late_parts = (
                    d[0] * u[0] + d[1] * u[1] + (w[0] * h[0] + w[1] * h[1]),
                    d[1] * u[0] - d[0] * u[1] + (w[1] * h[0] - w[0] * h[1]),
                    2.0 * (u[0] * h[0] + u[1] * h[1]),
                    d[0] * h[0] + d[1] * h[1],
                    d[1] * h[0] - d[0] * h[1],
                    square(h),
                )
                half = n // (zgroups // 2)
                for c, value in enumerate(late_parts):
                    late_ref[x, half, pl.ds(c * (nz // 2) + z - half * (nz // 2), 8), :] = value
                return totals[0] + square(d), totals[1] + square((d[0] - moved[0], d[1] - moved[1]))

            totals = lax.fori_loop(0, zgroups, descend, totals, unroll=4)
            if k == 2:
                pass_late(across, 0, 0, right)
                pass_late(across, 1, 0, left)
            elif k == 1:
                pass_late(right, 1, 1, right)
            elif k == 3:
                pass_late(left, 0, 2, left)
        image_part = jnp.zeros((1, ny), F32)
        for x in range(rows):
            image_part = image_part + square((v_ref[x, pl.ds(0, 1), :], v_ref[x, pl.ds(nz, 1), :]))
        image_fold = image_part[:, :128]
        for h in range(1, halves):
            image_fold = image_fold + image_part[:, h * 128:(h + 1) * 128]
        reduce_start(a, [fold(totals[0]), image_fold, fold(totals[1])])
        take(early.at[pl.ds(1, ns - 1)], x_recv.at[update, 0])

        def gather_early(n, carry, early=early):
            at = pl.ds(pl.multiple_of(n * 8, 8), 8)
            early_ref[src, at, :] = early_ref[src, at, :] + early[1, at, :] + early[2, at, :] + early[3, at, :]
            return carry

        lax.fori_loop(0, 3 * zgroups, gather_early, 0, unroll=4)
        reduce_middle(a)
        add_late(right, 0)
        pass_late(right, 0, 1, right)
        add_late(left, 1)
        pass_late(left, 1, 2, left)
        totals = reduce_end(a)
        length = totals[0:1] / (object_share * totals[1:2] + totals[2:3])

        def advance(x, z, carry, length=length, last=last):
            w, d = pair(w_ref, x, z), pair(d_ref, x, z)
            put(w_ref, x, z, (w[0] + length * d[0], w[1] + length * d[1]))
            if not last:
                s, h = pair(s_ref, x, z), pair(v_ref, x, z)
                put(s_ref, x, z, (s[0] + length * h[0], s[1] + length * h[1]))
            return carry

        each_block(advance, 0)
        for half in range(2):
            for place in (1, 2):
                take(late.at[place, half], late_took.at[update, place, half])

        def contrast(n, total, length=length, late=late, chi_next=chi_next):
            z = pl.multiple_of(n * 8, 8)
            terms = []
            half = n // (zgroups // 2)
            for c in range(6):
                at = pl.ds(c * (nz // 2) + z - half * (nz // 2), 8)
                terms.append(late_ref[src, half, at, :] + late[1, half, at, :] + late[2, half, at, :])
            parts = [
                early_ref[src, pl.ds(c * nz + z, 8), :] + length * (terms[c] + length * terms[3 + c]) for c in range(3)
            ]
            scale = 1.0 / jnp.maximum(parts[2], FLOOR_SHARE * ns)
            chi = (jnp.clip(parts[0] * scale, REAL_LOW, REAL_HIGH), jnp.clip(parts[1] * scale, 0.0, IMAG_HIGH))
            put(chi_next, src, z, chi)
            return total + square(chi)

        chi_part = lax.fori_loop(0, zgroups, contrast, zero, unroll=2)
        for k in (2, 1, 3):
            remote(chi_next.at[src], chi_next.at[src], x_send.at[update, 1], chi_took.at[update, k],
                   (lax.rem(src + k, ns), space)).start()
        if not last:
            reduce_start(2, [fold(chi_part)])
            reduce_middle(2)
        else:
            for k in range(1, ns):
                take(chi_next.at[0], chi_took.at[update, k])
        take(early.at[pl.ds(1, ns - 1)], x_send.at[update, 0])
        for half in range(2):
            for place in range(3):
                take(late.at[place, half], late_send.at[update, place, half])
        chi_ref = chi_next
    for update in range(OUTER):
        take(chi_out_ref.at[pl.ds(0, ns - 1)], x_send.at[update, 1])


def on_device(ns, g1, g2, contrast, measured, positions):
    _, nz, rows, ny = contrast.shape
    cfg = (ns, g1, g2, nz, ny, rows)
    transforms = 1 + 2 * OUTER
    reductions = 2 * OUTER
    chi0 = contrast.transpose(2, 0, 1, 3).reshape(rows, 2 * nz, ny)
    meas = measured[0].transpose(1, 0, 2)
    tables = decay_tables(nz, ny)
    hy = high_low(hartley(ny))
    hz = high_low(np.kron(np.eye(4), hartley(nz)))
    field = (rows, 2 * nz, ny)
    vmem = pl.BlockSpec(memory_space=pltpu.VMEM)
    w, chi = pl.pallas_call(
        functools.partial(kernel, cfg),
        out_shape=(jax.ShapeDtypeStruct(field, F32), jax.ShapeDtypeStruct(field, F32)),
        in_specs=[pl.BlockSpec(memory_space=pltpu.SMEM)] + [vmem] * 5,
        out_specs=(vmem, vmem),
        scratch_shapes=[pltpu.VMEM(field, F32)] * 7 + [
            pltpu.VMEM((2,) + field, F32),
            pltpu.VMEM((2 * rows, ny), F32),
            pltpu.VMEM((rows, 3 * nz, ny), F32),
            pltpu.VMEM((OUTER, ns, 3 * nz, ny), F32),
            pltpu.VMEM((rows, 2, 3 * nz, ny), F32),
            pltpu.VMEM((OUTER, 3, 2, 3 * nz, ny), F32),
            pltpu.VMEM((2, g1 // 2, 4, 8, 128), F32),
            pltpu.VMEM((2, g1 // 2, 4, 8, 128), F32),
            pltpu.VMEM((2, g1 // 2, 4, 8, 128), F32),
            pltpu.VMEM((2, 2, g1 // 2, 4, 8, 128), F32),
            pltpu.VMEM((transforms, 2, g1 // 2, 4, 8, 128), F32),
            pltpu.VMEM((transforms, g1 // 2, 4, 8, 128), F32),
            pltpu.VMEM((transforms, g2, 4, 8, 128), F32),
            pltpu.VMEM((transforms, g1 // 2, 4, 8, 128), F32),
            pltpu.VMEM((transforms, g1 // 2, 4, 8, 128), F32),
            pltpu.VMEM((reductions, g1, 8, 128), F32),
            pltpu.VMEM((reductions, ns * g2, 8, 128), F32),
            pltpu.SemaphoreType.DMA((transforms, 5)),
            pltpu.SemaphoreType.DMA((transforms, 5)),
            pltpu.SemaphoreType.DMA((reductions, 2)),
            pltpu.SemaphoreType.DMA((reductions, 2)),
            pltpu.SemaphoreType.DMA((OUTER, 2)),
            pltpu.SemaphoreType.DMA((OUTER, 2)),
            pltpu.SemaphoreType.DMA((OUTER, 3, 2)),
            pltpu.SemaphoreType.DMA((OUTER, 3, 2)),
            pltpu.SemaphoreType.DMA((OUTER, ns)),
        ],
        compiler_params=pltpu.CompilerParams(
            collective_id=0, has_side_effects=True, vmem_limit_bytes=40 * 1024 * 1024
        ),
    )(positions, chi0, meas, tables, hy, hz)
    sources = w.reshape(rows, 2, nz, ny).transpose(1, 2, 0, 3)[None]
    return sources, chi.reshape(rows, 2, nz, ny).transpose(1, 2, 0, 3)


def solution(mesh, g2=4):
    placed = (P(None, None, "space", None), P("src", None, "space", None), P("src", None))
    return jax.shard_map(
        functools.partial(on_device, mesh.shape["src"], mesh.shape["space"] // g2, g2),
        mesh=mesh,
        in_specs=placed,
        out_specs=(P("src", None, None, "space", None), P(None, None, "space", None)),
        check_vma=False,
    )
```

```python
import functools
import math

import jax
import jax.numpy as jnp
import ml_dtypes
import numpy as np
from jax import lax
from jax.experimental import pallas as pl
from jax.experimental.pallas import tpu as pltpu
from jax.sharding import PartitionSpec as P

OUTER = 2
WAVENUMBER = 2.0 * math.pi / 6.0
DAMPING = 0.3
SOURCE_GAP = 8.0
FLOOR_SHARE = 0.75
REAL_LOW = -0.25
REAL_HIGH = 0.35
IMAG_HIGH = 0.1
F32 = jnp.float32
BF16 = jnp.bfloat16
MESH = pl.DeviceIdType.MESH


def hartley(length):
    turn = np.outer(np.arange(length), np.arange(length)) % length
    angle = 2.0 * np.pi / length * turn
    return (np.cos(angle) + np.sin(angle)) / np.sqrt(length)


def high_low(table):
    high = table.astype(ml_dtypes.bfloat16)
    low = (table - high.astype(np.float64)).astype(ml_dtypes.bfloat16)
    return np.stack([high, low])


def modes(length):
    return 4.0 * np.sin(np.pi * np.arange(length) / length) ** 2


def decay_tables(depth, across):
    wave_sq = WAVENUMBER * WAVENUMBER
    trace = 2.0 + modes(depth)[:, None] + modes(across)[None, :] - wave_sq * (1.0 + 1j * DAMPING)
    root = np.sqrt(trace * trace - 4.0)
    first = (trace - root) / 2.0
    second = (trace + root) / 2.0
    small = np.where(np.abs(first) < np.abs(second), first, second)
    large = np.where(np.abs(first) < np.abs(second), second, first)
    small = 1.0 / large
    kappa = wave_sq / (large - small)
    tables = np.stack([small.real, small.imag, kappa.real, kappa.imag])
    return tables.astype(np.float32)


def cmul(a, b):
    return (a[0] * b[0] - a[1] * b[1], a[0] * b[1] + a[1] * b[0])


def cmadd(a, b, c):
    return (a[0] * b[0] - a[1] * b[1] + c[0], a[0] * b[1] + a[1] * b[0] + c[1])


def half_turn(fraction):
    angle = fraction * math.pi
    sq = angle * angle
    sine = jnp.full_like(sq, -1.0 / math.factorial(11))
    for order in (9, 7, 5, 3, 1):
        sine = sine * sq + (1.0 if order % 4 == 1 else -1.0) / math.factorial(order)
    cosine = jnp.full_like(sq, 1.0 / math.factorial(12))
    for order in (10, 8, 6, 4, 2, 0):
        cosine = cosine * sq + (1.0 if order % 4 == 0 else -1.0) / math.factorial(order)
    return sine * angle, cosine


def kernel(
    cfg,
    pos_ref, meas_ref, contrast_hbm, tab_hbm, hy_hbm, hz_hbm,
    w_hbm, chi_hbm,
    chi0_ref, tab_ref, hy_ref, hz_ref, w_ref, chi2_ref, chi1_ref, e_ref, s_ref, r_ref, d_ref, v_ref, b_ref, sp_all, rho_ref, early_ref, early_recv, late_ref, late_recv,
    send0_all, send1_all, send3_all, states_all, sums, recv1, recv2, recv3, recv4, red1, red2,
    ex_send, ex_recv, red_send, red_recv, x_send, x_recv, late_send, late_took, chi_took, local_sem,
):
    ns, g1, g2, nz, ny, rows = cfg
    halves = ny // 128
    nx = g1 * g2 * rows
    zgroups = nz // 8
    src = lax.axis_index("src")
    space = lax.axis_index("space")
    m = lax.rem(space, g1)
    chips = g1 // 2
    core = lax.rem(m, 2)
    chip = m // 2
    grp = space // g1
    base = grp * g1

    partner = (src, space + 1 - 2 * core)

    for x in range(rows):
        for c in range(2):
            pltpu.make_async_copy(
                contrast_hbm.at[c, :, x, :], chi0_ref.at[x, pl.ds(c * nz, nz), :], local_sem.at[0]
            ).start()
    pltpu.make_async_copy(hz_hbm, hz_ref, local_sem.at[1]).start()
    pltpu.make_async_copy(hy_hbm, hy_ref, local_sem.at[2]).start()
    pltpu.make_async_copy(tab_hbm, tab_ref, local_sem.at[3]).start()

    barrier = pltpu.get_barrier_semaphore()

    def greet_group(k, carry):
        pl.semaphore_signal(barrier, inc=1, device_id=(src, base + lax.rem(m + k, g1)), device_id_type=MESH)
        return carry

    def cross_peer(k):
        return lax.rem(src + k // g2, ns), lax.rem(grp + lax.rem(k, g2), g2) * g1 + m

    def greet_cross(k, carry):
        pl.semaphore_signal(barrier, inc=1, device_id=cross_peer(k), device_id_type=MESH)
        return carry

    lax.fori_loop(1, g1, greet_group, 0)
    lax.fori_loop(1, ns * g2, greet_cross, 0)

    def remote(src_ref, dst_ref, send_sem, recv_sem, device):
        return pltpu.make_async_remote_copy(
            src_ref=src_ref, dst_ref=dst_ref, send_sem=send_sem, recv_sem=recv_sem,
            device_id=device, device_id_type=MESH,
        )

    def take(ref, sem):
        pltpu.make_async_copy(ref, ref, sem).wait()

    def reduce_start(a, parts):
        red1[a, 0] = jnp.concatenate(parts + [jnp.zeros((8 - len(parts), 128), F32)], axis=0)

        def send(k, carry):
            remote(red1.at[a, 0], red1.at[a, k], red_send.at[a, 0], red_recv.at[a, 0],
                   (src, base + lax.rem(m + k, g1))).start()
            return carry

        lax.fori_loop(1, g1, send, 0)

    def reduce_middle(a):
        take(red1.at[a, pl.ds(1, g1 - 1)], red_recv.at[a, 0])

        def add(j, total):
            return total + red1[a, lax.rem(m - j + g1, g1)]

        red2[a, 0] = lax.fori_loop(0, g1, add, jnp.zeros((8, 128), F32), unroll=True)
        take(red1.at[a, pl.ds(1, g1 - 1)], red_send.at[a, 0])

        def send(k, carry):
            remote(red2.at[a, 0], red2.at[a, k], red_send.at[a, 1], red_recv.at[a, 1], cross_peer(k)).start()
            return carry

        lax.fori_loop(1, ns * g2, send, 0)

    def reduce_end(a):
        count = ns * g2
        take(red2.at[a, pl.ds(1, count - 1)], red_recv.at[a, 1])

        def add(j, total):
            slot = lax.rem(src - j // g2 + ns, ns) * g2 + lax.rem(grp - lax.rem(j, g2) + g2, g2)
            return total + red2[a, slot]

        total = lax.fori_loop(0, count, add, jnp.zeros((8, 128), F32), unroll=True)
        take(red2.at[a, pl.ds(1, count - 1)], red_send.at[a, 1])
        return jnp.sum(total, axis=1, keepdims=True)

    def fold(acc):
        part = acc[:, :128]
        for h in range(1, halves):
            part = part + acc[:, h * 128:(h + 1) * 128]
        return jnp.sum(part, axis=0, keepdims=True)

    def split(a):
        high = a.astype(BF16)
        return high, (a - high.astype(F32)).astype(BF16)

    def dot3(a, b):
        mm = functools.partial(jnp.dot, preferred_element_type=F32)
        return mm(a[0], b[0]) + (mm(a[1], b[0]) + mm(a[0], b[1]))

    def local(src_ref, dst_ref):
        hz = (hz_ref[0], hz_ref[1])
        hy = (hy_ref[0], hy_ref[1])
        for pair in range(rows // 2):
            block = src_ref[pl.ds(2 * pair, 2)].reshape(4 * nz, ny)
            depth_done = dot3(hz, split(block))
            done = dot3(split(depth_done), hy)
            dst_ref[pl.ds(2 * pair, 2)] = done.reshape(2, 2 * nz, ny)

    def tile(ref, lead, part, comp):
        z = pl.multiple_of(part // halves * 8, 8)
        y = pl.multiple_of(lax.rem(part, halves) * 128, 128)
        return ref.at[lead, pl.ds(comp * nz + z, 8), pl.ds(y, 128)]

    def ctable(part, which):
        z = pl.multiple_of(part // halves * 8, 8)
        y = pl.multiple_of(lax.rem(part, halves) * 128, 128)
        return tuple(tab_ref[2 * which + c, pl.ds(z, 8), pl.ds(y, 128)] for c in range(2))

    def spectral(sp_ref, lead, part):
        return (tile(sp_ref, lead, part, 0)[...], tile(sp_ref, lead, part, 1)[...])

    def sweep_out(t, extra=None):
        sp_ref, send0, send1 = sp_all.at[t % 2], send0_all.at[t % 2], send1_all.at[t % 2]

        def summarise(part):
            root = ctable(part, 0)
            rowv = [spectral(sp_ref, i, part) for i in range(rows)]
            if extra is not None:
                rowv = [extra(i, part, value) for i, value in enumerate(rowv)]
                for i in range(rows):
                    tile(sp_ref, i, part, 0)[...] = rowv[i][0]
                    tile(sp_ref, i, part, 1)[...] = rowv[i][1]
            ahead = rowv[0]
            for i in range(1, rows):
                ahead = cmadd(ahead, root, rowv[i])
            behind = rowv[rows - 1]
            for i in range(rows - 2, -1, -1):
                behind = cmadd(behind, root, rowv[i])
            return ahead + behind

        def other_half(k, carry):
            g = lax.rem(chip + k, chips)
            vals = summarise(2 * g + 1 - core)
            for c in range(4):
                send0[g, c] = vals[c]
            remote(send0.at[g], sums.at[t, core, g], ex_send.at[t, 0], ex_recv.at[t, 0], partner).start()
            return carry

        def own_half(k, carry):
            g = lax.rem(chip + k, chips)
            vals = summarise(2 * g + core)
            for c in range(4):
                sums[t, core, g, c] = vals[c]
            return carry

        lax.fori_loop(1, chips + 1, other_half, 0, unroll=2)
        lax.fori_loop(1, chips + 1, own_half, 0, unroll=2)
        take(sums.at[t, 1 - core], ex_recv.at[t, 0])

        def combine(g):
            block_root = power(ctable(2 * g + core, 0), int(math.log2(rows)))
            first = [sums[t, 0, g, c] for c in range(4)]
            second = [sums[t, 1, g, c] for c in range(4)]
            return cmadd(first[:2], block_root, second[:2]) + cmadd(second[2:], block_root, first[2:])

        def step(k, carry):
            g = lax.rem(chip + k, chips)
            vals = combine(g)
            for c in range(4):
                send1[g, c] = vals[c]
            remote(send1.at[g], recv1.at[t, k], ex_send.at[t, 1], ex_recv.at[t, 1],
                   (src, base + 2 * g + core)).start()
            return carry

        lax.fori_loop(1, chips, step, 0)
        vals = combine(chip)
        for c in range(4):
            recv1[t, 0, c] = vals[c]

    def power(value, doublings):
        for _ in range(doublings):
            value = cmul(value, value)
        return value

    def own_root():
        return ctable(m, 0)

    def chip_root():
        return power(own_root(), int(math.log2(2 * rows)))

    def middle_out(t):
        take(recv1.at[t, pl.ds(1, chips - 1)], ex_recv.at[t, 1])
        root = chip_root()

        def gather(j, carry):
            ahead, behind = carry
            slot_a = lax.rem(chip - j + chips, chips)
            slot_b = lax.rem(chip + 1 + j, chips)
            ahead = cmadd(ahead, root, (recv1[t, slot_a, 0], recv1[t, slot_a, 1]))
            behind = cmadd(behind, root, (recv1[t, slot_b, 2], recv1[t, slot_b, 3]))
            return ahead, behind

        zero = jnp.zeros((8, 128), F32)
        ahead, behind = lax.fori_loop(0, chips, gather, ((zero, zero), (zero, zero)), unroll=True)
        for c, value in enumerate(ahead + behind):
            recv2[t, 0, c] = value

        def send(k, carry):
            peer = lax.rem(grp + k, g2) * g1 + m
            remote(recv2.at[t, 0], recv2.at[t, k], ex_send.at[t, 2], ex_recv.at[t, 2], (src, peer)).start()
            return carry

        lax.fori_loop(1, g2, send, 0)

    def middle_back(t):
        send3 = send3_all.at[t % 2]
        root = chip_root()
        group_root = power(root, int(math.log2(chips)))
        turn = power(group_root, int(math.log2(g2)))
        real, imag = 1.0 - turn[0], turn[1]
        norm = 1.0 / (real * real + imag * imag)
        inverse = (real * norm, imag * norm)
        take(recv2.at[t, pl.ds(1, g2 - 1)], ex_recv.at[t, 2])
        left = (recv2[t, 0, 0], recv2[t, 0, 1])
        right = (recv2[t, 0, 2], recv2[t, 0, 3])
        for k in range(g2 - 1, 0, -1):
            left = cmadd(left, group_root, (recv2[t, k, 0], recv2[t, k, 1]))
            right = cmadd(right, group_root, (recv2[t, g2 - k, 2], recv2[t, g2 - k, 3]))
        left = cmul(left, inverse)
        right = cmul(right, inverse)

        def spread(j, carry):
            left, right = carry
            back = chips - 1 - j
            for c in range(2):
                send3[j, c] = left[c]
                send3[back, 2 + c] = right[c]
            slot_a = lax.rem(chip - j + chips, chips)
            slot_b = lax.rem(chip + 1 + j, chips)
            left = cmadd(left, root, (recv1[t, slot_a, 0], recv1[t, slot_a, 1]))
            right = cmadd(right, root, (recv1[t, slot_b, 2], recv1[t, slot_b, 3]))
            return left, right

        lax.fori_loop(0, chips, spread, (left, right), unroll=True)

        def send(k, carry):
            g = lax.rem(chip + k, chips)
            remote(send3.at[g], recv3.at[t, k], ex_send.at[t, 3], ex_recv.at[t, 3],
                   (src, base + 2 * g + core)).start()
            return carry

        lax.fori_loop(1, chips, send, 0)
        for c in range(4):
            recv3[t, 0, c] = send3[chip, c]

    def sweep_back(t):
        sp_ref, states = sp_all.at[t % 2], states_all.at[t % 2]
        take(recv3.at[t, pl.ds(1, chips - 1)], ex_recv.at[t, 3])

        def pass_on(k, carry):
            g = lax.rem(chip - k + chips, chips)
            block_root = power(ctable(2 * g + core, 0), int(math.log2(rows)))
            left = (recv3[t, k, 0], recv3[t, k, 1])
            right = (recv3[t, k, 2], recv3[t, k, 3])
            inner_left = cmadd(left, block_root, (sums[t, 0, g, 0], sums[t, 0, g, 1]))
            inner_right = cmadd(right, block_root, (sums[t, 1, g, 2], sums[t, 1, g, 3]))
            for c in range(2):
                states[0, g, c] = left[c]
                states[0, g, 2 + c] = inner_right[c]
                states[1, g, c] = inner_left[c]
                states[1, g, 2 + c] = right[c]
            remote(states.at[1 - core, g], recv4.at[t, g], ex_send.at[t, 4], ex_recv.at[t, 4], partner).start()
            return carry

        lax.fori_loop(0, chips, pass_on, 0, unroll=2)

        def apply(part, ends):
            root = ctable(part, 0)
            kappa = ctable(part, 1)
            rowv = [spectral(sp_ref, i, part) for i in range(rows)]
            state = ends[:2]
            ahead = []
            for i in range(rows):
                state = cmadd(state, root, rowv[i])
                ahead.append(state)
            state = cmul(ends[2:], root)
            for i in range(rows - 1, -1, -1):
                total = cmul((ahead[i][0] + state[0], ahead[i][1] + state[1]), kappa)
                tile(sp_ref, i, part, 0)[...] = total[0]
                tile(sp_ref, i, part, 1)[...] = total[1]
                if i:
                    state = cmul((state[0] + rowv[i][0], state[1] + rowv[i][1]), root)

        def own_half(g, carry):
            apply(2 * g + core, tuple(states[core, g, c] for c in range(4)))
            return carry

        def other_half(g, carry):
            apply(2 * g + 1 - core, tuple(recv4[t, g, c] for c in range(4)))
            return carry

        lax.fori_loop(0, chips, own_half, 0, unroll=2)
        take(recv4.at[t], ex_recv.at[t, 4])
        lax.fori_loop(0, chips, other_half, 0, unroll=2)

    def finish(t):
        take(recv4.at[t], ex_send.at[t, 0])
        take(recv1.at[t, pl.ds(1, chips - 1)], ex_send.at[t, 1])
        take(recv2.at[t, pl.ds(1, g2 - 1)], ex_send.at[t, 2])
        take(recv3.at[t, pl.ds(1, chips - 1)], ex_send.at[t, 3])
        take(recv4.at[t], ex_send.at[t, 4])

    def pair(ref, x, z):
        return (ref[x, pl.ds(z, 8), :], ref[x, pl.ds(nz + z, 8), :])

    def put(ref, x, z, value):
        ref[x, pl.ds(z, 8), :] = value[0]
        ref[x, pl.ds(nz + z, 8), :] = value[1]

    def each_block(body, init):
        def outer(n, carry):
            return body(n // zgroups, pl.multiple_of(lax.rem(n, zgroups) * 8, 8), carry)

        return lax.fori_loop(0, rows * zgroups, outer, init, unroll=4)

    def square(value):
        return value[0] * value[0] + value[1] * value[1]

    zero = jnp.zeros((8, ny), F32)
    source_x = pos_ref[0, 0].astype(F32)
    source_y = pos_ref[0, 1].astype(F32)
    offset_y = lax.broadcasted_iota(jnp.int32, (8, ny), 1).astype(F32) - source_y
    offset_y_sq = offset_y * offset_y
    level = lax.broadcasted_iota(jnp.int32, (8, ny), 0).astype(F32) + SOURCE_GAP

    def begin(x, z, carry):
        height = level + z.astype(F32)
        offset_x = (space * rows + x).astype(F32) - source_x
        dist = jnp.sqrt(height * height + offset_x * offset_x + offset_y_sq)
        turns = dist * (1.0 / 6.0)
        sine, cosine = half_turn(turns - jnp.floor(turns + 0.5))
        wave = (1.0 - 2.0 * sine * sine, 2.0 * sine * cosine)
        put(e_ref, x, z, wave)
        return carry

    def excite(x, z, total):
        field = cmul(pair(chi0_ref, x, z), pair(e_ref, x, z))
        put(w_ref, x, z, field)
        return total + square(field)

    each_block(begin, 0)
    take(chi0_ref, local_sem.at[0])
    object_part = each_block(excite, zero)
    data_part = jnp.zeros((1, ny), F32)
    for x in range(rows):
        for c in range(2):
            data_part = data_part + meas_ref[c, pl.ds(x, 1), :] * meas_ref[c, pl.ds(x, 1), :]
    data_fold = data_part[:, :128]
    for h in range(1, halves):
        data_fold = data_fold + data_part[:, h * 128:(h + 1) * 128]

    take(hz_ref, local_sem.at[1])
    take(hy_ref, local_sem.at[2])
    local(w_ref, sp_all.at[0])
    take(tab_ref, local_sem.at[3])
    pl.semaphore_wait(barrier, (g1 - 1) + (ns * g2 - 1))
    sweep_out(0)
    reduce_start(0, [data_fold, fold(object_part)])
    middle_out(0)
    reduce_middle(0)
    middle_back(0)
    totals = reduce_end(0)
    sweep_back(0)
    finish(0)
    local(sp_all.at[0], s_ref)
    data_total = totals[0:1]
    object_share = totals[1:2] / data_total
    ratio = 0.5 / DAMPING
    level_zero = 1.0 / math.sqrt(nz)
    chi_ref = chi0_ref
    for update in range(OUTER):
        t = 1 + 2 * update
        a = 1 + 2 * update
        last = update == OUTER - 1
        chi_next = chi2_ref if last else chi1_ref
        early, late = early_recv.at[update], late_recv.at[update]
        right, left, across = (lax.rem(src + k, ns) for k in (1, 3, 2))

        for k in (0, 3, 1, 2):
            x = lax.rem(src + k, ns)
            if update and k:
                take(chi_ref.at[0], chi_took.at[update - 1, ns - k])

            def residual(n, carry, x=x, chi_ref=chi_ref):
                z = pl.multiple_of(n * 8, 8)
                chi = pair(chi_ref, x, z)
                e, s, w = pair(e_ref, x, z), pair(s_ref, x, z), pair(w_ref, x, z)
                u = (e[0] + s[0], e[1] + s[1])
                field = cmul(chi, u)
                res = (field[0] - w[0], field[1] - w[1])
                put(r_ref, x, z, res)
                flipped = cmul(chi, (res[0], -res[1]))
                put(v_ref, x, z, (-flipped[0], -flipped[1]))
                put(b_ref, x, z, (res[0] + ratio * flipped[1], res[1] + ratio * flipped[0]))
                early_ref[x, pl.ds(z, 8), :] = w[0] * u[0] + w[1] * u[1]
                early_ref[x, pl.ds(nz + z, 8), :] = w[1] * u[0] - w[0] * u[1]
                early_ref[x, pl.ds(2 * nz + z, 8), :] = square(u)
                return carry

            lax.fori_loop(0, zgroups, residual, 0, unroll=4)
            if k:
                remote(early_ref.at[x], early.at[k], x_send.at[update, 0], x_recv.at[update, 0], (x, space)).start()
        rho = jnp.concatenate(
            [
                meas_ref[c, pl.ds(x, 1), :] - s_ref[x, pl.ds(c * nz, 1), :]
                for x in range(rows) for c in range(2)
            ],
            axis=0,
        )
        rho_ref[...] = level_zero * dot3(split(rho), (hy_ref[0], hy_ref[1]))

        first, second = sp_all.at[t % 2], sp_all.at[(t + 1) % 2]
        local(v_ref, first)
        if update:
            local(b_ref, second)
            object_share = float(ns) * reduce_end(2)[0:1] / data_total

        def rho_tile(i, part, c, object_share=object_share):
            y = pl.multiple_of(lax.rem(part, halves) * 128, 128)
            return object_share * rho_ref[pl.ds(2 * i + c, 1), pl.ds(y, 128)]

        def add_first(i, part, value, rho_tile=rho_tile):
            return value[0] + rho_tile(i, part, 0), value[1] - rho_tile(i, part, 1)

        def add_second(i, part, value, rho_tile=rho_tile):
            return value[0] + ratio * rho_tile(i, part, 1), value[1] - ratio * rho_tile(i, part, 0)

        sweep_out(t, add_first)
        if not update:
            local(b_ref, second)
        sweep_out(t + 1, add_second)
        middle_out(t)
        middle_out(t + 1)
        middle_back(t)
        middle_back(t + 1)
        sweep_back(t)
        local(first, d_ref)
        sweep_back(t + 1)
        local(second, v_ref)
        finish(t)
        finish(t + 1)

        def pass_late(row, half, place, device, update=update, late=late):
            remote(late_ref.at[row, half], late.at[place, half], late_send.at[update, place, half],
                   late_took.at[update, place, half], (device, space)).start()

        def add_late(row, half, update=update, late=late):
            take(late.at[0, half], late_took.at[update, 0, half])

            def add(n, carry):
                at = pl.ds(pl.multiple_of(n * 8, 8), 8)
                late_ref[row, half, at, :] = late_ref[row, half, at, :] + late[0, half, at, :]
                return carry

            lax.fori_loop(0, 3 * zgroups, add, 0, unroll=8)

        totals = (zero, zero)
        for k in (2, 1, 3, 0):
            x = lax.rem(src + k, ns)

            def descend(n, totals, x=x, chi_ref=chi_ref):
                z = pl.multiple_of(n * 8, 8)
                res, image, other = pair(r_ref, x, z), pair(d_ref, x, z), pair(v_ref, x, z)
                d = (res[0] + image[0], res[1] - image[1])
                h = (other[0] + ratio * image[1], other[1] + ratio * image[0])
                put(d_ref, x, z, d)
                put(v_ref, x, z, h)
                moved = cmul(pair(chi_ref, x, z), h)
                e, s, w = pair(e_ref, x, z), pair(s_ref, x, z), pair(w_ref, x, z)
                u = (e[0] + s[0], e[1] + s[1])
                late_parts = (
                    d[0] * u[0] + d[1] * u[1] + (w[0] * h[0] + w[1] * h[1]),
                    d[1] * u[0] - d[0] * u[1] + (w[1] * h[0] - w[0] * h[1]),
                    2.0 * (u[0] * h[0] + u[1] * h[1]),
                    d[0] * h[0] + d[1] * h[1],
                    d[1] * h[0] - d[0] * h[1],
                    square(h),
                )
                half = n // (zgroups // 2)
                for c, value in enumerate(late_parts):
                    late_ref[x, half, pl.ds(c * (nz // 2) + z - half * (nz // 2), 8), :] = value
                return totals[0] + square(d), totals[1] + square((d[0] - moved[0], d[1] - moved[1]))

            totals = lax.fori_loop(0, zgroups, descend, totals, unroll=4)
            if k == 2:
                pass_late(across, 0, 0, right)
                pass_late(across, 1, 0, left)
            elif k == 1:
                pass_late(right, 1, 1, right)
            elif k == 3:
                pass_late(left, 0, 2, left)
        image_part = jnp.zeros((1, ny), F32)
        for x in range(rows):
            image_part = image_part + square((v_ref[x, pl.ds(0, 1), :], v_ref[x, pl.ds(nz, 1), :]))
        image_fold = image_part[:, :128]
        for h in range(1, halves):
            image_fold = image_fold + image_part[:, h * 128:(h + 1) * 128]
        reduce_start(a, [fold(totals[0]), image_fold, fold(totals[1])])
        take(early.at[pl.ds(1, ns - 1)], x_recv.at[update, 0])

        def gather_early(n, carry, early=early):
            at = pl.ds(pl.multiple_of(n * 8, 8), 8)
            early_ref[src, at, :] = early_ref[src, at, :] + early[1, at, :] + early[2, at, :] + early[3, at, :]
            return carry

        lax.fori_loop(0, 3 * zgroups, gather_early, 0, unroll=4)
        reduce_middle(a)
        add_late(right, 0)
        pass_late(right, 0, 1, right)
        add_late(left, 1)
        pass_late(left, 1, 2, left)
        totals = reduce_end(a)
        length = totals[0:1] / (object_share * totals[1:2] + totals[2:3])

        def advance(x, z, carry, length=length, last=last):
            w, d = pair(w_ref, x, z), pair(d_ref, x, z)
            put(w_ref, x, z, (w[0] + length * d[0], w[1] + length * d[1]))
            if not last:
                s, h = pair(s_ref, x, z), pair(v_ref, x, z)
                put(s_ref, x, z, (s[0] + length * h[0], s[1] + length * h[1]))
            return carry

        each_block(advance, 0)
        if last:
            for x in range(rows):
                for c in range(2):
                    pltpu.make_async_copy(
                        w_ref.at[x, pl.ds(c * nz, nz), :], w_hbm.at[c, :, x, :], local_sem.at[4]
                    ).start()
        for half in range(2):
            for place in (1, 2):
                take(late.at[place, half], late_took.at[update, place, half])

        def contrast(n, total, length=length, late=late, chi_next=chi_next):
            z = pl.multiple_of(n * 8, 8)
            terms = []
            half = n // (zgroups // 2)
            for c in range(6):
                at = pl.ds(c * (nz // 2) + z - half * (nz // 2), 8)
                terms.append(late_ref[src, half, at, :] + late[1, half, at, :] + late[2, half, at, :])
            parts = [
                early_ref[src, pl.ds(c * nz + z, 8), :] + length * (terms[c] + length * terms[3 + c]) for c in range(3)
            ]
            scale = 1.0 / jnp.maximum(parts[2], FLOOR_SHARE * ns)
            chi = (jnp.clip(parts[0] * scale, REAL_LOW, REAL_HIGH), jnp.clip(parts[1] * scale, 0.0, IMAG_HIGH))
            put(chi_next, src, z, chi)
            return total + square(chi)

        chi_part = lax.fori_loop(0, zgroups, contrast, zero, unroll=2)
        if not last:
            reduce_start(2, [fold(chi_part)])
        for k in (2, 1, 3):
            remote(chi_next.at[src], chi_next.at[src], x_send.at[update, 1], chi_took.at[update, k],
                   (lax.rem(src + k, ns), space)).start()
        if not last:
            reduce_middle(2)
        else:
            for k in (0, 1, 3, 2):
                x = lax.rem(src + k, ns)
                if k:
                    take(chi_next.at[0], chi_took.at[update, ns - k])
                for c in range(2):
                    pltpu.make_async_copy(
                        chi_next.at[x, pl.ds(c * nz, nz), :], chi_hbm.at[c, :, x, :], local_sem.at[5]
                    ).start()
        take(early.at[pl.ds(1, ns - 1)], x_send.at[update, 0])
        for half in range(2):
            for place in range(3):
                take(late.at[place, half], late_send.at[update, place, half])
        chi_ref = chi_next
    for update in range(OUTER):
        take(chi2_ref.at[pl.ds(0, ns - 1)], x_send.at[update, 1])
    take(w_ref, local_sem.at[4])
    take(chi2_ref, local_sem.at[5])


def on_device(ns, g1, g2, contrast, measured, positions):
    _, nz, rows, ny = contrast.shape
    cfg = (ns, g1, g2, nz, ny, rows)
    transforms = 1 + 2 * OUTER
    reductions = 2 * OUTER
    tables = decay_tables(nz, ny)
    hy = high_low(hartley(ny))
    hz = high_low(np.kron(np.eye(4), hartley(nz)))
    field = (rows, 2 * nz, ny)
    vmem = pl.BlockSpec(memory_space=pltpu.VMEM)
    anywhere = pl.BlockSpec(memory_space=pltpu.HBM)
    w, chi = pl.pallas_call(
        functools.partial(kernel, cfg),
        out_shape=(jax.ShapeDtypeStruct(contrast.shape, F32), jax.ShapeDtypeStruct(contrast.shape, F32)),
        in_specs=[pl.BlockSpec(memory_space=pltpu.SMEM), vmem] + [anywhere] * 4,
        out_specs=(anywhere, anywhere),
        scratch_shapes=[
            pltpu.VMEM(field, F32),
            pltpu.VMEM(tables.shape, F32),
            pltpu.VMEM(hy.shape, BF16),
            pltpu.VMEM(hz.shape, BF16),
        ] + [pltpu.VMEM(field, F32)] * 9 + [
            pltpu.VMEM((2,) + field, F32),
            pltpu.VMEM((2 * rows, ny), F32),
            pltpu.VMEM((rows, 3 * nz, ny), F32),
            pltpu.VMEM((OUTER, ns, 3 * nz, ny), F32),
            pltpu.VMEM((rows, 2, 3 * nz, ny), F32),
            pltpu.VMEM((OUTER, 3, 2, 3 * nz, ny), F32),
            pltpu.VMEM((2, g1 // 2, 4, 8, 128), F32),
            pltpu.VMEM((2, g1 // 2, 4, 8, 128), F32),
            pltpu.VMEM((2, g1 // 2, 4, 8, 128), F32),
            pltpu.VMEM((2, 2, g1 // 2, 4, 8, 128), F32),
            pltpu.VMEM((transforms, 2, g1 // 2, 4, 8, 128), F32),
            pltpu.VMEM((transforms, g1 // 2, 4, 8, 128), F32),
            pltpu.VMEM((transforms, g2, 4, 8, 128), F32),
            pltpu.VMEM((transforms, g1 // 2, 4, 8, 128), F32),
            pltpu.VMEM((transforms, g1 // 2, 4, 8, 128), F32),
            pltpu.VMEM((reductions, g1, 8, 128), F32),
            pltpu.VMEM((reductions, ns * g2, 8, 128), F32),
            pltpu.SemaphoreType.DMA((transforms, 5)),
            pltpu.SemaphoreType.DMA((transforms, 5)),
            pltpu.SemaphoreType.DMA((reductions, 2)),
            pltpu.SemaphoreType.DMA((reductions, 2)),
            pltpu.SemaphoreType.DMA((OUTER, 2)),
            pltpu.SemaphoreType.DMA((OUTER, 2)),
            pltpu.SemaphoreType.DMA((OUTER, 3, 2)),
            pltpu.SemaphoreType.DMA((OUTER, 3, 2)),
            pltpu.SemaphoreType.DMA((OUTER, ns)),
            pltpu.SemaphoreType.DMA((6,)),
        ],
        compiler_params=pltpu.CompilerParams(
            collective_id=0, has_side_effects=True, vmem_limit_bytes=56 * 1024 * 1024
        ),
    )(positions, measured[0], contrast, tables, hy, hz)
    return w[None], chi


def solution(mesh, g2=4):
    placed = (P(None, None, "space", None), P("src", None, "space", None), P("src", None))
    return jax.shard_map(
        functools.partial(on_device, mesh.shape["src"], mesh.shape["space"] // g2, g2),
        mesh=mesh,
        in_specs=placed,
        out_specs=(P("src", None, None, "space", None), P(None, None, "space", None)),
        check_vma=False,
    )
```

```python
import functools
import math

import jax
import jax.numpy as jnp
import ml_dtypes
import numpy as np
from jax import lax
from jax.experimental import pallas as pl
from jax.experimental.pallas import tpu as pltpu
from jax.sharding import PartitionSpec as P

OUTER = 2
WAVENUMBER = 2.0 * math.pi / 6.0
DAMPING = 0.3
SOURCE_GAP = 8.0
FLOOR_SHARE = 0.75
REAL_LOW = -0.25
REAL_HIGH = 0.35
IMAG_HIGH = 0.1
F32 = jnp.float32
BF16 = jnp.bfloat16
MESH = pl.DeviceIdType.MESH


def hartley(length):
    turn = np.outer(np.arange(length), np.arange(length)) % length
    angle = 2.0 * np.pi / length * turn
    return (np.cos(angle) + np.sin(angle)) / np.sqrt(length)


def high_low(table):
    high = table.astype(ml_dtypes.bfloat16)
    low = (table - high.astype(np.float64)).astype(ml_dtypes.bfloat16)
    return np.stack([high, low])


def modes(length):
    return 4.0 * np.sin(np.pi * np.arange(length) / length) ** 2


def decay_tables(depth, across):
    wave_sq = WAVENUMBER * WAVENUMBER
    trace = 2.0 + modes(depth)[:, None] + modes(across)[None, :] - wave_sq * (1.0 + 1j * DAMPING)
    root = np.sqrt(trace * trace - 4.0)
    first = (trace - root) / 2.0
    second = (trace + root) / 2.0
    small = np.where(np.abs(first) < np.abs(second), first, second)
    large = np.where(np.abs(first) < np.abs(second), second, first)
    small = 1.0 / large
    kappa = wave_sq / (large - small)
    tables = np.stack([small.real, small.imag, kappa.real, kappa.imag])
    return tables.astype(np.float32)


def cmul(a, b):
    return (a[0] * b[0] - a[1] * b[1], a[0] * b[1] + a[1] * b[0])


def cmadd(a, b, c):
    return (a[0] * b[0] - a[1] * b[1] + c[0], a[0] * b[1] + a[1] * b[0] + c[1])


def half_turn(fraction):
    angle = fraction * math.pi
    sq = angle * angle
    sine = jnp.full_like(sq, -1.0 / math.factorial(11))
    for order in (9, 7, 5, 3, 1):
        sine = sine * sq + (1.0 if order % 4 == 1 else -1.0) / math.factorial(order)
    cosine = jnp.full_like(sq, 1.0 / math.factorial(12))
    for order in (10, 8, 6, 4, 2, 0):
        cosine = cosine * sq + (1.0 if order % 4 == 0 else -1.0) / math.factorial(order)
    return sine * angle, cosine


def kernel(
    cfg,
    pos_ref, meas_ref, contrast_hbm, tab_hbm, hy_hbm, hz_hbm,
    w_hbm, chi_hbm,
    chi0_ref, tab_ref, hy_ref, hz_ref, w_ref, chi2_ref, chi1_ref, e_ref, s_ref, r_ref, d_ref, v_ref, b_ref, sp_all, rho_ref, early_ref, early_recv, late_ref, late_recv,
    send0_all, send1_all, send3_all, states_all, sums, recv1, recv2, recv3, recv4, red1, red2,
    ex_send, ex_recv, red_send, red_recv, x_send, x_recv, late_send, late_took, chi_took, local_sem,
):
    ns, g1, g2, nz, ny, rows = cfg
    halves = ny // 128
    nx = g1 * g2 * rows
    zgroups = nz // 8
    src = lax.axis_index("src")
    space = lax.axis_index("space")
    m = lax.rem(space, g1)
    chips = g1 // 2
    core = lax.rem(m, 2)
    chip = m // 2
    grp = space // g1
    base = grp * g1

    partner = (src, space + 1 - 2 * core)

    for x in range(rows):
        for c in range(2):
            pltpu.make_async_copy(
                contrast_hbm.at[c, :, x, :], chi0_ref.at[x, pl.ds(c * nz, nz), :], local_sem.at[0]
            ).start()
    pltpu.make_async_copy(hz_hbm, hz_ref, local_sem.at[1]).start()
    pltpu.make_async_copy(hy_hbm, hy_ref, local_sem.at[2]).start()
    pltpu.make_async_copy(tab_hbm, tab_ref, local_sem.at[3]).start()

    barrier = pltpu.get_barrier_semaphore()

    zs = g1 * g2 // 8
    z_at, y_at = space // 8, lax.rem(space // 2, 4)

    def column_peer(k):
        return src, (lax.rem(z_at + k // 2, zs) * 4 + y_at) * 2 + lax.rem(core + k, 2)

    def plane_peer(k):
        return lax.rem(src + k // 4, ns), (z_at * 4 + lax.rem(y_at + k, 4)) * 2 + core

    def greet_column(k, carry):
        pl.semaphore_signal(barrier, inc=1, device_id=column_peer(k), device_id_type=MESH)
        return carry

    def greet_plane(k, carry):
        pl.semaphore_signal(barrier, inc=1, device_id=plane_peer(k), device_id_type=MESH)
        return carry

    def greet_diagonal(k, carry):
        z_other = z_at + 1 - 2 * lax.rem(z_at, 2)
        pl.semaphore_signal(barrier, inc=1, device_id=(src, (z_other * 4 + lax.rem(y_at + k, 4)) * 2 + core),
                            device_id_type=MESH)
        return carry

    lax.fori_loop(1, 2 * zs, greet_column, 0)
    lax.fori_loop(1, 4 * ns, greet_plane, 0)
    lax.fori_loop(1, 4, greet_diagonal, 0)

    def remote(src_ref, dst_ref, send_sem, recv_sem, device):
        return pltpu.make_async_remote_copy(
            src_ref=src_ref, dst_ref=dst_ref, send_sem=send_sem, recv_sem=recv_sem,
            device_id=device, device_id_type=MESH,
        )

    def take(ref, sem):
        pltpu.make_async_copy(ref, ref, sem).wait()

    def reduce_start(a, parts):
        red1[a, 0] = jnp.concatenate(parts + [jnp.zeros((8 - len(parts), 128), F32)], axis=0)

        def send(n, carry):
            k = lax.rem(n + zs - 2, 2 * zs - 1) + 1
            remote(red1.at[a, 0], red1.at[a, k], red_send.at[a, 0], red_recv.at[a, 0], column_peer(k)).start()
            return carry

        lax.fori_loop(1, 2 * zs, send, 0)

    def reduce_middle(a):
        take(red1.at[a, pl.ds(1, 2 * zs - 1)], red_recv.at[a, 0])

        def add(j, total):
            slot = lax.rem(z_at - j // 2 + zs, zs) * 2 + lax.rem(core + j, 2)
            return total + red1[a, slot]

        red2[a, 0] = lax.fori_loop(0, 2 * zs, add, jnp.zeros((8, 128), F32), unroll=True)

        def send(n, carry):
            k = lax.rem(n + 2 * ns, 4 * ns - 1) + 1
            remote(red2.at[a, 0], red2.at[a, k], red_send.at[a, 1], red_recv.at[a, 1], plane_peer(k)).start()
            return carry

        lax.fori_loop(1, 4 * ns, send, 0)
        take(red1.at[a, pl.ds(1, 2 * zs - 1)], red_send.at[a, 0])

    def reduce_end(a):
        take(red2.at[a, pl.ds(1, 4 * ns - 1)], red_recv.at[a, 1])

        def add(j, total):
            slot = lax.rem(src - j // 4 + ns, ns) * 4 + lax.rem(y_at - lax.rem(j, 4) + 4, 4)
            return total + red2[a, slot]

        total = lax.fori_loop(0, 4 * ns, add, jnp.zeros((8, 128), F32), unroll=True)
        take(red2.at[a, pl.ds(1, 4 * ns - 1)], red_send.at[a, 1])
        return jnp.sum(total, axis=1, keepdims=True)

    def fold(acc):
        part = acc[:, :128]
        for h in range(1, halves):
            part = part + acc[:, h * 128:(h + 1) * 128]
        return jnp.sum(part, axis=0, keepdims=True)

    def split(a):
        high = a.astype(BF16)
        return high, (a - high.astype(F32)).astype(BF16)

    def dot3(a, b):
        mm = functools.partial(jnp.dot, preferred_element_type=F32)
        return mm(a[0], b[0]) + (mm(a[1], b[0]) + mm(a[0], b[1]))

    def local(src_ref, dst_ref):
        hz = (hz_ref[0], hz_ref[1])
        hy = (hy_ref[0], hy_ref[1])
        for pair in range(rows // 2):
            block = src_ref[pl.ds(2 * pair, 2)].reshape(4 * nz, ny)
            depth_done = dot3(hz, split(block))
            done = dot3(split(depth_done), hy)
            dst_ref[pl.ds(2 * pair, 2)] = done.reshape(2, 2 * nz, ny)

    def tile(ref, lead, part, comp):
        z = pl.multiple_of(part // halves * 8, 8)
        y = pl.multiple_of(lax.rem(part, halves) * 128, 128)
        return ref.at[lead, pl.ds(comp * nz + z, 8), pl.ds(y, 128)]

    def ctable(part, which):
        z = pl.multiple_of(part // halves * 8, 8)
        y = pl.multiple_of(lax.rem(part, halves) * 128, 128)
        return tuple(tab_ref[2 * which + c, pl.ds(z, 8), pl.ds(y, 128)] for c in range(2))

    def spectral(sp_ref, lead, part):
        return (tile(sp_ref, lead, part, 0)[...], tile(sp_ref, lead, part, 1)[...])

    def sweep_out(t, extra=None):
        sp_ref, send0, send1 = sp_all.at[t % 2], send0_all.at[t % 2], send1_all.at[t % 2]

        def summarise(part):
            root = ctable(part, 0)
            rowv = [spectral(sp_ref, i, part) for i in range(rows)]
            if extra is not None:
                rowv = [extra(i, part, value) for i, value in enumerate(rowv)]
                for i in range(rows):
                    tile(sp_ref, i, part, 0)[...] = rowv[i][0]
                    tile(sp_ref, i, part, 1)[...] = rowv[i][1]
            ahead = rowv[0]
            for i in range(1, rows):
                ahead = cmadd(ahead, root, rowv[i])
            behind = rowv[rows - 1]
            for i in range(rows - 2, -1, -1):
                behind = cmadd(behind, root, rowv[i])
            return ahead + behind

        def other_half(k, carry):
            g = lax.rem(chip + k, chips)
            vals = summarise(2 * g + 1 - core)
            for c in range(4):
                send0[g, c] = vals[c]
            remote(send0.at[g], sums.at[t, core, g], ex_send.at[t, 0], ex_recv.at[t, 0], partner).start()
            return carry

        def own_half(k, carry):
            g = lax.rem(chip + k, chips)
            vals = summarise(2 * g + core)
            for c in range(4):
                sums[t, core, g, c] = vals[c]
            return carry

        lax.fori_loop(1, chips + 1, other_half, 0, unroll=2)
        lax.fori_loop(1, chips + 1, own_half, 0, unroll=2)
        take(sums.at[t, 1 - core], ex_recv.at[t, 0])

        def combine(g):
            block_root = power(ctable(2 * g + core, 0), int(math.log2(rows)))
            first = [sums[t, 0, g, c] for c in range(4)]
            second = [sums[t, 1, g, c] for c in range(4)]
            return cmadd(first[:2], block_root, second[:2]) + cmadd(second[2:], block_root, first[2:])

        def step(k, carry):
            g = lax.rem(chip + k, chips)
            vals = combine(g)
            for c in range(4):
                send1[g, c] = vals[c]
            remote(send1.at[g], recv1.at[t, k], ex_send.at[t, 1], ex_recv.at[t, 1],
                   (src, base + 2 * g + core)).start()
            return carry

        lax.fori_loop(1, chips, step, 0)
        vals = combine(chip)
        for c in range(4):
            recv1[t, 0, c] = vals[c]

    def power(value, doublings):
        for _ in range(doublings):
            value = cmul(value, value)
        return value

    def own_root():
        return ctable(m, 0)

    def chip_root():
        return power(own_root(), int(math.log2(2 * rows)))

    def middle_out(t):
        take(recv1.at[t, pl.ds(1, chips - 1)], ex_recv.at[t, 1])
        root = chip_root()

        def gather(j, carry):
            ahead, behind = carry
            slot_a = lax.rem(chip - j + chips, chips)
            slot_b = lax.rem(chip + 1 + j, chips)
            ahead = cmadd(ahead, root, (recv1[t, slot_a, 0], recv1[t, slot_a, 1]))
            behind = cmadd(behind, root, (recv1[t, slot_b, 2], recv1[t, slot_b, 3]))
            return ahead, behind

        zero = jnp.zeros((8, 128), F32)
        ahead, behind = lax.fori_loop(0, chips, gather, ((zero, zero), (zero, zero)), unroll=True)
        for c, value in enumerate(ahead + behind):
            recv2[t, 0, c] = value

        def send(k, carry):
            peer = lax.rem(grp + k, g2) * g1 + m
            remote(recv2.at[t, 0], recv2.at[t, k], ex_send.at[t, 2], ex_recv.at[t, 2], (src, peer)).start()
            return carry

        for k in (2, 1, 3):
            send(k, 0)

    def middle_back(t):
        send3 = send3_all.at[t % 2]
        root = chip_root()
        group_root = power(root, int(math.log2(chips)))
        turn = power(group_root, int(math.log2(g2)))
        real, imag = 1.0 - turn[0], turn[1]
        norm = 1.0 / (real * real + imag * imag)
        inverse = (real * norm, imag * norm)
        take(recv2.at[t, pl.ds(1, g2 - 1)], ex_recv.at[t, 2])
        left = (recv2[t, 0, 0], recv2[t, 0, 1])
        right = (recv2[t, 0, 2], recv2[t, 0, 3])
        for k in range(g2 - 1, 0, -1):
            left = cmadd(left, group_root, (recv2[t, k, 0], recv2[t, k, 1]))
            right = cmadd(right, group_root, (recv2[t, g2 - k, 2], recv2[t, g2 - k, 3]))
        left = cmul(left, inverse)
        right = cmul(right, inverse)

        def spread(j, carry):
            left, right = carry
            back = chips - 1 - j
            for c in range(2):
                send3[j, c] = left[c]
                send3[back, 2 + c] = right[c]
            slot_a = lax.rem(chip - j + chips, chips)
            slot_b = lax.rem(chip + 1 + j, chips)
            left = cmadd(left, root, (recv1[t, slot_a, 0], recv1[t, slot_a, 1]))
            right = cmadd(right, root, (recv1[t, slot_b, 2], recv1[t, slot_b, 3]))
            return left, right

        lax.fori_loop(0, chips, spread, (left, right), unroll=True)

        def send(k, carry):
            g = lax.rem(chip + k, chips)
            remote(send3.at[g], recv3.at[t, k], ex_send.at[t, 3], ex_recv.at[t, 3],
                   (src, base + 2 * g + core)).start()
            return carry

        lax.fori_loop(1, chips, send, 0)
        for c in range(4):
            recv3[t, 0, c] = send3[chip, c]

    def sweep_back(t):
        sp_ref, states = sp_all.at[t % 2], states_all.at[t % 2]
        take(recv3.at[t, pl.ds(1, chips - 1)], ex_recv.at[t, 3])

        def pass_on(k, carry):
            g = lax.rem(chip - k + chips, chips)
            block_root = power(ctable(2 * g + core, 0), int(math.log2(rows)))
            left = (recv3[t, k, 0], recv3[t, k, 1])
            right = (recv3[t, k, 2], recv3[t, k, 3])
            inner_left = cmadd(left, block_root, (sums[t, 0, g, 0], sums[t, 0, g, 1]))
            inner_right = cmadd(right, block_root, (sums[t, 1, g, 2], sums[t, 1, g, 3]))
            for c in range(2):
                states[0, g, c] = left[c]
                states[0, g, 2 + c] = inner_right[c]
                states[1, g, c] = inner_left[c]
                states[1, g, 2 + c] = right[c]
            remote(states.at[1 - core, g], recv4.at[t, g], ex_send.at[t, 4], ex_recv.at[t, 4], partner).start()
            return carry

        lax.fori_loop(0, chips, pass_on, 0, unroll=2)

        def apply(part, ends):
            root = ctable(part, 0)
            kappa = ctable(part, 1)
            rowv = [spectral(sp_ref, i, part) for i in range(rows)]
            state = ends[:2]
            ahead = []
            for i in range(rows):
                state = cmadd(state, root, rowv[i])
                ahead.append(state)
            state = cmul(ends[2:], root)
            for i in range(rows - 1, -1, -1):
                total = cmul((ahead[i][0] + state[0], ahead[i][1] + state[1]), kappa)
                tile(sp_ref, i, part, 0)[...] = total[0]
                tile(sp_ref, i, part, 1)[...] = total[1]
                if i:
                    state = cmul((state[0] + rowv[i][0], state[1] + rowv[i][1]), root)

        def own_half(g, carry):
            apply(2 * g + core, tuple(states[core, g, c] for c in range(4)))
            return carry

        def other_half(g, carry):
            apply(2 * g + 1 - core, tuple(recv4[t, g, c] for c in range(4)))
            return carry

        lax.fori_loop(0, chips, own_half, 0, unroll=2)
        take(recv4.at[t], ex_recv.at[t, 4])
        lax.fori_loop(0, chips, other_half, 0, unroll=2)

    def finish(t):
        take(recv4.at[t], ex_send.at[t, 0])
        take(recv1.at[t, pl.ds(1, chips - 1)], ex_send.at[t, 1])
        take(recv2.at[t, pl.ds(1, g2 - 1)], ex_send.at[t, 2])
        take(recv3.at[t, pl.ds(1, chips - 1)], ex_send.at[t, 3])
        take(recv4.at[t], ex_send.at[t, 4])

    def pair(ref, x, z):
        return (ref[x, pl.ds(z, 8), :], ref[x, pl.ds(nz + z, 8), :])

    def put(ref, x, z, value):
        ref[x, pl.ds(z, 8), :] = value[0]
        ref[x, pl.ds(nz + z, 8), :] = value[1]

    def each_block(body, init):
        def outer(n, carry):
            return body(n // zgroups, pl.multiple_of(lax.rem(n, zgroups) * 8, 8), carry)

        return lax.fori_loop(0, rows * zgroups, outer, init, unroll=4)

    def square(value):
        return value[0] * value[0] + value[1] * value[1]

    zero = jnp.zeros((8, ny), F32)
    source_x = pos_ref[0, 0].astype(F32)
    source_y = pos_ref[0, 1].astype(F32)
    offset_y = lax.broadcasted_iota(jnp.int32, (8, ny), 1).astype(F32) - source_y
    offset_y_sq = offset_y * offset_y
    level = lax.broadcasted_iota(jnp.int32, (8, ny), 0).astype(F32) + SOURCE_GAP

    def begin(x, z, carry):
        height = level + z.astype(F32)
        offset_x = (space * rows + x).astype(F32) - source_x
        dist = jnp.sqrt(height * height + offset_x * offset_x + offset_y_sq)
        turns = dist * (1.0 / 6.0)
        sine, cosine = half_turn(turns - jnp.floor(turns + 0.5))
        wave = (1.0 - 2.0 * sine * sine, 2.0 * sine * cosine)
        put(e_ref, x, z, wave)
        return carry

    def excite(x, z, total):
        field = cmul(pair(chi0_ref, x, z), pair(e_ref, x, z))
        put(w_ref, x, z, field)
        return total + square(field)

    each_block(begin, 0)
    take(chi0_ref, local_sem.at[0])
    object_part = each_block(excite, zero)
    data_part = jnp.zeros((1, ny), F32)
    for x in range(rows):
        for c in range(2):
            data_part = data_part + meas_ref[c, pl.ds(x, 1), :] * meas_ref[c, pl.ds(x, 1), :]
    data_fold = data_part[:, :128]
    for h in range(1, halves):
        data_fold = data_fold + data_part[:, h * 128:(h + 1) * 128]

    take(hz_ref, local_sem.at[1])
    take(hy_ref, local_sem.at[2])
    local(w_ref, sp_all.at[0])
    take(tab_ref, local_sem.at[3])
    pl.semaphore_wait(barrier, (2 * zs - 1) + (4 * ns - 1) + 3)
    sweep_out(0)
    reduce_start(0, [data_fold, fold(object_part)])
    middle_out(0)
    reduce_middle(0)
    middle_back(0)
    totals = reduce_end(0)
    sweep_back(0)
    finish(0)
    local(sp_all.at[0], s_ref)
    data_total = totals[0:1]
    object_share = totals[1:2] / data_total
    ratio = 0.5 / DAMPING
    level_zero = 1.0 / math.sqrt(nz)
    chi_ref = chi0_ref
    for update in range(OUTER):
        t = 1 + 2 * update
        a = 1 + 2 * update
        last = update == OUTER - 1
        chi_next = chi2_ref if last else chi1_ref
        early, late = early_recv.at[update], late_recv.at[update]
        right, left, across = (lax.rem(src + k, ns) for k in (1, 3, 2))

        for k in (0, 3, 1, 2):
            x = lax.rem(src + k, ns)
            if update and k:
                take(chi_ref.at[0], chi_took.at[update - 1, ns - k])

            def residual(n, carry, x=x, chi_ref=chi_ref):
                z = pl.multiple_of(n * 8, 8)
                chi = pair(chi_ref, x, z)
                e, s, w = pair(e_ref, x, z), pair(s_ref, x, z), pair(w_ref, x, z)
                u = (e[0] + s[0], e[1] + s[1])
                field = cmul(chi, u)
                res = (field[0] - w[0], field[1] - w[1])
                put(r_ref, x, z, res)
                flipped = cmul(chi, (res[0], -res[1]))
                put(v_ref, x, z, (-flipped[0], -flipped[1]))
                put(b_ref, x, z, (res[0] + ratio * flipped[1], res[1] + ratio * flipped[0]))
                early_ref[x, pl.ds(z, 8), :] = w[0] * u[0] + w[1] * u[1]
                early_ref[x, pl.ds(nz + z, 8), :] = w[1] * u[0] - w[0] * u[1]
                early_ref[x, pl.ds(2 * nz + z, 8), :] = square(u)
                return carry

            lax.fori_loop(0, zgroups, residual, 0, unroll=4)
            if k:
                remote(early_ref.at[x], early.at[k], x_send.at[update, 0], x_recv.at[update, 0], (x, space)).start()
        rho = jnp.concatenate(
            [
                meas_ref[c, pl.ds(x, 1), :] - s_ref[x, pl.ds(c * nz, 1), :]
                for x in range(rows) for c in range(2)
            ],
            axis=0,
        )
        rho_ref[...] = level_zero * dot3(split(rho), (hy_ref[0], hy_ref[1]))

        first, second = sp_all.at[t % 2], sp_all.at[(t + 1) % 2]
        local(v_ref, first)
        if update:
            local(b_ref, second)
            object_share = float(ns) * reduce_end(2)[0:1] / data_total

        def rho_tile(i, part, c, object_share=object_share):
            y = pl.multiple_of(lax.rem(part, halves) * 128, 128)
            return object_share * rho_ref[pl.ds(2 * i + c, 1), pl.ds(y, 128)]

        def add_first(i, part, value, rho_tile=rho_tile):
            return value[0] + rho_tile(i, part, 0), value[1] - rho_tile(i, part, 1)

        def add_second(i, part, value, rho_tile=rho_tile):
            return value[0] + ratio * rho_tile(i, part, 1), value[1] - ratio * rho_tile(i, part, 0)

        sweep_out(t, add_first)
        if not update:
            local(b_ref, second)
        sweep_out(t + 1, add_second)
        middle_out(t)
        middle_out(t + 1)
        middle_back(t)
        middle_back(t + 1)
        sweep_back(t)
        local(first, d_ref)
        sweep_back(t + 1)
        local(second, v_ref)
        finish(t)
        finish(t + 1)

        def pass_late(row, half, place, device, update=update, late=late):
            remote(late_ref.at[row, half], late.at[place, half], late_send.at[update, place, half],
                   late_took.at[update, place, half], (device, space)).start()

        def add_late(row, half, update=update, late=late):
            take(late.at[0, half], late_took.at[update, 0, half])

            def add(n, carry):
                at = pl.ds(pl.multiple_of(n * 8, 8), 8)
                late_ref[row, half, at, :] = late_ref[row, half, at, :] + late[0, half, at, :]
                return carry

            lax.fori_loop(0, 3 * zgroups, add, 0, unroll=8)

        totals = (zero, zero)
        for k in (2, 1, 3, 0):
            x = lax.rem(src + k, ns)

            def descend(n, totals, x=x, chi_ref=chi_ref):
                z = pl.multiple_of(n * 8, 8)
                res, image, other = pair(r_ref, x, z), pair(d_ref, x, z), pair(v_ref, x, z)
                d = (res[0] + image[0], res[1] - image[1])
                h = (other[0] + ratio * image[1], other[1] + ratio * image[0])
                put(d_ref, x, z, d)
                put(v_ref, x, z, h)
                moved = cmul(pair(chi_ref, x, z), h)
                e, s, w = pair(e_ref, x, z), pair(s_ref, x, z), pair(w_ref, x, z)
                u = (e[0] + s[0], e[1] + s[1])
                late_parts = (
                    d[0] * u[0] + d[1] * u[1] + (w[0] * h[0] + w[1] * h[1]),
                    d[1] * u[0] - d[0] * u[1] + (w[1] * h[0] - w[0] * h[1]),
                    2.0 * (u[0] * h[0] + u[1] * h[1]),
                    d[0] * h[0] + d[1] * h[1],
                    d[1] * h[0] - d[0] * h[1],
                    square(h),
                )
                half = n // (zgroups // 2)
                for c, value in enumerate(late_parts):
                    late_ref[x, half, pl.ds(c * (nz // 2) + z - half * (nz // 2), 8), :] = value
                return totals[0] + square(d), totals[1] + square((d[0] - moved[0], d[1] - moved[1]))

            totals = lax.fori_loop(0, zgroups, descend, totals, unroll=4)
            if k == 2:
                pass_late(across, 0, 0, right)
                pass_late(across, 1, 0, left)
            elif k == 1:
                pass_late(right, 1, 1, right)
            elif k == 3:
                pass_late(left, 0, 2, left)
        image_part = jnp.zeros((1, ny), F32)
        for x in range(rows):
            image_part = image_part + square((v_ref[x, pl.ds(0, 1), :], v_ref[x, pl.ds(nz, 1), :]))
        image_fold = image_part[:, :128]
        for h in range(1, halves):
            image_fold = image_fold + image_part[:, h * 128:(h + 1) * 128]
        reduce_start(a, [fold(totals[0]), image_fold, fold(totals[1])])
        take(early.at[pl.ds(1, ns - 1)], x_recv.at[update, 0])

        def gather_early(n, carry, early=early):
            at = pl.ds(pl.multiple_of(n * 8, 8), 8)
            early_ref[src, at, :] = early_ref[src, at, :] + early[1, at, :] + early[2, at, :] + early[3, at, :]
            return carry

        lax.fori_loop(0, 3 * zgroups, gather_early, 0, unroll=4)
        reduce_middle(a)
        add_late(right, 0)
        pass_late(right, 0, 1, right)
        add_late(left, 1)
        pass_late(left, 1, 2, left)
        totals = reduce_end(a)
        length = totals[0:1] / (object_share * totals[1:2] + totals[2:3])

        def advance(x, z, carry, length=length, last=last):
            w, d = pair(w_ref, x, z), pair(d_ref, x, z)
            put(w_ref, x, z, (w[0] + length * d[0], w[1] + length * d[1]))
            if not last:
                s, h = pair(s_ref, x, z), pair(v_ref, x, z)
                put(s_ref, x, z, (s[0] + length * h[0], s[1] + length * h[1]))
            return carry

        each_block(advance, 0)
        if last:
            for x in range(rows):
                for c in range(2):
                    pltpu.make_async_copy(
                        w_ref.at[x, pl.ds(c * nz, nz), :], w_hbm.at[c, :, x, :], local_sem.at[4]
                    ).start()
        for half in range(2):
            for place in (1, 2):
                take(late.at[place, half], late_took.at[update, place, half])

        def contrast(n, total, length=length, late=late, chi_next=chi_next):
            z = pl.multiple_of(n * 8, 8)
            terms = []
            half = n // (zgroups // 2)
            for c in range(6):
                at = pl.ds(c * (nz // 2) + z - half * (nz // 2), 8)
                terms.append(late_ref[src, half, at, :] + late[1, half, at, :] + late[2, half, at, :])
            parts = [
                early_ref[src, pl.ds(c * nz + z, 8), :] + length * (terms[c] + length * terms[3 + c]) for c in range(3)
            ]
            scale = 1.0 / jnp.maximum(parts[2], FLOOR_SHARE * ns)
            chi = (jnp.clip(parts[0] * scale, REAL_LOW, REAL_HIGH), jnp.clip(parts[1] * scale, 0.0, IMAG_HIGH))
            put(chi_next, src, z, chi)
            return total + square(chi)

        chi_part = lax.fori_loop(0, zgroups, contrast, zero, unroll=2)
        if not last:
            reduce_start(2, [fold(chi_part)])
        for k in (2, 1, 3):
            remote(chi_next.at[src], chi_next.at[src], x_send.at[update, 1], chi_took.at[update, k],
                   (lax.rem(src + k, ns), space)).start()
        if not last:
            reduce_middle(2)
        else:
            for k in (0, 1, 3, 2):
                x = lax.rem(src + k, ns)
                if k:
                    take(chi_next.at[0], chi_took.at[update, ns - k])
                for c in range(2):
                    pltpu.make_async_copy(
                        chi_next.at[x, pl.ds(c * nz, nz), :], chi_hbm.at[c, :, x, :], local_sem.at[5]
                    ).start()
        take(early.at[pl.ds(1, ns - 1)], x_send.at[update, 0])
        for half in range(2):
            for place in range(3):
                take(late.at[place, half], late_send.at[update, place, half])
        chi_ref = chi_next
    for update in range(OUTER):
        take(chi2_ref.at[pl.ds(0, ns - 1)], x_send.at[update, 1])
    take(w_ref, local_sem.at[4])
    take(chi2_ref, local_sem.at[5])


def on_device(ns, g1, g2, contrast, measured, positions):
    _, nz, rows, ny = contrast.shape
    cfg = (ns, g1, g2, nz, ny, rows)
    transforms = 1 + 2 * OUTER
    reductions = 2 * OUTER
    tables = decay_tables(nz, ny)
    hy = high_low(hartley(ny))
    hz = high_low(np.kron(np.eye(4), hartley(nz)))
    field = (rows, 2 * nz, ny)
    vmem = pl.BlockSpec(memory_space=pltpu.VMEM)
    anywhere = pl.BlockSpec(memory_space=pltpu.HBM)
    w, chi = pl.pallas_call(
        functools.partial(kernel, cfg),
        out_shape=(jax.ShapeDtypeStruct(contrast.shape, F32), jax.ShapeDtypeStruct(contrast.shape, F32)),
        in_specs=[pl.BlockSpec(memory_space=pltpu.SMEM), vmem] + [anywhere] * 4,
        out_specs=(anywhere, anywhere),
        scratch_shapes=[
            pltpu.VMEM(field, F32),
            pltpu.VMEM(tables.shape, F32),
            pltpu.VMEM(hy.shape, BF16),
            pltpu.VMEM(hz.shape, BF16),
        ] + [pltpu.VMEM(field, F32)] * 9 + [
            pltpu.VMEM((2,) + field, F32),
            pltpu.VMEM((2 * rows, ny), F32),
            pltpu.VMEM((rows, 3 * nz, ny), F32),
            pltpu.VMEM((OUTER, ns, 3 * nz, ny), F32),
            pltpu.VMEM((rows, 2, 3 * nz, ny), F32),
            pltpu.VMEM((OUTER, 3, 2, 3 * nz, ny), F32),
            pltpu.VMEM((2, g1 // 2, 4, 8, 128), F32),
            pltpu.VMEM((2, g1 // 2, 4, 8, 128), F32),
            pltpu.VMEM((2, g1 // 2, 4, 8, 128), F32),
            pltpu.VMEM((2, 2, g1 // 2, 4, 8, 128), F32),
            pltpu.VMEM((transforms, 2, g1 // 2, 4, 8, 128), F32),
            pltpu.VMEM((transforms, g1 // 2, 4, 8, 128), F32),
            pltpu.VMEM((transforms, g2, 4, 8, 128), F32),
            pltpu.VMEM((transforms, g1 // 2, 4, 8, 128), F32),
            pltpu.VMEM((transforms, g1 // 2, 4, 8, 128), F32),
            pltpu.VMEM((reductions, g1 * g2 // 4, 8, 128), F32),
            pltpu.VMEM((reductions, 4 * ns, 8, 128), F32),
            pltpu.SemaphoreType.DMA((transforms, 5)),
            pltpu.SemaphoreType.DMA((transforms, 5)),
            pltpu.SemaphoreType.DMA((reductions, 2)),
            pltpu.SemaphoreType.DMA((reductions, 2)),
            pltpu.SemaphoreType.DMA((OUTER, 2)),
            pltpu.SemaphoreType.DMA((OUTER, 2)),
            pltpu.SemaphoreType.DMA((OUTER, 3, 2)),
            pltpu.SemaphoreType.DMA((OUTER, 3, 2)),
            pltpu.SemaphoreType.DMA((OUTER, ns)),
            pltpu.SemaphoreType.DMA((6,)),
        ],
        compiler_params=pltpu.CompilerParams(
            collective_id=0, has_side_effects=True, vmem_limit_bytes=56 * 1024 * 1024
        ),
    )(positions, measured[0], contrast, tables, hy, hz)
    return w[None], chi


def solution(mesh, g2=4):
    placed = (P(None, None, "space", None), P("src", None, "space", None), P("src", None))
    return jax.shard_map(
        functools.partial(on_device, mesh.shape["src"], mesh.shape["space"] // g2, g2),
        mesh=mesh,
        in_specs=placed,
        out_specs=(P("src", None, None, "space", None), P(None, None, "space", None)),
        check_vma=False,
    )
```

```python
import functools
import math

import jax
import jax.numpy as jnp
import ml_dtypes
import numpy as np
from jax import lax
from jax.experimental import pallas as pl
from jax.experimental.pallas import tpu as pltpu
from jax.sharding import PartitionSpec as P

OUTER = 2
WAVENUMBER = 2.0 * math.pi / 6.0
DAMPING = 0.3
SOURCE_GAP = 8.0
FLOOR_SHARE = 0.75
REAL_LOW = -0.25
REAL_HIGH = 0.35
IMAG_HIGH = 0.1
F32 = jnp.float32
BF16 = jnp.bfloat16
MESH = pl.DeviceIdType.MESH


def hartley(length):
    turn = np.outer(np.arange(length), np.arange(length)) % length
    angle = 2.0 * np.pi / length * turn
    return (np.cos(angle) + np.sin(angle)) / np.sqrt(length)


def high_low(table):
    high = table.astype(ml_dtypes.bfloat16)
    low = (table - high.astype(np.float64)).astype(ml_dtypes.bfloat16)
    return np.stack([high, low])


def modes(length):
    return 4.0 * np.sin(np.pi * np.arange(length) / length) ** 2


def decay_tables(depth, across):
    wave_sq = WAVENUMBER * WAVENUMBER
    trace = 2.0 + modes(depth)[:, None] + modes(across)[None, :] - wave_sq * (1.0 + 1j * DAMPING)
    root = np.sqrt(trace * trace - 4.0)
    first = (trace - root) / 2.0
    second = (trace + root) / 2.0
    small = np.where(np.abs(first) < np.abs(second), first, second)
    large = np.where(np.abs(first) < np.abs(second), second, first)
    small = 1.0 / large
    kappa = wave_sq / (large - small)
    tables = np.stack([small.real, small.imag, kappa.real, kappa.imag])
    return tables.astype(np.float32)


def cmul(a, b):
    return (a[0] * b[0] - a[1] * b[1], a[0] * b[1] + a[1] * b[0])


def cmadd(a, b, c):
    return (a[0] * b[0] - a[1] * b[1] + c[0], a[0] * b[1] + a[1] * b[0] + c[1])


def half_turn(fraction):
    angle = fraction * math.pi
    sq = angle * angle
    sine = jnp.full_like(sq, -1.0 / math.factorial(11))
    for order in (9, 7, 5, 3, 1):
        sine = sine * sq + (1.0 if order % 4 == 1 else -1.0) / math.factorial(order)
    cosine = jnp.full_like(sq, 1.0 / math.factorial(12))
    for order in (10, 8, 6, 4, 2, 0):
        cosine = cosine * sq + (1.0 if order % 4 == 0 else -1.0) / math.factorial(order)
    return sine * angle, cosine


def kernel(
    cfg,
    pos_ref, meas_ref, contrast_hbm, tab_hbm, hy_hbm, hz_hbm,
    w_hbm, chi_hbm,
    chi0_ref, tab_ref, hy_ref, hz_ref, w_ref, chi2_ref, chi1_ref, e_ref, s_ref, r_ref, d_ref, v_ref, b_ref, sp_all, rho_ref, early_ref, early_recv, late_ref, late_recv,
    send0_all, send1_all, send3_all, states_all, sums, recv1, recv2, recv3, recv4, red1, red2,
    ex_send, ex_recv, red_send, red_recv, x_send, x_recv, late_send, late_took, chi_took, local_sem,
):
    ns, g1, g2, nz, ny, rows = cfg
    halves = ny // 128
    nx = g1 * g2 * rows
    zgroups = nz // 8
    src = lax.axis_index("src")
    space = lax.axis_index("space")
    m = lax.rem(space, g1)
    chips = g1 // 2
    core = lax.rem(m, 2)
    chip = m // 2
    far_first = (6, 2, 5, 3, 7, 1, 4)
    grp = space // g1
    base = grp * g1

    partner = (src, space + 1 - 2 * core)

    for x in range(rows):
        for c in range(2):
            pltpu.make_async_copy(
                contrast_hbm.at[c, :, x, :], chi0_ref.at[x, pl.ds(c * nz, nz), :], local_sem.at[0]
            ).start()
    pltpu.make_async_copy(hz_hbm, hz_ref, local_sem.at[1]).start()
    pltpu.make_async_copy(hy_hbm, hy_ref, local_sem.at[2]).start()
    pltpu.make_async_copy(tab_hbm, tab_ref, local_sem.at[3]).start()

    barrier = pltpu.get_barrier_semaphore()

    zs = g1 * g2 // 8
    z_at, y_at = space // 8, lax.rem(space // 2, 4)

    def column_peer(k):
        return src, (lax.rem(z_at + k // 2, zs) * 4 + y_at) * 2 + lax.rem(core + k, 2)

    def plane_peer(k):
        return lax.rem(src + k // 4, ns), (z_at * 4 + lax.rem(y_at + k, 4)) * 2 + core

    def greet_column(k, carry):
        pl.semaphore_signal(barrier, inc=1, device_id=column_peer(k), device_id_type=MESH)
        return carry

    def greet_plane(k, carry):
        pl.semaphore_signal(barrier, inc=1, device_id=plane_peer(k), device_id_type=MESH)
        return carry

    def greet_diagonal(k, carry):
        z_other = z_at + 1 - 2 * lax.rem(z_at, 2)
        pl.semaphore_signal(barrier, inc=1, device_id=(src, (z_other * 4 + lax.rem(y_at + k, 4)) * 2 + core),
                            device_id_type=MESH)
        return carry

    lax.fori_loop(1, 2 * zs, greet_column, 0)
    lax.fori_loop(1, 4 * ns, greet_plane, 0)
    lax.fori_loop(1, 4, greet_diagonal, 0)

    def remote(src_ref, dst_ref, send_sem, recv_sem, device):
        return pltpu.make_async_remote_copy(
            src_ref=src_ref, dst_ref=dst_ref, send_sem=send_sem, recv_sem=recv_sem,
            device_id=device, device_id_type=MESH,
        )

    def take(ref, sem):
        pltpu.make_async_copy(ref, ref, sem).wait()

    def reduce_start(a, parts):
        red1[a, 0] = jnp.concatenate(parts + [jnp.zeros((8 - len(parts), 128), F32)], axis=0)

        def send(n, carry):
            k = lax.rem(n + zs - 2, 2 * zs - 1) + 1
            remote(red1.at[a, 0], red1.at[a, k], red_send.at[a, 0], red_recv.at[a, 0], column_peer(k)).start()
            return carry

        lax.fori_loop(1, 2 * zs, send, 0)

    def reduce_middle(a):
        take(red1.at[a, pl.ds(1, 2 * zs - 1)], red_recv.at[a, 0])

        def add(j, total):
            slot = lax.rem(z_at - j // 2 + zs, zs) * 2 + lax.rem(core + j, 2)
            return total + red1[a, slot]

        red2[a, 0] = lax.fori_loop(0, 2 * zs, add, jnp.zeros((8, 128), F32), unroll=True)

        def send(n, carry):
            k = lax.rem(n + 2 * ns, 4 * ns - 1) + 1
            remote(red2.at[a, 0], red2.at[a, k], red_send.at[a, 1], red_recv.at[a, 1], plane_peer(k)).start()
            return carry

        lax.fori_loop(1, 4 * ns, send, 0)
        take(red1.at[a, pl.ds(1, 2 * zs - 1)], red_send.at[a, 0])

    def reduce_end(a):
        take(red2.at[a, pl.ds(1, 4 * ns - 1)], red_recv.at[a, 1])

        def add(j, total):
            slot = lax.rem(src - j // 4 + ns, ns) * 4 + lax.rem(y_at - lax.rem(j, 4) + 4, 4)
            return total + red2[a, slot]

        total = lax.fori_loop(0, 4 * ns, add, jnp.zeros((8, 128), F32), unroll=True)
        take(red2.at[a, pl.ds(1, 4 * ns - 1)], red_send.at[a, 1])
        return jnp.sum(total, axis=1, keepdims=True)

    def fold(acc):
        part = acc[:, :128]
        for h in range(1, halves):
            part = part + acc[:, h * 128:(h + 1) * 128]
        return jnp.sum(part, axis=0, keepdims=True)

    def split(a):
        high = a.astype(BF16)
        return high, (a - high.astype(F32)).astype(BF16)

    def dot3(a, b):
        mm = functools.partial(jnp.dot, preferred_element_type=F32)
        return mm(a[0], b[0]) + (mm(a[1], b[0]) + mm(a[0], b[1]))

    def local_pair(src_ref, dst_ref, n):
        at = pl.ds(2 * n, 2)
        depth_done = dot3((hz_ref[0], hz_ref[1]), split(src_ref[at].reshape(4 * nz, ny)))
        dst_ref[at] = dot3(split(depth_done), (hy_ref[0], hy_ref[1])).reshape(2, 2 * nz, ny)

    def local(src_ref, dst_ref):
        for n in range(rows // 2):
            local_pair(src_ref, dst_ref, n)

    def tile(ref, lead, part, comp):
        z = pl.multiple_of(part // halves * 8, 8)
        y = pl.multiple_of(lax.rem(part, halves) * 128, 128)
        return ref.at[lead, pl.ds(comp * nz + z, 8), pl.ds(y, 128)]

    def ctable(part, which):
        z = pl.multiple_of(part // halves * 8, 8)
        y = pl.multiple_of(lax.rem(part, halves) * 128, 128)
        return tuple(tab_ref[2 * which + c, pl.ds(z, 8), pl.ds(y, 128)] for c in range(2))

    def spectral(sp_ref, lead, part):
        return (tile(sp_ref, lead, part, 0)[...], tile(sp_ref, lead, part, 1)[...])

    def sweep_out(t, extra=None):
        sp_ref, send0, send1 = sp_all.at[t % 2], send0_all.at[t % 2], send1_all.at[t % 2]

        def summarise(part):
            root = ctable(part, 0)
            rowv = [spectral(sp_ref, i, part) for i in range(rows)]
            if extra is not None:
                rowv = [extra(i, part, value) for i, value in enumerate(rowv)]
                for i in range(rows):
                    tile(sp_ref, i, part, 0)[...] = rowv[i][0]
                    tile(sp_ref, i, part, 1)[...] = rowv[i][1]
            ahead = rowv[0]
            for i in range(1, rows):
                ahead = cmadd(ahead, root, rowv[i])
            behind = rowv[rows - 1]
            for i in range(rows - 2, -1, -1):
                behind = cmadd(behind, root, rowv[i])
            return ahead + behind

        def other_half(k, carry):
            g = lax.rem(chip + k, chips)
            vals = summarise(2 * g + 1 - core)
            for c in range(4):
                send0[g, c] = vals[c]
            remote(send0.at[g], sums.at[t, core, g], ex_send.at[t, 0], ex_recv.at[t, 0], partner).start()
            return carry

        def own_half(k, carry):
            g = lax.rem(chip + k, chips)
            vals = summarise(2 * g + core)
            for c in range(4):
                sums[t, core, g, c] = vals[c]
            return carry

        lax.fori_loop(1, chips + 1, other_half, 0, unroll=2)
        lax.fori_loop(1, chips + 1, own_half, 0, unroll=2)
        take(sums.at[t, 1 - core], ex_recv.at[t, 0])

        def combine(g):
            block_root = power(ctable(2 * g + core, 0), int(math.log2(rows)))
            first = [sums[t, 0, g, c] for c in range(4)]
            second = [sums[t, 1, g, c] for c in range(4)]
            return cmadd(first[:2], block_root, second[:2]) + cmadd(second[2:], block_root, first[2:])

        def step(k, carry):
            g = lax.rem(chip + k, chips)
            vals = combine(g)
            for c in range(4):
                send1[g, c] = vals[c]
            remote(send1.at[g], recv1.at[t, k], ex_send.at[t, 1], ex_recv.at[t, 1],
                   (src, base + 2 * g + core)).start()
            return carry

        for k in far_first:
            step(k, 0)
        vals = combine(chip)
        for c in range(4):
            recv1[t, 0, c] = vals[c]

    def power(value, doublings):
        for _ in range(doublings):
            value = cmul(value, value)
        return value

    def own_root():
        return ctable(m, 0)

    def chip_root():
        return power(own_root(), int(math.log2(2 * rows)))

    def middle_out(t):
        take(recv1.at[t, pl.ds(1, chips - 1)], ex_recv.at[t, 1])
        root = chip_root()

        def gather(j, carry):
            ahead, behind = carry
            slot_a = lax.rem(chip - j + chips, chips)
            slot_b = lax.rem(chip + 1 + j, chips)
            ahead = cmadd(ahead, root, (recv1[t, slot_a, 0], recv1[t, slot_a, 1]))
            behind = cmadd(behind, root, (recv1[t, slot_b, 2], recv1[t, slot_b, 3]))
            return ahead, behind

        zero = jnp.zeros((8, 128), F32)
        ahead, behind = lax.fori_loop(0, chips, gather, ((zero, zero), (zero, zero)), unroll=True)
        for c, value in enumerate(ahead + behind):
            recv2[t, 0, c] = value

        def send(k, carry):
            peer = lax.rem(grp + k, g2) * g1 + m
            remote(recv2.at[t, 0], recv2.at[t, k], ex_send.at[t, 2], ex_recv.at[t, 2], (src, peer)).start()
            return carry

        for k in (2, 1, 3):
            send(k, 0)

    def middle_back(t):
        send3 = send3_all.at[t % 2]
        root = chip_root()
        group_root = power(root, int(math.log2(chips)))
        turn = power(group_root, int(math.log2(g2)))
        real, imag = 1.0 - turn[0], turn[1]
        norm = 1.0 / (real * real + imag * imag)
        inverse = (real * norm, imag * norm)
        take(recv2.at[t, pl.ds(1, g2 - 1)], ex_recv.at[t, 2])
        left = (recv2[t, 0, 0], recv2[t, 0, 1])
        right = (recv2[t, 0, 2], recv2[t, 0, 3])
        for k in range(g2 - 1, 0, -1):
            left = cmadd(left, group_root, (recv2[t, k, 0], recv2[t, k, 1]))
            right = cmadd(right, group_root, (recv2[t, g2 - k, 2], recv2[t, g2 - k, 3]))
        left = cmul(left, inverse)
        right = cmul(right, inverse)

        def spread(j, carry):
            left, right = carry
            back = chips - 1 - j
            for c in range(2):
                send3[j, c] = left[c]
                send3[back, 2 + c] = right[c]
            slot_a = lax.rem(chip - j + chips, chips)
            slot_b = lax.rem(chip + 1 + j, chips)
            left = cmadd(left, root, (recv1[t, slot_a, 0], recv1[t, slot_a, 1]))
            right = cmadd(right, root, (recv1[t, slot_b, 2], recv1[t, slot_b, 3]))
            return left, right

        lax.fori_loop(0, chips, spread, (left, right), unroll=True)

        def send(k, carry):
            g = lax.rem(chip + k, chips)
            remote(send3.at[g], recv3.at[t, k], ex_send.at[t, 3], ex_recv.at[t, 3],
                   (src, base + 2 * g + core)).start()
            return carry

        for k in far_first:
            send(k, 0)
        for c in range(4):
            recv3[t, 0, c] = send3[chip, c]

    def sweep_back(t):
        sp_ref, states = sp_all.at[t % 2], states_all.at[t % 2]
        take(recv3.at[t, pl.ds(1, chips - 1)], ex_recv.at[t, 3])

        def pass_on(k, carry):
            g = lax.rem(chip - k + chips, chips)
            block_root = power(ctable(2 * g + core, 0), int(math.log2(rows)))
            left = (recv3[t, k, 0], recv3[t, k, 1])
            right = (recv3[t, k, 2], recv3[t, k, 3])
            inner_left = cmadd(left, block_root, (sums[t, 0, g, 0], sums[t, 0, g, 1]))
            inner_right = cmadd(right, block_root, (sums[t, 1, g, 2], sums[t, 1, g, 3]))
            for c in range(2):
                states[0, g, c] = left[c]
                states[0, g, 2 + c] = inner_right[c]
                states[1, g, c] = inner_left[c]
                states[1, g, 2 + c] = right[c]
            remote(states.at[1 - core, g], recv4.at[t, g], ex_send.at[t, 4], ex_recv.at[t, 4], partner).start()
            return carry

        lax.fori_loop(0, chips, pass_on, 0, unroll=2)

        def apply(part, ends):
            root = ctable(part, 0)
            kappa = ctable(part, 1)
            rowv = [spectral(sp_ref, i, part) for i in range(rows)]
            state = ends[:2]
            ahead = []
            for i in range(rows):
                state = cmadd(state, root, rowv[i])
                ahead.append(state)
            state = cmul(ends[2:], root)
            for i in range(rows - 1, -1, -1):
                total = cmul((ahead[i][0] + state[0], ahead[i][1] + state[1]), kappa)
                tile(sp_ref, i, part, 0)[...] = total[0]
                tile(sp_ref, i, part, 1)[...] = total[1]
                if i:
                    state = cmul((state[0] + rowv[i][0], state[1] + rowv[i][1]), root)

        def own_half(g, carry):
            apply(2 * g + core, tuple(states[core, g, c] for c in range(4)))
            return carry

        def other_half(g, carry):
            apply(2 * g + 1 - core, tuple(recv4[t, g, c] for c in range(4)))
            return carry

        lax.fori_loop(0, chips, own_half, 0, unroll=2)
        take(recv4.at[t], ex_recv.at[t, 4])
        lax.fori_loop(0, chips, other_half, 0, unroll=2)

    def finish(t):
        take(recv4.at[t], ex_send.at[t, 0])
        take(recv1.at[t, pl.ds(1, chips - 1)], ex_send.at[t, 1])
        take(recv2.at[t, pl.ds(1, g2 - 1)], ex_send.at[t, 2])
        take(recv3.at[t, pl.ds(1, chips - 1)], ex_send.at[t, 3])
        take(recv4.at[t], ex_send.at[t, 4])

    def pair(ref, x, z):
        return (ref[x, pl.ds(z, 8), :], ref[x, pl.ds(nz + z, 8), :])

    def put(ref, x, z, value):
        ref[x, pl.ds(z, 8), :] = value[0]
        ref[x, pl.ds(nz + z, 8), :] = value[1]

    def each_block(body, init):
        def outer(n, carry):
            return body(n // zgroups, pl.multiple_of(lax.rem(n, zgroups) * 8, 8), carry)

        return lax.fori_loop(0, rows * zgroups, outer, init, unroll=4)

    def square(value):
        return value[0] * value[0] + value[1] * value[1]

    zero = jnp.zeros((8, ny), F32)
    source_x = pos_ref[0, 0].astype(F32)
    source_y = pos_ref[0, 1].astype(F32)
    offset_y = lax.broadcasted_iota(jnp.int32, (8, ny), 1).astype(F32) - source_y
    offset_y_sq = offset_y * offset_y
    level = lax.broadcasted_iota(jnp.int32, (8, ny), 0).astype(F32) + SOURCE_GAP

    def begin(x, z, carry):
        height = level + z.astype(F32)
        offset_x = (space * rows + x).astype(F32) - source_x
        dist = jnp.sqrt(height * height + offset_x * offset_x + offset_y_sq)
        turns = dist * (1.0 / 6.0)
        sine, cosine = half_turn(turns - jnp.floor(turns + 0.5))
        wave = (1.0 - 2.0 * sine * sine, 2.0 * sine * cosine)
        put(e_ref, x, z, wave)
        return carry

    def excite(x, z, total):
        field = cmul(pair(chi0_ref, x, z), pair(e_ref, x, z))
        put(w_ref, x, z, field)
        return total + square(field)

    each_block(begin, 0)
    take(chi0_ref, local_sem.at[0])
    object_part = each_block(excite, zero)
    data_part = jnp.zeros((1, ny), F32)
    for x in range(rows):
        for c in range(2):
            data_part = data_part + meas_ref[c, pl.ds(x, 1), :] * meas_ref[c, pl.ds(x, 1), :]
    data_fold = data_part[:, :128]
    for h in range(1, halves):
        data_fold = data_fold + data_part[:, h * 128:(h + 1) * 128]

    take(hz_ref, local_sem.at[1])
    take(hy_ref, local_sem.at[2])
    local(w_ref, sp_all.at[0])
    take(tab_ref, local_sem.at[3])
    pl.semaphore_wait(barrier, (2 * zs - 1) + (4 * ns - 1) + 3)
    sweep_out(0)
    reduce_start(0, [data_fold, fold(object_part)])
    middle_out(0)
    reduce_middle(0)
    middle_back(0)
    totals = reduce_end(0)
    sweep_back(0)
    finish(0)
    local(sp_all.at[0], s_ref)
    data_total = totals[0:1]
    object_share = totals[1:2] / data_total
    ratio = 0.5 / DAMPING
    level_zero = 1.0 / math.sqrt(nz)
    chi_ref = chi0_ref
    for update in range(OUTER):
        t = 1 + 2 * update
        a = 1 + 2 * update
        last = update == OUTER - 1
        chi_next = chi2_ref if last else chi1_ref
        early, late = early_recv.at[update], late_recv.at[update]
        right, left, across = (lax.rem(src + k, ns) for k in (1, 3, 2))

        own_pair = src // 2
        mate = src + 1 - 2 * lax.rem(src, 2)
        first, second = sp_all.at[t % 2], sp_all.at[(t + 1) % 2]
        for place, x in enumerate((src, mate, lax.rem(mate + 2, ns), across)):
            k = lax.rem(x - src + ns, ns)
            if update and place:
                take(chi_ref.at[0], chi_took.at[update - 1, ns - k])

            def residual(n, carry, x=x, chi_ref=chi_ref):
                z = pl.multiple_of(n * 8, 8)
                chi = pair(chi_ref, x, z)
                e, s, w = pair(e_ref, x, z), pair(s_ref, x, z), pair(w_ref, x, z)
                u = (e[0] + s[0], e[1] + s[1])
                field = cmul(chi, u)
                res = (field[0] - w[0], field[1] - w[1])
                put(r_ref, x, z, res)
                flipped = cmul(chi, (res[0], -res[1]))
                put(v_ref, x, z, (-flipped[0], -flipped[1]))
                put(b_ref, x, z, (res[0] + ratio * flipped[1], res[1] + ratio * flipped[0]))
                early_ref[x, pl.ds(z, 8), :] = w[0] * u[0] + w[1] * u[1]
                early_ref[x, pl.ds(nz + z, 8), :] = w[1] * u[0] - w[0] * u[1]
                early_ref[x, pl.ds(2 * nz + z, 8), :] = square(u)
                return carry

            lax.fori_loop(0, zgroups, residual, 0, unroll=4)
            if place:
                remote(early_ref.at[x], early.at[k], x_send.at[update, 0], x_recv.at[update, 0], (x, space)).start()
            if update and place == 1:
                local_pair(v_ref, first, own_pair)
                local_pair(b_ref, second, own_pair)
        rho = jnp.concatenate(
            [
                meas_ref[c, pl.ds(x, 1), :] - s_ref[x, pl.ds(c * nz, 1), :]
                for x in range(rows) for c in range(2)
            ],
            axis=0,
        )
        rho_ref[...] = level_zero * dot3(split(rho), (hy_ref[0], hy_ref[1]))

        if not update:
            local(v_ref, first)
        else:
            local_pair(v_ref, first, 1 - own_pair)
            local_pair(b_ref, second, 1 - own_pair)
            object_share = float(ns) * reduce_end(2)[0:1] / data_total

        def rho_tile(i, part, c, object_share=object_share):
            y = pl.multiple_of(lax.rem(part, halves) * 128, 128)
            return object_share * rho_ref[pl.ds(2 * i + c, 1), pl.ds(y, 128)]

        def add_first(i, part, value, rho_tile=rho_tile):
            return value[0] + rho_tile(i, part, 0), value[1] - rho_tile(i, part, 1)

        def add_second(i, part, value, rho_tile=rho_tile):
            return value[0] + ratio * rho_tile(i, part, 1), value[1] - ratio * rho_tile(i, part, 0)

        sweep_out(t, add_first)
        if not update:
            local(b_ref, second)
        sweep_out(t + 1, add_second)
        middle_out(t)
        middle_out(t + 1)
        middle_back(t)
        middle_back(t + 1)
        sweep_back(t)
        local(first, d_ref)
        sweep_back(t + 1)
        local_pair(second, v_ref, 1 - own_pair)

        def pass_late(row, half, place, device, update=update, late=late):
            remote(late_ref.at[row, half], late.at[place, half], late_send.at[update, place, half],
                   late_took.at[update, place, half], (device, space)).start()

        def add_late(row, half, update=update, late=late):
            take(late.at[0, half], late_took.at[update, 0, half])

            def add(n, carry):
                at = pl.ds(pl.multiple_of(n * 8, 8), 8)
                late_ref[row, half, at, :] = late_ref[row, half, at, :] + late[0, half, at, :]
                return carry

            lax.fori_loop(0, 3 * zgroups, add, 0, unroll=8)

        totals = (zero, zero)
        for k in (2, 1, 3, 0):
            x = lax.rem(src + k, ns)
            if k == 1:
                local_pair(second, v_ref, own_pair)

            def descend(n, totals, x=x, chi_ref=chi_ref):
                z = pl.multiple_of(n * 8, 8)
                res, image, other = pair(r_ref, x, z), pair(d_ref, x, z), pair(v_ref, x, z)
                d = (res[0] + image[0], res[1] - image[1])
                h = (other[0] + ratio * image[1], other[1] + ratio * image[0])
                put(d_ref, x, z, d)
                put(v_ref, x, z, h)
                moved = cmul(pair(chi_ref, x, z), h)
                e, s, w = pair(e_ref, x, z), pair(s_ref, x, z), pair(w_ref, x, z)
                u = (e[0] + s[0], e[1] + s[1])
                late_parts = (
                    d[0] * u[0] + d[1] * u[1] + (w[0] * h[0] + w[1] * h[1]),
                    d[1] * u[0] - d[0] * u[1] + (w[1] * h[0] - w[0] * h[1]),
                    2.0 * (u[0] * h[0] + u[1] * h[1]),
                    d[0] * h[0] + d[1] * h[1],
                    d[1] * h[0] - d[0] * h[1],
                    square(h),
                )
                half = n // (zgroups // 2)
                for c, value in enumerate(late_parts):
                    late_ref[x, half, pl.ds(c * (nz // 2) + z - half * (nz // 2), 8), :] = value
                return totals[0] + square(d), totals[1] + square((d[0] - moved[0], d[1] - moved[1]))

            totals = lax.fori_loop(0, zgroups, descend, totals, unroll=4)
            if k == 2:
                pass_late(across, 0, 0, right)
                pass_late(across, 1, 0, left)
            elif k == 1:
                pass_late(right, 1, 1, right)
            elif k == 3:
                pass_late(left, 0, 2, left)
        finish(t)
        finish(t + 1)
        image_part = jnp.zeros((1, ny), F32)
        for x in range(rows):
            image_part = image_part + square((v_ref[x, pl.ds(0, 1), :], v_ref[x, pl.ds(nz, 1), :]))
        image_fold = image_part[:, :128]
        for h in range(1, halves):
            image_fold = image_fold + image_part[:, h * 128:(h + 1) * 128]
        reduce_start(a, [fold(totals[0]), image_fold, fold(totals[1])])
        take(early.at[pl.ds(1, ns - 1)], x_recv.at[update, 0])

        def gather_early(n, carry, early=early):
            at = pl.ds(pl.multiple_of(n * 8, 8), 8)
            early_ref[src, at, :] = early_ref[src, at, :] + early[1, at, :] + early[2, at, :] + early[3, at, :]
            return carry

        lax.fori_loop(0, 3 * zgroups, gather_early, 0, unroll=4)
        reduce_middle(a)
        add_late(right, 0)
        pass_late(right, 0, 1, right)
        add_late(left, 1)
        pass_late(left, 1, 2, left)
        totals = reduce_end(a)
        length = totals[0:1] / (object_share * totals[1:2] + totals[2:3])

        def advance(x, z, carry, length=length, last=last):
            w, d = pair(w_ref, x, z), pair(d_ref, x, z)
            put(w_ref, x, z, (w[0] + length * d[0], w[1] + length * d[1]))
            if not last:
                s, h = pair(s_ref, x, z), pair(v_ref, x, z)
                put(s_ref, x, z, (s[0] + length * h[0], s[1] + length * h[1]))
            return carry

        each_block(advance, 0)
        if last:
            for x in range(rows):
                for c in range(2):
                    at = pl.ds(c * nz, nz)
                    pltpu.make_async_copy(w_ref.at[x, at, :], w_hbm.at[x, at, :], local_sem.at[4]).start()
        for half in range(2):
            for place in (1, 2):
                take(late.at[place, half], late_took.at[update, place, half])

        def contrast(n, total, length=length, late=late, chi_next=chi_next):
            z = pl.multiple_of(n * 8, 8)
            terms = []
            half = n // (zgroups // 2)
            for c in range(6):
                at = pl.ds(c * (nz // 2) + z - half * (nz // 2), 8)
                terms.append(late_ref[src, half, at, :] + late[1, half, at, :] + late[2, half, at, :])
            parts = [
                early_ref[src, pl.ds(c * nz + z, 8), :] + length * (terms[c] + length * terms[3 + c]) for c in range(3)
            ]
            scale = 1.0 / jnp.maximum(parts[2], FLOOR_SHARE * ns)
            chi = (jnp.clip(parts[0] * scale, REAL_LOW, REAL_HIGH), jnp.clip(parts[1] * scale, 0.0, IMAG_HIGH))
            put(chi_next, src, z, chi)
            return total + square(chi)

        chi_part = lax.fori_loop(0, zgroups, contrast, zero, unroll=2)
        if not last:
            reduce_start(2, [fold(chi_part)])
        for k in (2, 1, 3):
            remote(chi_next.at[src], chi_next.at[src], x_send.at[update, 1], chi_took.at[update, k],
                   (lax.rem(src + k, ns), space)).start()
        if not last:
            reduce_middle(2)
        else:
            for k in (0, 1, 3, 2):
                x = lax.rem(src + k, ns)
                if k:
                    take(chi_next.at[0], chi_took.at[update, ns - k])
                for c in range(2):
                    at = pl.ds(c * nz, nz)
                    pltpu.make_async_copy(chi_next.at[x, at, :], chi_hbm.at[x, at, :], local_sem.at[5]).start()
        take(early.at[pl.ds(1, ns - 1)], x_send.at[update, 0])
        for half in range(2):
            for place in range(3):
                take(late.at[place, half], late_send.at[update, place, half])
        chi_ref = chi_next
    for update in range(OUTER):
        take(chi2_ref.at[pl.ds(0, ns - 1)], x_send.at[update, 1])
    take(w_ref, local_sem.at[4])
    take(chi2_ref, local_sem.at[5])


def unfold(w_ref, chi_ref, w_out, chi_out, sem):
    for n, (src_ref, dst_ref) in enumerate(((w_ref, w_out), (chi_ref, chi_out))):
        rows, nz = src_ref.shape[0], src_ref.shape[1] // 2
        for x in range(rows):
            for c in range(2):
                pltpu.make_async_copy(src_ref.at[x, pl.ds(c * nz, nz), :], dst_ref.at[c, :, x, :], sem.at[n]).start()
    pltpu.make_async_copy(w_ref, w_ref, sem.at[0]).wait()
    pltpu.make_async_copy(chi_ref, chi_ref, sem.at[1]).wait()


def on_device(ns, g1, g2, contrast, measured, positions):
    _, nz, rows, ny = contrast.shape
    cfg = (ns, g1, g2, nz, ny, rows)
    transforms = 1 + 2 * OUTER
    reductions = 2 * OUTER
    tables = decay_tables(nz, ny)
    hy = high_low(hartley(ny))
    hz = high_low(np.kron(np.eye(4), hartley(nz)))
    field = (rows, 2 * nz, ny)
    vmem = pl.BlockSpec(memory_space=pltpu.VMEM)
    anywhere = pl.BlockSpec(memory_space=pltpu.HBM)
    w, chi = pl.pallas_call(
        functools.partial(kernel, cfg),
        out_shape=(jax.ShapeDtypeStruct(field, F32), jax.ShapeDtypeStruct(field, F32)),
        in_specs=[pl.BlockSpec(memory_space=pltpu.SMEM), vmem] + [anywhere] * 4,
        out_specs=(anywhere, anywhere),
        scratch_shapes=[
            pltpu.VMEM(field, F32),
            pltpu.VMEM(tables.shape, F32),
            pltpu.VMEM(hy.shape, BF16),
            pltpu.VMEM(hz.shape, BF16),
        ] + [pltpu.VMEM(field, F32)] * 9 + [
            pltpu.VMEM((2,) + field, F32),
            pltpu.VMEM((2 * rows, ny), F32),
            pltpu.VMEM((rows, 3 * nz, ny), F32),
            pltpu.VMEM((OUTER, ns, 3 * nz, ny), F32),
            pltpu.VMEM((rows, 2, 3 * nz, ny), F32),
            pltpu.VMEM((OUTER, 3, 2, 3 * nz, ny), F32),
            pltpu.VMEM((2, g1 // 2, 4, 8, 128), F32),
            pltpu.VMEM((2, g1 // 2, 4, 8, 128), F32),
            pltpu.VMEM((2, g1 // 2, 4, 8, 128), F32),
            pltpu.VMEM((2, 2, g1 // 2, 4, 8, 128), F32),
            pltpu.VMEM((transforms, 2, g1 // 2, 4, 8, 128), F32),
            pltpu.VMEM((transforms, g1 // 2, 4, 8, 128), F32),
            pltpu.VMEM((transforms, g2, 4, 8, 128), F32),
            pltpu.VMEM((transforms, g1 // 2, 4, 8, 128), F32),
            pltpu.VMEM((transforms, g1 // 2, 4, 8, 128), F32),
            pltpu.VMEM((reductions, g1 * g2 // 4, 8, 128), F32),
            pltpu.VMEM((reductions, 4 * ns, 8, 128), F32),
            pltpu.SemaphoreType.DMA((transforms, 5)),
            pltpu.SemaphoreType.DMA((transforms, 5)),
            pltpu.SemaphoreType.DMA((reductions, 2)),
            pltpu.SemaphoreType.DMA((reductions, 2)),
            pltpu.SemaphoreType.DMA((OUTER, 2)),
            pltpu.SemaphoreType.DMA((OUTER, 2)),
            pltpu.SemaphoreType.DMA((OUTER, 3, 2)),
            pltpu.SemaphoreType.DMA((OUTER, 3, 2)),
            pltpu.SemaphoreType.DMA((OUTER, ns)),
            pltpu.SemaphoreType.DMA((6,)),
        ],
        compiler_params=pltpu.CompilerParams(
            collective_id=0, has_side_effects=True, vmem_limit_bytes=56 * 1024 * 1024
        ),
    )(positions, measured[0], contrast, tables, hy, hz)
    w, chi = pl.pallas_call(
        unfold,
        out_shape=(jax.ShapeDtypeStruct(contrast.shape, F32), jax.ShapeDtypeStruct(contrast.shape, F32)),
        in_specs=[anywhere, anywhere],
        out_specs=(anywhere, anywhere),
        scratch_shapes=[pltpu.SemaphoreType.DMA((2,))],
    )(w, chi)
    return w[None], chi


def solution(mesh, g2=4):
    placed = (P(None, None, "space", None), P("src", None, "space", None), P("src", None))
    return jax.shard_map(
        functools.partial(on_device, mesh.shape["src"], mesh.shape["space"] // g2, g2),
        mesh=mesh,
        in_specs=placed,
        out_specs=(P("src", None, None, "space", None), P(None, None, "space", None)),
        check_vma=False,
    )
```

```python
import functools
import math

import jax
import jax.numpy as jnp
import ml_dtypes
import numpy as np
from jax import lax
from jax.experimental import pallas as pl
from jax.experimental.pallas import tpu as pltpu
from jax.sharding import PartitionSpec as P

OUTER = 2
WAVENUMBER = 2.0 * math.pi / 6.0
DAMPING = 0.3
SOURCE_GAP = 8.0
FLOOR_SHARE = 0.75
REAL_LOW = -0.25
REAL_HIGH = 0.35
IMAG_HIGH = 0.1
F32 = jnp.float32
BF16 = jnp.bfloat16
MESH = pl.DeviceIdType.MESH


def hartley(length):
    turn = np.outer(np.arange(length), np.arange(length)) % length
    angle = 2.0 * np.pi / length * turn
    return (np.cos(angle) + np.sin(angle)) / np.sqrt(length)


def high_low(table):
    high = table.astype(ml_dtypes.bfloat16)
    low = (table - high.astype(np.float64)).astype(ml_dtypes.bfloat16)
    return np.stack([high, low])


def modes(length):
    return 4.0 * np.sin(np.pi * np.arange(length) / length) ** 2


def decay_tables(depth, across):
    wave_sq = WAVENUMBER * WAVENUMBER
    trace = 2.0 + modes(depth)[:, None] + modes(across)[None, :] - wave_sq * (1.0 + 1j * DAMPING)
    root = np.sqrt(trace * trace - 4.0)
    first = (trace - root) / 2.0
    second = (trace + root) / 2.0
    small = np.where(np.abs(first) < np.abs(second), first, second)
    large = np.where(np.abs(first) < np.abs(second), second, first)
    small = 1.0 / large
    kappa = wave_sq / (large - small)
    tables = np.stack([small.real, small.imag, kappa.real, kappa.imag])
    return tables.astype(np.float32)


def cmul(a, b):
    return (a[0] * b[0] - a[1] * b[1], a[0] * b[1] + a[1] * b[0])


def cmadd(a, b, c):
    return (a[0] * b[0] - a[1] * b[1] + c[0], a[0] * b[1] + a[1] * b[0] + c[1])


def half_turn(fraction):
    angle = fraction * math.pi
    sq = angle * angle
    sine = jnp.full_like(sq, -1.0 / math.factorial(11))
    for order in (9, 7, 5, 3, 1):
        sine = sine * sq + (1.0 if order % 4 == 1 else -1.0) / math.factorial(order)
    cosine = jnp.full_like(sq, 1.0 / math.factorial(12))
    for order in (10, 8, 6, 4, 2, 0):
        cosine = cosine * sq + (1.0 if order % 4 == 0 else -1.0) / math.factorial(order)
    return sine * angle, cosine


def kernel(
    cfg,
    pos_ref, meas_ref, contrast_hbm, tab_hbm, hy_hbm, hz_hbm,
    w_hbm, chi_hbm,
    chi0_ref, tab_ref, hy_ref, hz_ref, w_ref, chi2_ref, chi1_ref, e_ref, s_ref, r_ref, d_ref, v_ref, b_ref, sp_all, rho_ref, early_ref, early_recv, late_ref, late_recv,
    send0_all, send1_all, send3_all, states_all, sums, recv1, recv2, recv3, recv4, red1, red2,
    ex_send, ex_recv, red_send, red_recv, x_send, x_recv, late_send, late_took, chi_took, local_sem,
):
    ns, g1, g2, nz, ny, rows = cfg
    halves = ny // 128
    nx = g1 * g2 * rows
    zgroups = nz // 8
    src = lax.axis_index("src")
    space = lax.axis_index("space")
    m = lax.rem(space, g1)
    chips = g1 // 2
    core = lax.rem(m, 2)
    chip = m // 2
    far_first = (6, 2, 5, 3, 7, 1, 4)
    grp = space // g1
    base = grp * g1

    partner = (src, space + 1 - 2 * core)

    for x in range(rows):
        for c in range(2):
            pltpu.make_async_copy(
                contrast_hbm.at[c, :, x, :], chi0_ref.at[x, pl.ds(c * nz, nz), :], local_sem.at[0]
            ).start()
    pltpu.make_async_copy(hz_hbm, hz_ref, local_sem.at[1]).start()
    pltpu.make_async_copy(hy_hbm, hy_ref, local_sem.at[2]).start()
    pltpu.make_async_copy(tab_hbm, tab_ref, local_sem.at[3]).start()

    barrier = pltpu.get_barrier_semaphore()

    zs = g1 * g2 // 8
    z_at, y_at = space // 8, lax.rem(space // 2, 4)

    def column_peer(k):
        return src, (lax.rem(z_at + k // 2, zs) * 4 + y_at) * 2 + lax.rem(core + k, 2)

    def plane_peer(k):
        return lax.rem(src + k // 4, ns), (z_at * 4 + lax.rem(y_at + k, 4)) * 2 + core

    def greet_column(k, carry):
        pl.semaphore_signal(barrier, inc=1, device_id=column_peer(k), device_id_type=MESH)
        return carry

    def greet_plane(k, carry):
        pl.semaphore_signal(barrier, inc=1, device_id=plane_peer(k), device_id_type=MESH)
        return carry

    def greet_diagonal(k, carry):
        z_other = z_at + 1 - 2 * lax.rem(z_at, 2)
        pl.semaphore_signal(barrier, inc=1, device_id=(src, (z_other * 4 + lax.rem(y_at + k, 4)) * 2 + core),
                            device_id_type=MESH)
        return carry

    lax.fori_loop(1, 2 * zs, greet_column, 0)
    lax.fori_loop(1, 4 * ns, greet_plane, 0)
    lax.fori_loop(1, 4, greet_diagonal, 0)

    def remote(src_ref, dst_ref, send_sem, recv_sem, device):
        return pltpu.make_async_remote_copy(
            src_ref=src_ref, dst_ref=dst_ref, send_sem=send_sem, recv_sem=recv_sem,
            device_id=device, device_id_type=MESH,
        )

    def take(ref, sem):
        pltpu.make_async_copy(ref, ref, sem).wait()

    def reduce_start(a, parts):
        red1[a, 0] = jnp.concatenate(parts + [jnp.zeros((8 - len(parts), 128), F32)], axis=0)

        def send(n, carry):
            k = lax.rem(n + zs - 2, 2 * zs - 1) + 1
            remote(red1.at[a, 0], red1.at[a, k], red_send.at[a, 0], red_recv.at[a, 0], column_peer(k)).start()
            return carry

        lax.fori_loop(1, 2 * zs, send, 0)

    def reduce_middle(a):
        take(red1.at[a, pl.ds(1, 2 * zs - 1)], red_recv.at[a, 0])

        def add(j, total):
            slot = lax.rem(z_at - j // 2 + zs, zs) * 2 + lax.rem(core + j, 2)
            return total + red1[a, slot]

        red2[a, 0] = lax.fori_loop(0, 2 * zs, add, jnp.zeros((8, 128), F32), unroll=True)

        def send(n, carry):
            k = lax.rem(n + 2 * ns, 4 * ns - 1) + 1
            remote(red2.at[a, 0], red2.at[a, k], red_send.at[a, 1], red_recv.at[a, 1], plane_peer(k)).start()
            return carry

        lax.fori_loop(1, 4 * ns, send, 0)
        take(red1.at[a, pl.ds(1, 2 * zs - 1)], red_send.at[a, 0])

    def reduce_end(a):
        take(red2.at[a, pl.ds(1, 4 * ns - 1)], red_recv.at[a, 1])

        def add(j, total):
            slot = lax.rem(src - j // 4 + ns, ns) * 4 + lax.rem(y_at - lax.rem(j, 4) + 4, 4)
            return total + red2[a, slot]

        total = lax.fori_loop(0, 4 * ns, add, jnp.zeros((8, 128), F32), unroll=True)
        take(red2.at[a, pl.ds(1, 4 * ns - 1)], red_send.at[a, 1])
        return jnp.sum(total, axis=1, keepdims=True)

    def fold(acc):
        part = acc[:, :128]
        for h in range(1, halves):
            part = part + acc[:, h * 128:(h + 1) * 128]
        return jnp.sum(part, axis=0, keepdims=True)

    def split(a):
        high = a.astype(BF16)
        return high, (a - high.astype(F32)).astype(BF16)

    def dot3(a, b):
        mm = functools.partial(jnp.dot, preferred_element_type=F32)
        return mm(a[0], b[0]) + (mm(a[1], b[0]) + mm(a[0], b[1]))

    def local_pair(src_ref, dst_ref, n):
        at = pl.ds(2 * n, 2)
        depth_done = dot3((hz_ref[0], hz_ref[1]), split(src_ref[at].reshape(4 * nz, ny)))
        dst_ref[at] = dot3(split(depth_done), (hy_ref[0], hy_ref[1])).reshape(2, 2 * nz, ny)

    def local(src_ref, dst_ref):
        for n in range(rows // 2):
            local_pair(src_ref, dst_ref, n)

    def tile(ref, lead, part, comp):
        z = pl.multiple_of(part // halves * 8, 8)
        y = pl.multiple_of(lax.rem(part, halves) * 128, 128)
        return ref.at[lead, pl.ds(comp * nz + z, 8), pl.ds(y, 128)]

    def ctable(part, which):
        z = pl.multiple_of(part // halves * 8, 8)
        y = pl.multiple_of(lax.rem(part, halves) * 128, 128)
        return tuple(tab_ref[2 * which + c, pl.ds(z, 8), pl.ds(y, 128)] for c in range(2))

    def spectral(sp_ref, lead, part):
        return (tile(sp_ref, lead, part, 0)[...], tile(sp_ref, lead, part, 1)[...])

    def sweep_out(t, extra=None):
        sp_ref, send0, send1 = sp_all.at[t % 2], send0_all.at[t % 2], send1_all.at[t % 2]

        def summarise(part):
            root = ctable(part, 0)
            rowv = [spectral(sp_ref, i, part) for i in range(rows)]
            if extra is not None:
                rowv = [extra(i, part, value) for i, value in enumerate(rowv)]
                for i in range(rows):
                    tile(sp_ref, i, part, 0)[...] = rowv[i][0]
                    tile(sp_ref, i, part, 1)[...] = rowv[i][1]
            ahead = rowv[0]
            for i in range(1, rows):
                ahead = cmadd(ahead, root, rowv[i])
            behind = rowv[rows - 1]
            for i in range(rows - 2, -1, -1):
                behind = cmadd(behind, root, rowv[i])
            return ahead + behind

        def other_half(k, carry):
            g = lax.rem(chip + k, chips)
            vals = summarise(2 * g + 1 - core)
            for c in range(4):
                send0[g, c] = vals[c]
            remote(send0.at[g], sums.at[t, core, g], ex_send.at[t, 0], ex_recv.at[t, 0], partner).start()
            return carry

        def own_half(k, carry):
            g = lax.rem(chip + k, chips)
            vals = summarise(2 * g + core)
            for c in range(4):
                sums[t, core, g, c] = vals[c]
            return carry

        lax.fori_loop(1, chips + 1, other_half, 0, unroll=2)
        lax.fori_loop(1, chips + 1, own_half, 0, unroll=2)
        take(sums.at[t, 1 - core], ex_recv.at[t, 0])

        def combine(g):
            block_root = power(ctable(2 * g + core, 0), int(math.log2(rows)))
            first = [sums[t, 0, g, c] for c in range(4)]
            second = [sums[t, 1, g, c] for c in range(4)]
            return cmadd(first[:2], block_root, second[:2]) + cmadd(second[2:], block_root, first[2:])

        def step(k, carry):
            g = lax.rem(chip + k, chips)
            vals = combine(g)
            for c in range(4):
                send1[g, c] = vals[c]
            remote(send1.at[g], recv1.at[t, k], ex_send.at[t, 1], ex_recv.at[t, 1],
                   (src, base + 2 * g + core)).start()
            return carry

        for k in far_first:
            step(k, 0)
        vals = combine(chip)
        for c in range(4):
            recv1[t, 0, c] = vals[c]

    def power(value, doublings):
        for _ in range(doublings):
            value = cmul(value, value)
        return value

    def own_root():
        return ctable(m, 0)

    def chip_root():
        return power(own_root(), int(math.log2(2 * rows)))

    def middle_out(t):
        take(recv1.at[t, pl.ds(1, chips - 1)], ex_recv.at[t, 1])
        root = chip_root()

        def gather(j, carry):
            ahead, behind = carry
            slot_a = lax.rem(chip - j + chips, chips)
            slot_b = lax.rem(chip + 1 + j, chips)
            ahead = cmadd(ahead, root, (recv1[t, slot_a, 0], recv1[t, slot_a, 1]))
            behind = cmadd(behind, root, (recv1[t, slot_b, 2], recv1[t, slot_b, 3]))
            return ahead, behind

        zero = jnp.zeros((8, 128), F32)
        ahead, behind = lax.fori_loop(0, chips, gather, ((zero, zero), (zero, zero)), unroll=True)
        for c, value in enumerate(ahead + behind):
            recv2[t, 0, c] = value

        def send(k, carry):
            peer = lax.rem(grp + k, g2) * g1 + m
            remote(recv2.at[t, 0], recv2.at[t, k], ex_send.at[t, 2], ex_recv.at[t, 2], (src, peer)).start()
            return carry

        for k in (2, 1, 3):
            send(k, 0)

    def middle_back(t):
        send3 = send3_all.at[t % 2]
        root = chip_root()
        group_root = power(root, int(math.log2(chips)))
        turn = power(group_root, int(math.log2(g2)))
        real, imag = 1.0 - turn[0], turn[1]
        norm = 1.0 / (real * real + imag * imag)
        inverse = (real * norm, imag * norm)
        take(recv2.at[t, pl.ds(1, g2 - 1)], ex_recv.at[t, 2])
        left = (recv2[t, 0, 0], recv2[t, 0, 1])
        right = (recv2[t, 0, 2], recv2[t, 0, 3])
        for k in range(g2 - 1, 0, -1):
            left = cmadd(left, group_root, (recv2[t, k, 0], recv2[t, k, 1]))
            right = cmadd(right, group_root, (recv2[t, g2 - k, 2], recv2[t, g2 - k, 3]))
        left = cmul(left, inverse)
        right = cmul(right, inverse)

        def spread(j, carry):
            left, right = carry
            back = chips - 1 - j
            for c in range(2):
                send3[j, c] = left[c]
                send3[back, 2 + c] = right[c]
            slot_a = lax.rem(chip - j + chips, chips)
            slot_b = lax.rem(chip + 1 + j, chips)
            left = cmadd(left, root, (recv1[t, slot_a, 0], recv1[t, slot_a, 1]))
            right = cmadd(right, root, (recv1[t, slot_b, 2], recv1[t, slot_b, 3]))
            return left, right

        lax.fori_loop(0, chips, spread, (left, right), unroll=True)

        def send(k, carry):
            g = lax.rem(chip + k, chips)
            remote(send3.at[g], recv3.at[t, k], ex_send.at[t, 3], ex_recv.at[t, 3],
                   (src, base + 2 * g + core)).start()
            return carry

        for k in far_first:
            send(k, 0)
        for c in range(4):
            recv3[t, 0, c] = send3[chip, c]

    def sweep_back(t):
        sp_ref, states = sp_all.at[t % 2], states_all.at[t % 2]
        take(recv3.at[t, pl.ds(1, chips - 1)], ex_recv.at[t, 3])

        def pass_on(k, carry):
            g = lax.rem(chip - k + chips, chips)
            block_root = power(ctable(2 * g + core, 0), int(math.log2(rows)))
            left = (recv3[t, k, 0], recv3[t, k, 1])
            right = (recv3[t, k, 2], recv3[t, k, 3])
            inner_left = cmadd(left, block_root, (sums[t, 0, g, 0], sums[t, 0, g, 1]))
            inner_right = cmadd(right, block_root, (sums[t, 1, g, 2], sums[t, 1, g, 3]))
            for c in range(2):
                states[0, g, c] = left[c]
                states[0, g, 2 + c] = inner_right[c]
                states[1, g, c] = inner_left[c]
                states[1, g, 2 + c] = right[c]
            remote(states.at[1 - core, g], recv4.at[t, g], ex_send.at[t, 4], ex_recv.at[t, 4], partner).start()
            return carry

        lax.fori_loop(0, chips, pass_on, 0, unroll=2)

        def apply(part, ends):
            root = ctable(part, 0)
            kappa = ctable(part, 1)
            rowv = [spectral(sp_ref, i, part) for i in range(rows)]
            state = ends[:2]
            ahead = []
            for i in range(rows):
                state = cmadd(state, root, rowv[i])
                ahead.append(state)
            state = cmul(ends[2:], root)
            for i in range(rows - 1, -1, -1):
                total = cmul((ahead[i][0] + state[0], ahead[i][1] + state[1]), kappa)
                tile(sp_ref, i, part, 0)[...] = total[0]
                tile(sp_ref, i, part, 1)[...] = total[1]
                if i:
                    state = cmul((state[0] + rowv[i][0], state[1] + rowv[i][1]), root)

        def own_half(g, carry):
            apply(2 * g + core, tuple(states[core, g, c] for c in range(4)))
            return carry

        def other_half(g, carry):
            apply(2 * g + 1 - core, tuple(recv4[t, g, c] for c in range(4)))
            return carry

        lax.fori_loop(0, chips, own_half, 0, unroll=2)
        take(recv4.at[t], ex_recv.at[t, 4])
        lax.fori_loop(0, chips, other_half, 0, unroll=2)

    def finish(t):
        take(recv4.at[t], ex_send.at[t, 0])
        take(recv1.at[t, pl.ds(1, chips - 1)], ex_send.at[t, 1])
        take(recv2.at[t, pl.ds(1, g2 - 1)], ex_send.at[t, 2])
        take(recv3.at[t, pl.ds(1, chips - 1)], ex_send.at[t, 3])
        take(recv4.at[t], ex_send.at[t, 4])

    def pair(ref, x, z):
        return (ref[x, pl.ds(z, 8), :], ref[x, pl.ds(nz + z, 8), :])

    def put(ref, x, z, value):
        ref[x, pl.ds(z, 8), :] = value[0]
        ref[x, pl.ds(nz + z, 8), :] = value[1]

    def each_block(body, init):
        def outer(n, carry):
            return body(n // zgroups, pl.multiple_of(lax.rem(n, zgroups) * 8, 8), carry)

        return lax.fori_loop(0, rows * zgroups, outer, init, unroll=4)

    def square(value):
        return value[0] * value[0] + value[1] * value[1]

    zero = jnp.zeros((8, ny), F32)
    source_x = pos_ref[0, 0].astype(F32)
    source_y = pos_ref[0, 1].astype(F32)
    offset_y = lax.broadcasted_iota(jnp.int32, (8, ny), 1).astype(F32) - source_y
    offset_y_sq = offset_y * offset_y
    level = lax.broadcasted_iota(jnp.int32, (8, ny), 0).astype(F32) + SOURCE_GAP

    def begin(x, z, carry):
        height = level + z.astype(F32)
        offset_x = (space * rows + x).astype(F32) - source_x
        dist = jnp.sqrt(height * height + offset_x * offset_x + offset_y_sq)
        turns = dist * (1.0 / 6.0)
        sine, cosine = half_turn(turns - jnp.floor(turns + 0.5))
        wave = (1.0 - 2.0 * sine * sine, 2.0 * sine * cosine)
        put(e_ref, x, z, wave)
        return carry

    def excite(x, z, total):
        field = cmul(pair(chi0_ref, x, z), pair(e_ref, x, z))
        put(w_ref, x, z, field)
        return total + square(field)

    each_block(begin, 0)
    take(chi0_ref, local_sem.at[0])
    object_part = each_block(excite, zero)
    data_part = jnp.zeros((1, ny), F32)
    for x in range(rows):
        for c in range(2):
            data_part = data_part + meas_ref[c, pl.ds(x, 1), :] * meas_ref[c, pl.ds(x, 1), :]
    data_fold = data_part[:, :128]
    for h in range(1, halves):
        data_fold = data_fold + data_part[:, h * 128:(h + 1) * 128]

    take(hz_ref, local_sem.at[1])
    take(hy_ref, local_sem.at[2])
    local(w_ref, sp_all.at[0])
    take(tab_ref, local_sem.at[3])
    pl.semaphore_wait(barrier, (2 * zs - 1) + (4 * ns - 1) + 3)
    sweep_out(0)
    reduce_start(0, [data_fold, fold(object_part)])
    middle_out(0)
    reduce_middle(0)
    middle_back(0)
    totals = reduce_end(0)
    sweep_back(0)
    finish(0)
    local(sp_all.at[0], s_ref)
    data_total = totals[0:1]
    object_share = totals[1:2] / data_total
    ratio = 0.5 / DAMPING
    level_zero = 1.0 / math.sqrt(nz)
    chi_ref = chi0_ref
    for update in range(OUTER):
        t = 1 + 2 * update
        a = 1 + 2 * update
        last = update == OUTER - 1
        chi_next = chi2_ref if last else chi1_ref
        early, late = early_recv.at[update], late_recv.at[update]
        right, left, across = (lax.rem(src + k, ns) for k in (1, 3, 2))

        own_pair = src // 2
        mate = src + 1 - 2 * lax.rem(src, 2)
        first, second = sp_all.at[t % 2], sp_all.at[(t + 1) % 2]
        for place, x in enumerate((src, mate, lax.rem(mate + 2, ns), across)):
            k = lax.rem(x - src + ns, ns)
            if update and place:
                take(chi_ref.at[0], chi_took.at[update - 1, ns - k])

            def residual(n, carry, x=x, chi_ref=chi_ref):
                z = pl.multiple_of(n * 8, 8)
                chi = pair(chi_ref, x, z)
                e, s, w = pair(e_ref, x, z), pair(s_ref, x, z), pair(w_ref, x, z)
                u = (e[0] + s[0], e[1] + s[1])
                field = cmul(chi, u)
                res = (field[0] - w[0], field[1] - w[1])
                put(r_ref, x, z, res)
                flipped = cmul(chi, (res[0], -res[1]))
                put(v_ref, x, z, (-flipped[0], -flipped[1]))
                put(b_ref, x, z, (res[0] + ratio * flipped[1], res[1] + ratio * flipped[0]))
                early_ref[x, pl.ds(z, 8), :] = w[0] * u[0] + w[1] * u[1]
                early_ref[x, pl.ds(nz + z, 8), :] = w[1] * u[0] - w[0] * u[1]
                early_ref[x, pl.ds(2 * nz + z, 8), :] = square(u)
                return carry

            lax.fori_loop(0, zgroups, residual, 0, unroll=4)
            if place:
                remote(early_ref.at[x], early.at[k], x_send.at[update, 0], x_recv.at[update, 0], (x, space)).start()
            if update and place == 1:
                local_pair(v_ref, first, own_pair)
                local_pair(b_ref, second, own_pair)
        rho = jnp.concatenate(
            [
                meas_ref[c, pl.ds(x, 1), :] - s_ref[x, pl.ds(c * nz, 1), :]
                for x in range(rows) for c in range(2)
            ],
            axis=0,
        )
        rho_ref[...] = level_zero * dot3(split(rho), (hy_ref[0], hy_ref[1]))

        if not update:
            local(v_ref, first)
        else:
            local_pair(v_ref, first, 1 - own_pair)
            local_pair(b_ref, second, 1 - own_pair)
            object_share = float(ns) * reduce_end(2)[0:1] / data_total

        def rho_tile(i, part, c, object_share=object_share):
            y = pl.multiple_of(lax.rem(part, halves) * 128, 128)
            return object_share * rho_ref[pl.ds(2 * i + c, 1), pl.ds(y, 128)]

        def add_first(i, part, value, rho_tile=rho_tile):
            return value[0] + rho_tile(i, part, 0), value[1] - rho_tile(i, part, 1)

        def add_second(i, part, value, rho_tile=rho_tile):
            return value[0] + ratio * rho_tile(i, part, 1), value[1] - ratio * rho_tile(i, part, 0)

        sweep_out(t, add_first)
        if not update:
            local(b_ref, second)
        sweep_out(t + 1, add_second)
        middle_out(t)
        middle_out(t + 1)
        middle_back(t)
        middle_back(t + 1)
        sweep_back(t)
        local(first, d_ref)
        sweep_back(t + 1)
        local_pair(second, v_ref, 1 - own_pair)

        def pass_late(row, half, place, device, update=update, late=late):
            remote(late_ref.at[row, half], late.at[place, half], late_send.at[update, place, half],
                   late_took.at[update, place, half], (device, space)).start()

        def add_late(row, half, update=update, late=late):
            take(late.at[0, half], late_took.at[update, 0, half])

            def add(n, carry):
                at = pl.ds(pl.multiple_of(n * 8, 8), 8)
                late_ref[row, half, at, :] = late_ref[row, half, at, :] + late[0, half, at, :]
                return carry

            lax.fori_loop(0, 3 * zgroups, add, 0, unroll=8)

        totals = (zero, zero)
        for k in (2, 1, 3, 0):
            x = lax.rem(src + k, ns)
            if k == 1:
                local_pair(second, v_ref, own_pair)

            def descend(n, totals, x=x, chi_ref=chi_ref):
                z = pl.multiple_of(n * 8, 8)
                res, image, other = pair(r_ref, x, z), pair(d_ref, x, z), pair(v_ref, x, z)
                d = (res[0] + image[0], res[1] - image[1])
                h = (other[0] + ratio * image[1], other[1] + ratio * image[0])
                put(d_ref, x, z, d)
                put(v_ref, x, z, h)
                moved = cmul(pair(chi_ref, x, z), h)
                e, s, w = pair(e_ref, x, z), pair(s_ref, x, z), pair(w_ref, x, z)
                u = (e[0] + s[0], e[1] + s[1])
                late_parts = (
                    d[0] * u[0] + d[1] * u[1] + (w[0] * h[0] + w[1] * h[1]),
                    d[1] * u[0] - d[0] * u[1] + (w[1] * h[0] - w[0] * h[1]),
                    2.0 * (u[0] * h[0] + u[1] * h[1]),
                    d[0] * h[0] + d[1] * h[1],
                    d[1] * h[0] - d[0] * h[1],
                    square(h),
                )
                half = n // (zgroups // 2)
                for c, value in enumerate(late_parts):
                    late_ref[x, half, pl.ds(c * (nz // 2) + z - half * (nz // 2), 8), :] = value
                return totals[0] + square(d), totals[1] + square((d[0] - moved[0], d[1] - moved[1]))

            totals = lax.fori_loop(0, zgroups, descend, totals, unroll=4)
            if k == 2:
                pass_late(across, 0, 0, right)
                pass_late(across, 1, 0, left)
            elif k == 1:
                pass_late(right, 1, 1, right)
            elif k == 3:
                pass_late(left, 0, 2, left)
        finish(t)
        finish(t + 1)
        image_part = jnp.zeros((1, ny), F32)
        for x in range(rows):
            image_part = image_part + square((v_ref[x, pl.ds(0, 1), :], v_ref[x, pl.ds(nz, 1), :]))
        image_fold = image_part[:, :128]
        for h in range(1, halves):
            image_fold = image_fold + image_part[:, h * 128:(h + 1) * 128]
        reduce_start(a, [fold(totals[0]), image_fold, fold(totals[1])])
        take(early.at[pl.ds(1, ns - 1)], x_recv.at[update, 0])

        def gather_early(n, carry, early=early):
            at = pl.ds(pl.multiple_of(n * 8, 8), 8)
            early_ref[src, at, :] = early_ref[src, at, :] + early[1, at, :] + early[2, at, :] + early[3, at, :]
            return carry

        lax.fori_loop(0, 3 * zgroups, gather_early, 0, unroll=4)
        reduce_middle(a)
        add_late(right, 0)
        pass_late(right, 0, 1, right)
        add_late(left, 1)
        pass_late(left, 1, 2, left)
        totals = reduce_end(a)
        length = totals[0:1] / (object_share * totals[1:2] + totals[2:3])

        def advance(x, z, carry, length=length, last=last):
            w, d = pair(w_ref, x, z), pair(d_ref, x, z)
            put(w_ref, x, z, (w[0] + length * d[0], w[1] + length * d[1]))
            if not last:
                s, h = pair(s_ref, x, z), pair(v_ref, x, z)
                put(s_ref, x, z, (s[0] + length * h[0], s[1] + length * h[1]))
            return carry

        each_block(advance, 0)
        if last:
            for x in range(rows):
                for c in range(2):
                    at = pl.ds(c * nz, nz)
                    pltpu.make_async_copy(w_ref.at[x, at, :], w_hbm.at[x, at, :], local_sem.at[4]).start()
        for half in range(2):
            for place in (1, 2):
                take(late.at[place, half], late_took.at[update, place, half])

        def contrast(n, total, length=length, late=late, chi_next=chi_next):
            z = pl.multiple_of(n * 8, 8)
            terms = []
            half = n // (zgroups // 2)
            for c in range(6):
                at = pl.ds(c * (nz // 2) + z - half * (nz // 2), 8)
                terms.append(late_ref[src, half, at, :] + late[1, half, at, :] + late[2, half, at, :])
            parts = [
                early_ref[src, pl.ds(c * nz + z, 8), :] + length * (terms[c] + length * terms[3 + c]) for c in range(3)
            ]
            scale = 1.0 / jnp.maximum(parts[2], FLOOR_SHARE * ns)
            chi = (jnp.clip(parts[0] * scale, REAL_LOW, REAL_HIGH), jnp.clip(parts[1] * scale, 0.0, IMAG_HIGH))
            put(chi_next, src, z, chi)
            return total + square(chi)

        chi_part = lax.fori_loop(0, zgroups, contrast, zero, unroll=2)
        if not last:
            reduce_start(2, [fold(chi_part)])
        for k in (2, 1, 3):
            remote(chi_next.at[src], chi_next.at[src], x_send.at[update, 1], chi_took.at[update, k],
                   (lax.rem(src + k, ns), space)).start()
        if not last:
            reduce_middle(2)
        else:
            for k in (0, 1, 3, 2):
                x = lax.rem(src + k, ns)
                if k:
                    take(chi_next.at[0], chi_took.at[update, ns - k])
                for c in range(2):
                    at = pl.ds(c * nz, nz)
                    pltpu.make_async_copy(chi_next.at[x, at, :], chi_hbm.at[x, at, :], local_sem.at[5]).start()
        take(early.at[pl.ds(1, ns - 1)], x_send.at[update, 0])
        for half in range(2):
            for place in range(3):
                take(late.at[place, half], late_send.at[update, place, half])
        chi_ref = chi_next
    for update in range(OUTER):
        take(chi2_ref.at[pl.ds(0, ns - 1)], x_send.at[update, 1])
    take(w_ref, local_sem.at[4])
    take(chi2_ref, local_sem.at[5])


def unfold(w_ref, chi_ref, w_out, chi_out, sem):
    for n, (src_ref, dst_ref) in enumerate(((w_ref, w_out), (chi_ref, chi_out))):
        rows, nz = src_ref.shape[0], src_ref.shape[1] // 2
        for x in range(rows):
            for c in range(2):
                pltpu.make_async_copy(src_ref.at[x, pl.ds(c * nz, nz), :], dst_ref.at[c, :, x, :], sem.at[n]).start()
    pltpu.make_async_copy(w_ref, w_ref, sem.at[0]).wait()
    pltpu.make_async_copy(chi_ref, chi_ref, sem.at[1]).wait()


def on_device(ns, g1, g2, contrast, measured, positions):
    _, nz, rows, ny = contrast.shape
    cfg = (ns, g1, g2, nz, ny, rows)
    transforms = 1 + 2 * OUTER
    reductions = 2 * OUTER
    tables = decay_tables(nz, ny)
    hy = high_low(hartley(ny))
    hz = high_low(np.kron(np.eye(4), hartley(nz)))
    field = (rows, 2 * nz, ny)
    vmem = pl.BlockSpec(memory_space=pltpu.VMEM)
    anywhere = pl.BlockSpec(memory_space=pltpu.HBM)
    w, chi = pl.pallas_call(
        functools.partial(kernel, cfg),
        out_shape=(jax.ShapeDtypeStruct(field, F32), jax.ShapeDtypeStruct(field, F32)),
        in_specs=[pl.BlockSpec(memory_space=pltpu.SMEM), vmem] + [anywhere] * 4,
        out_specs=(anywhere, anywhere),
        scratch_shapes=[
            pltpu.VMEM(field, F32),
            pltpu.VMEM(tables.shape, F32),
            pltpu.VMEM(hy.shape, BF16),
            pltpu.VMEM(hz.shape, BF16),
        ] + [pltpu.VMEM(field, F32)] * 9 + [
            pltpu.VMEM((2,) + field, F32),
            pltpu.VMEM((2 * rows, ny), F32),
            pltpu.VMEM((rows, 3 * nz, ny), F32),
            pltpu.VMEM((OUTER, ns, 3 * nz, ny), F32),
            pltpu.VMEM((rows, 2, 3 * nz, ny), F32),
            pltpu.VMEM((OUTER, 3, 2, 3 * nz, ny), F32),
            pltpu.VMEM((2, g1 // 2, 4, 8, 128), F32),
            pltpu.VMEM((2, g1 // 2, 4, 8, 128), F32),
            pltpu.VMEM((2, g1 // 2, 4, 8, 128), F32),
            pltpu.VMEM((2, 2, g1 // 2, 4, 8, 128), F32),
            pltpu.VMEM((transforms, 2, g1 // 2, 4, 8, 128), F32),
            pltpu.VMEM((transforms, g1 // 2, 4, 8, 128), F32),
            pltpu.VMEM((transforms, g2, 4, 8, 128), F32),
            pltpu.VMEM((transforms, g1 // 2, 4, 8, 128), F32),
            pltpu.VMEM((transforms, g1 // 2, 4, 8, 128), F32),
            pltpu.VMEM((reductions, g1 * g2 // 4, 8, 128), F32),
            pltpu.VMEM((reductions, 4 * ns, 8, 128), F32),
            pltpu.SemaphoreType.DMA((transforms, 5)),
            pltpu.SemaphoreType.DMA((transforms, 5)),
            pltpu.SemaphoreType.DMA((reductions, 2)),
            pltpu.SemaphoreType.DMA((reductions, 2)),
            pltpu.SemaphoreType.DMA((OUTER, 2)),
            pltpu.SemaphoreType.DMA((OUTER, 2)),
            pltpu.SemaphoreType.DMA((OUTER, 3, 2)),
            pltpu.SemaphoreType.DMA((OUTER, 3, 2)),
            pltpu.SemaphoreType.DMA((OUTER, ns)),
            pltpu.SemaphoreType.DMA((6,)),
        ],
        compiler_params=pltpu.CompilerParams(
            collective_id=0, has_side_effects=True, vmem_limit_bytes=56 * 1024 * 1024
        ),
    )(positions, measured[0], contrast, tables, hy, hz)
    w, chi = pl.pallas_call(
        unfold,
        out_shape=(jax.ShapeDtypeStruct(contrast.shape, F32), jax.ShapeDtypeStruct(contrast.shape, F32)),
        in_specs=[vmem, vmem],
        out_specs=(anywhere, anywhere),
        scratch_shapes=[pltpu.SemaphoreType.DMA((2,))],
        compiler_params=pltpu.CompilerParams(vmem_limit_bytes=56 * 1024 * 1024),
    )(w, chi)
    return w[None], chi


def solution(mesh, g2=4):
    placed = (P(None, None, "space", None), P("src", None, "space", None), P("src", None))
    return jax.shard_map(
        functools.partial(on_device, mesh.shape["src"], mesh.shape["space"] // g2, g2),
        mesh=mesh,
        in_specs=placed,
        out_specs=(P("src", None, None, "space", None), P(None, None, "space", None)),
        check_vma=False,
    )
```

```python
import functools
import math

import jax
import jax.numpy as jnp
import ml_dtypes
import numpy as np
from jax import lax
from jax.experimental import pallas as pl
from jax.experimental.pallas import tpu as pltpu
from jax.sharding import PartitionSpec as P

OUTER = 2
WAVENUMBER = 2.0 * math.pi / 6.0
DAMPING = 0.3
SOURCE_GAP = 8.0
FLOOR_SHARE = 0.75
REAL_LOW = -0.25
REAL_HIGH = 0.35
IMAG_HIGH = 0.1
F32 = jnp.float32
BF16 = jnp.bfloat16
MESH = pl.DeviceIdType.MESH


def hartley(length):
    turn = np.outer(np.arange(length), np.arange(length)) % length
    angle = 2.0 * np.pi / length * turn
    return (np.cos(angle) + np.sin(angle)) / np.sqrt(length)


def high_low(table):
    high = table.astype(ml_dtypes.bfloat16)
    low = (table - high.astype(np.float64)).astype(ml_dtypes.bfloat16)
    return np.stack([high, low])


def modes(length):
    return 4.0 * np.sin(np.pi * np.arange(length) / length) ** 2


def decay_tables(depth, across):
    wave_sq = WAVENUMBER * WAVENUMBER
    trace = 2.0 + modes(depth)[:, None] + modes(across)[None, :] - wave_sq * (1.0 + 1j * DAMPING)
    root = np.sqrt(trace * trace - 4.0)
    first = (trace - root) / 2.0
    second = (trace + root) / 2.0
    small = np.where(np.abs(first) < np.abs(second), first, second)
    large = np.where(np.abs(first) < np.abs(second), second, first)
    small = 1.0 / large
    kappa = wave_sq / (large - small)
    tables = np.stack([small.real, small.imag, kappa.real, kappa.imag])
    return tables.astype(np.float32)


def cmul(a, b):
    return (a[0] * b[0] - a[1] * b[1], a[0] * b[1] + a[1] * b[0])


def cmadd(a, b, c):
    return (a[0] * b[0] - a[1] * b[1] + c[0], a[0] * b[1] + a[1] * b[0] + c[1])


def half_turn(fraction):
    angle = fraction * math.pi
    sq = angle * angle
    sine = jnp.full_like(sq, -1.0 / math.factorial(11))
    for order in (9, 7, 5, 3, 1):
        sine = sine * sq + (1.0 if order % 4 == 1 else -1.0) / math.factorial(order)
    cosine = jnp.full_like(sq, 1.0 / math.factorial(12))
    for order in (10, 8, 6, 4, 2, 0):
        cosine = cosine * sq + (1.0 if order % 4 == 0 else -1.0) / math.factorial(order)
    return sine * angle, cosine


def kernel(
    cfg,
    pos_ref, meas_ref, contrast_hbm, tab_hbm, hy_hbm, hz_hbm,
    w_hbm, chi_hbm,
    chi0_ref, tab_ref, hy_ref, hz_ref, w_ref, chi2_ref, chi1_ref, e_ref, s_ref, r_ref, d_ref, v_ref, b_ref, sp_all, rho_ref, early_ref, early_recv, late_ref, late_recv,
    send0_all, send1_all, send3_all, states_all, sums, recv1, recv2, recv3, recv4, red1, red2,
    ex_send, ex_recv, red_send, red_recv, x_send, x_recv, late_send, late_took, chi_took, local_sem,
):
    ns, g1, g2, nz, ny, rows = cfg
    halves = ny // 128
    nx = g1 * g2 * rows
    zgroups = nz // 8
    src = lax.axis_index("src")
    space = lax.axis_index("space")
    m = lax.rem(space, g1)
    chips = g1 // 2
    core = lax.rem(m, 2)
    chip = m // 2
    far_first = (6, 2, 5, 3, 7, 1, 4)
    grp = space // g1
    base = grp * g1

    partner = (src, space + 1 - 2 * core)

    for x in range(rows):
        for c in range(2):
            pltpu.make_async_copy(
                contrast_hbm.at[c, :, x, :], chi0_ref.at[x, pl.ds(c * nz, nz), :], local_sem.at[0]
            ).start()
    pltpu.make_async_copy(hz_hbm, hz_ref, local_sem.at[1]).start()
    pltpu.make_async_copy(hy_hbm, hy_ref, local_sem.at[2]).start()
    pltpu.make_async_copy(tab_hbm, tab_ref, local_sem.at[3]).start()

    barrier = pltpu.get_barrier_semaphore()

    zs = g1 * g2 // 8
    z_at, y_at = space // 8, lax.rem(space // 2, 4)

    def column_peer(k):
        return src, (lax.rem(z_at + k // 2, zs) * 4 + y_at) * 2 + lax.rem(core + k, 2)

    def plane_peer(k):
        return lax.rem(src + k // 4, ns), (z_at * 4 + lax.rem(y_at + k, 4)) * 2 + core

    def greet_column(k, carry):
        pl.semaphore_signal(barrier, inc=1, device_id=column_peer(k), device_id_type=MESH)
        return carry

    def greet_plane(k, carry):
        pl.semaphore_signal(barrier, inc=1, device_id=plane_peer(k), device_id_type=MESH)
        return carry

    def greet_diagonal(k, carry):
        z_other = z_at + 1 - 2 * lax.rem(z_at, 2)
        pl.semaphore_signal(barrier, inc=1, device_id=(src, (z_other * 4 + lax.rem(y_at + k, 4)) * 2 + core),
                            device_id_type=MESH)
        return carry

    lax.fori_loop(1, 2 * zs, greet_column, 0)
    lax.fori_loop(1, 4 * ns, greet_plane, 0)
    lax.fori_loop(1, 4, greet_diagonal, 0)

    def remote(src_ref, dst_ref, send_sem, recv_sem, device):
        return pltpu.make_async_remote_copy(
            src_ref=src_ref, dst_ref=dst_ref, send_sem=send_sem, recv_sem=recv_sem,
            device_id=device, device_id_type=MESH,
        )

    def take(ref, sem):
        pltpu.make_async_copy(ref, ref, sem).wait()

    def reduce_start(a, parts):
        red1[a, 0] = jnp.concatenate(parts + [jnp.zeros((8 - len(parts), 128), F32)], axis=0)

        def send(n, carry):
            k = lax.rem(n + zs - 2, 2 * zs - 1) + 1
            remote(red1.at[a, 0], red1.at[a, k], red_send.at[a, 0], red_recv.at[a, 0], column_peer(k)).start()
            return carry

        lax.fori_loop(1, 2 * zs, send, 0)

    def reduce_middle(a):
        take(red1.at[a, pl.ds(1, 2 * zs - 1)], red_recv.at[a, 0])

        def add(j, total):
            slot = lax.rem(z_at - j // 2 + zs, zs) * 2 + lax.rem(core + j, 2)
            return total + red1[a, slot]

        red2[a, 0] = lax.fori_loop(0, 2 * zs, add, jnp.zeros((8, 128), F32), unroll=True)

        def send(n, carry):
            k = lax.rem(n + 2 * ns, 4 * ns - 1) + 1
            remote(red2.at[a, 0], red2.at[a, k], red_send.at[a, 1], red_recv.at[a, 1], plane_peer(k)).start()
            return carry

        lax.fori_loop(1, 4 * ns, send, 0)
        take(red1.at[a, pl.ds(1, 2 * zs - 1)], red_send.at[a, 0])

    def reduce_end(a):
        take(red2.at[a, pl.ds(1, 4 * ns - 1)], red_recv.at[a, 1])

        def add(j, total):
            slot = lax.rem(src - j // 4 + ns, ns) * 4 + lax.rem(y_at - lax.rem(j, 4) + 4, 4)
            return total + red2[a, slot]

        total = lax.fori_loop(0, 4 * ns, add, jnp.zeros((8, 128), F32), unroll=True)
        take(red2.at[a, pl.ds(1, 4 * ns - 1)], red_send.at[a, 1])
        return jnp.sum(total, axis=1, keepdims=True)

    def fold(acc):
        part = acc[:, :128]
        for h in range(1, halves):
            part = part + acc[:, h * 128:(h + 1) * 128]
        return jnp.sum(part, axis=0, keepdims=True)

    def split(a):
        high = a.astype(BF16)
        return high, (a - high.astype(F32)).astype(BF16)

    def dot3(a, b):
        mm = functools.partial(jnp.dot, preferred_element_type=F32)
        return mm(a[0], b[0]) + (mm(a[1], b[0]) + mm(a[0], b[1]))

    def local_pair(src_ref, dst_ref, n):
        at = pl.ds(2 * n, 2)
        depth_done = dot3((hz_ref[0], hz_ref[1]), split(src_ref[at].reshape(4 * nz, ny)))
        dst_ref[at] = dot3(split(depth_done), (hy_ref[0], hy_ref[1])).reshape(2, 2 * nz, ny)

    def local(src_ref, dst_ref):
        for n in range(rows // 2):
            local_pair(src_ref, dst_ref, n)

    def tile(ref, lead, part, comp):
        z = pl.multiple_of(part // halves * 8, 8)
        y = pl.multiple_of(lax.rem(part, halves) * 128, 128)
        return ref.at[lead, pl.ds(comp * nz + z, 8), pl.ds(y, 128)]

    def ctable(part, which):
        z = pl.multiple_of(part // halves * 8, 8)
        y = pl.multiple_of(lax.rem(part, halves) * 128, 128)
        return tuple(tab_ref[2 * which + c, pl.ds(z, 8), pl.ds(y, 128)] for c in range(2))

    def spectral(sp_ref, lead, part):
        return (tile(sp_ref, lead, part, 0)[...], tile(sp_ref, lead, part, 1)[...])

    def sweep_out(t, extra=None):
        sp_ref, send0, send1 = sp_all.at[t % 2], send0_all.at[t % 2], send1_all.at[t % 2]

        def summarise(part):
            root = ctable(part, 0)
            rowv = [spectral(sp_ref, i, part) for i in range(rows)]
            if extra is not None:
                rowv = [extra(i, part, value) for i, value in enumerate(rowv)]
                for i in range(rows):
                    tile(sp_ref, i, part, 0)[...] = rowv[i][0]
                    tile(sp_ref, i, part, 1)[...] = rowv[i][1]
            ahead = rowv[0]
            for i in range(1, rows):
                ahead = cmadd(ahead, root, rowv[i])
            behind = rowv[rows - 1]
            for i in range(rows - 2, -1, -1):
                behind = cmadd(behind, root, rowv[i])
            return ahead + behind

        def other_half(k, carry):
            g = lax.rem(chip + k, chips)
            vals = summarise(2 * g + 1 - core)
            for c in range(4):
                send0[g, c] = vals[c]
            remote(send0.at[g], sums.at[t, core, g], ex_send.at[t, 0], ex_recv.at[t, 0], partner).start()
            return carry

        def own_half(k, carry):
            g = lax.rem(chip + k, chips)
            vals = summarise(2 * g + core)
            for c in range(4):
                sums[t, core, g, c] = vals[c]
            return carry

        lax.fori_loop(1, chips + 1, other_half, 0, unroll=4)
        lax.fori_loop(1, chips + 1, own_half, 0, unroll=4)
        take(sums.at[t, 1 - core], ex_recv.at[t, 0])

        def combine(g):
            block_root = power(ctable(2 * g + core, 0), int(math.log2(rows)))
            first = [sums[t, 0, g, c] for c in range(4)]
            second = [sums[t, 1, g, c] for c in range(4)]
            return cmadd(first[:2], block_root, second[:2]) + cmadd(second[2:], block_root, first[2:])

        def step(k, carry):
            g = lax.rem(chip + k, chips)
            vals = combine(g)
            for c in range(4):
                send1[g, c] = vals[c]
            remote(send1.at[g], recv1.at[t, k], ex_send.at[t, 1], ex_recv.at[t, 1],
                   (src, base + 2 * g + core)).start()
            return carry

        for k in far_first:
            step(k, 0)
        vals = combine(chip)
        for c in range(4):
            recv1[t, 0, c] = vals[c]

    def power(value, doublings):
        for _ in range(doublings):
            value = cmul(value, value)
        return value

    def own_root():
        return ctable(m, 0)

    def chip_root():
        return power(own_root(), int(math.log2(2 * rows)))

    def middle_out(t):
        take(recv1.at[t, pl.ds(1, chips - 1)], ex_recv.at[t, 1])
        root = chip_root()

        def gather(j, carry):
            ahead, behind = carry
            slot_a = lax.rem(chip - j + chips, chips)
            slot_b = lax.rem(chip + 1 + j, chips)
            ahead = cmadd(ahead, root, (recv1[t, slot_a, 0], recv1[t, slot_a, 1]))
            behind = cmadd(behind, root, (recv1[t, slot_b, 2], recv1[t, slot_b, 3]))
            return ahead, behind

        zero = jnp.zeros((8, 128), F32)
        ahead, behind = lax.fori_loop(0, chips, gather, ((zero, zero), (zero, zero)), unroll=True)
        for c, value in enumerate(ahead + behind):
            recv2[t, 0, c] = value

        def send(k, carry):
            peer = lax.rem(grp + k, g2) * g1 + m
            remote(recv2.at[t, 0], recv2.at[t, k], ex_send.at[t, 2], ex_recv.at[t, 2], (src, peer)).start()
            return carry

        for k in (2, 1, 3):
            send(k, 0)

    def middle_back(t):
        send3 = send3_all.at[t % 2]
        root = chip_root()
        group_root = power(root, int(math.log2(chips)))
        turn = power(group_root, int(math.log2(g2)))
        real, imag = 1.0 - turn[0], turn[1]
        norm = 1.0 / (real * real + imag * imag)
        inverse = (real * norm, imag * norm)
        take(recv2.at[t, pl.ds(1, g2 - 1)], ex_recv.at[t, 2])
        left = (recv2[t, 0, 0], recv2[t, 0, 1])
        right = (recv2[t, 0, 2], recv2[t, 0, 3])
        for k in range(g2 - 1, 0, -1):
            left = cmadd(left, group_root, (recv2[t, k, 0], recv2[t, k, 1]))
            right = cmadd(right, group_root, (recv2[t, g2 - k, 2], recv2[t, g2 - k, 3]))
        left = cmul(left, inverse)
        right = cmul(right, inverse)

        def spread(j, carry):
            left, right = carry
            back = chips - 1 - j
            for c in range(2):
                send3[j, c] = left[c]
                send3[back, 2 + c] = right[c]
            slot_a = lax.rem(chip - j + chips, chips)
            slot_b = lax.rem(chip + 1 + j, chips)
            left = cmadd(left, root, (recv1[t, slot_a, 0], recv1[t, slot_a, 1]))
            right = cmadd(right, root, (recv1[t, slot_b, 2], recv1[t, slot_b, 3]))
            return left, right

        lax.fori_loop(0, chips, spread, (left, right), unroll=True)

        def send(k, carry):
            g = lax.rem(chip + k, chips)
            remote(send3.at[g], recv3.at[t, k], ex_send.at[t, 3], ex_recv.at[t, 3],
                   (src, base + 2 * g + core)).start()
            return carry

        for k in far_first:
            send(k, 0)
        for c in range(4):
            recv3[t, 0, c] = send3[chip, c]

    def sweep_back(t):
        sp_ref, states = sp_all.at[t % 2], states_all.at[t % 2]
        take(recv3.at[t, pl.ds(1, chips - 1)], ex_recv.at[t, 3])

        def pass_on(k, carry):
            g = lax.rem(chip - k + chips, chips)
            block_root = power(ctable(2 * g + core, 0), int(math.log2(rows)))
            left = (recv3[t, k, 0], recv3[t, k, 1])
            right = (recv3[t, k, 2], recv3[t, k, 3])
            inner_left = cmadd(left, block_root, (sums[t, 0, g, 0], sums[t, 0, g, 1]))
            inner_right = cmadd(right, block_root, (sums[t, 1, g, 2], sums[t, 1, g, 3]))
            for c in range(2):
                states[0, g, c] = left[c]
                states[0, g, 2 + c] = inner_right[c]
                states[1, g, c] = inner_left[c]
                states[1, g, 2 + c] = right[c]
            remote(states.at[1 - core, g], recv4.at[t, g], ex_send.at[t, 4], ex_recv.at[t, 4], partner).start()
            return carry

        lax.fori_loop(0, chips, pass_on, 0, unroll=4)

        def apply(part, ends):
            root = ctable(part, 0)
            kappa = ctable(part, 1)
            rowv = [spectral(sp_ref, i, part) for i in range(rows)]
            state = ends[:2]
            ahead = []
            for i in range(rows):
                state = cmadd(state, root, rowv[i])
                ahead.append(state)
            state = cmul(ends[2:], root)
            for i in range(rows - 1, -1, -1):
                total = cmul((ahead[i][0] + state[0], ahead[i][1] + state[1]), kappa)
                tile(sp_ref, i, part, 0)[...] = total[0]
                tile(sp_ref, i, part, 1)[...] = total[1]
                if i:
                    state = cmul((state[0] + rowv[i][0], state[1] + rowv[i][1]), root)

        def own_half(g, carry):
            apply(2 * g + core, tuple(states[core, g, c] for c in range(4)))
            return carry

        def other_half(g, carry):
            apply(2 * g + 1 - core, tuple(recv4[t, g, c] for c in range(4)))
            return carry

        lax.fori_loop(0, chips, own_half, 0, unroll=4)
        take(recv4.at[t], ex_recv.at[t, 4])
        lax.fori_loop(0, chips, other_half, 0, unroll=4)

    def finish(t):
        take(recv4.at[t], ex_send.at[t, 0])
        take(recv1.at[t, pl.ds(1, chips - 1)], ex_send.at[t, 1])
        take(recv2.at[t, pl.ds(1, g2 - 1)], ex_send.at[t, 2])
        take(recv3.at[t, pl.ds(1, chips - 1)], ex_send.at[t, 3])
        take(recv4.at[t], ex_send.at[t, 4])

    def pair(ref, x, z):
        return (ref[x, pl.ds(z, 8), :], ref[x, pl.ds(nz + z, 8), :])

    def put(ref, x, z, value):
        ref[x, pl.ds(z, 8), :] = value[0]
        ref[x, pl.ds(nz + z, 8), :] = value[1]

    def each_block(body, init):
        def outer(n, carry):
            return body(n // zgroups, pl.multiple_of(lax.rem(n, zgroups) * 8, 8), carry)

        return lax.fori_loop(0, rows * zgroups, outer, init, unroll=4)

    def square(value):
        return value[0] * value[0] + value[1] * value[1]

    zero = jnp.zeros((8, ny), F32)
    source_x = pos_ref[0, 0].astype(F32)
    source_y = pos_ref[0, 1].astype(F32)
    offset_y = lax.broadcasted_iota(jnp.int32, (8, ny), 1).astype(F32) - source_y
    offset_y_sq = offset_y * offset_y
    level = lax.broadcasted_iota(jnp.int32, (8, ny), 0).astype(F32) + SOURCE_GAP

    def begin(x, z, carry):
        height = level + z.astype(F32)
        offset_x = (space * rows + x).astype(F32) - source_x
        dist = jnp.sqrt(height * height + offset_x * offset_x + offset_y_sq)
        turns = dist * (1.0 / 6.0)
        sine, cosine = half_turn(turns - jnp.floor(turns + 0.5))
        wave = (1.0 - 2.0 * sine * sine, 2.0 * sine * cosine)
        put(e_ref, x, z, wave)
        return carry

    def excite(x, z, total):
        field = cmul(pair(chi0_ref, x, z), pair(e_ref, x, z))
        put(w_ref, x, z, field)
        return total + square(field)

    each_block(begin, 0)
    take(chi0_ref, local_sem.at[0])
    object_part = each_block(excite, zero)
    data_part = jnp.zeros((1, ny), F32)
    for x in range(rows):
        for c in range(2):
            data_part = data_part + meas_ref[c, pl.ds(x, 1), :] * meas_ref[c, pl.ds(x, 1), :]
    data_fold = data_part[:, :128]
    for h in range(1, halves):
        data_fold = data_fold + data_part[:, h * 128:(h + 1) * 128]

    take(hz_ref, local_sem.at[1])
    take(hy_ref, local_sem.at[2])
    local(w_ref, sp_all.at[0])
    take(tab_ref, local_sem.at[3])
    pl.semaphore_wait(barrier, (2 * zs - 1) + (4 * ns - 1) + 3)
    sweep_out(0)
    reduce_start(0, [data_fold, fold(object_part)])
    middle_out(0)
    reduce_middle(0)
    middle_back(0)
    totals = reduce_end(0)
    sweep_back(0)
    finish(0)
    local(sp_all.at[0], s_ref)
    data_total = totals[0:1]
    object_share = totals[1:2] / data_total
    ratio = 0.5 / DAMPING
    level_zero = 1.0 / math.sqrt(nz)
    chi_ref = chi0_ref
    for update in range(OUTER):
        t = 1 + 2 * update
        a = 1 + 2 * update
        last = update == OUTER - 1
        chi_next = chi2_ref if last else chi1_ref
        early, late = early_recv.at[update], late_recv.at[update]
        right, left, across = (lax.rem(src + k, ns) for k in (1, 3, 2))

        own_pair = src // 2
        mate = src + 1 - 2 * lax.rem(src, 2)
        first, second = sp_all.at[t % 2], sp_all.at[(t + 1) % 2]
        for place, x in enumerate((src, mate, lax.rem(mate + 2, ns), across)):
            k = lax.rem(x - src + ns, ns)
            if update and place:
                take(chi_ref.at[0], chi_took.at[update - 1, ns - k])

            def residual(n, carry, x=x, chi_ref=chi_ref):
                z = pl.multiple_of(n * 8, 8)
                chi = pair(chi_ref, x, z)
                e, s, w = pair(e_ref, x, z), pair(s_ref, x, z), pair(w_ref, x, z)
                u = (e[0] + s[0], e[1] + s[1])
                field = cmul(chi, u)
                res = (field[0] - w[0], field[1] - w[1])
                put(r_ref, x, z, res)
                flipped = cmul(chi, (res[0], -res[1]))
                put(v_ref, x, z, (-flipped[0], -flipped[1]))
                put(b_ref, x, z, (res[0] + ratio * flipped[1], res[1] + ratio * flipped[0]))
                early_ref[x, pl.ds(z, 8), :] = w[0] * u[0] + w[1] * u[1]
                early_ref[x, pl.ds(nz + z, 8), :] = w[1] * u[0] - w[0] * u[1]
                early_ref[x, pl.ds(2 * nz + z, 8), :] = square(u)
                return carry

            lax.fori_loop(0, zgroups, residual, 0, unroll=4)
            if place:
                remote(early_ref.at[x], early.at[k], x_send.at[update, 0], x_recv.at[update, 0], (x, space)).start()
            if update and place == 1:
                local_pair(v_ref, first, own_pair)
                local_pair(b_ref, second, own_pair)
        rho = jnp.concatenate(
            [
                meas_ref[c, pl.ds(x, 1), :] - s_ref[x, pl.ds(c * nz, 1), :]
                for x in range(rows) for c in range(2)
            ],
            axis=0,
        )
        rho_ref[...] = level_zero * dot3(split(rho), (hy_ref[0], hy_ref[1]))

        if not update:
            local(v_ref, first)
        else:
            local_pair(v_ref, first, 1 - own_pair)
            local_pair(b_ref, second, 1 - own_pair)
            object_share = float(ns) * reduce_end(2)[0:1] / data_total

        def rho_tile(i, part, c, object_share=object_share):
            y = pl.multiple_of(lax.rem(part, halves) * 128, 128)
            return object_share * rho_ref[pl.ds(2 * i + c, 1), pl.ds(y, 128)]

        def add_first(i, part, value, rho_tile=rho_tile):
            return value[0] + rho_tile(i, part, 0), value[1] - rho_tile(i, part, 1)

        def add_second(i, part, value, rho_tile=rho_tile):
            return value[0] + ratio * rho_tile(i, part, 1), value[1] - ratio * rho_tile(i, part, 0)

        sweep_out(t, add_first)
        if not update:
            local(b_ref, second)
        sweep_out(t + 1, add_second)
        middle_out(t)
        middle_out(t + 1)
        middle_back(t)
        middle_back(t + 1)
        sweep_back(t)
        local(first, d_ref)
        sweep_back(t + 1)
        local_pair(second, v_ref, 1 - own_pair)

        def pass_late(row, half, place, device, update=update, late=late):
            remote(late_ref.at[row, half], late.at[place, half], late_send.at[update, place, half],
                   late_took.at[update, place, half], (device, space)).start()

        def add_late(row, half, update=update, late=late):
            take(late.at[0, half], late_took.at[update, 0, half])

            def add(n, carry):
                at = pl.ds(pl.multiple_of(n * 8, 8), 8)
                late_ref[row, half, at, :] = late_ref[row, half, at, :] + late[0, half, at, :]
                return carry

            lax.fori_loop(0, 3 * zgroups, add, 0, unroll=8)

        totals = (zero, zero)
        for k in (2, 1, 3, 0):
            x = lax.rem(src + k, ns)
            if k == 1:
                local_pair(second, v_ref, own_pair)

            def descend(n, totals, x=x, chi_ref=chi_ref):
                z = pl.multiple_of(n * 8, 8)
                res, image, other = pair(r_ref, x, z), pair(d_ref, x, z), pair(v_ref, x, z)
                d = (res[0] + image[0], res[1] - image[1])
                h = (other[0] + ratio * image[1], other[1] + ratio * image[0])
                put(d_ref, x, z, d)
                put(v_ref, x, z, h)
                moved = cmul(pair(chi_ref, x, z), h)
                e, s, w = pair(e_ref, x, z), pair(s_ref, x, z), pair(w_ref, x, z)
                u = (e[0] + s[0], e[1] + s[1])
                late_parts = (
                    d[0] * u[0] + d[1] * u[1] + (w[0] * h[0] + w[1] * h[1]),
                    d[1] * u[0] - d[0] * u[1] + (w[1] * h[0] - w[0] * h[1]),
                    2.0 * (u[0] * h[0] + u[1] * h[1]),
                    d[0] * h[0] + d[1] * h[1],
                    d[1] * h[0] - d[0] * h[1],
                    square(h),
                )
                half = n // (zgroups // 2)
                for c, value in enumerate(late_parts):
                    late_ref[x, half, pl.ds(c * (nz // 2) + z - half * (nz // 2), 8), :] = value
                return totals[0] + square(d), totals[1] + square((d[0] - moved[0], d[1] - moved[1]))

            totals = lax.fori_loop(0, zgroups, descend, totals, unroll=4)
            if k == 2:
                pass_late(across, 0, 0, right)
                pass_late(across, 1, 0, left)
            elif k == 1:
                pass_late(right, 1, 1, right)
            elif k == 3:
                pass_late(left, 0, 2, left)
        finish(t)
        finish(t + 1)
        image_part = jnp.zeros((1, ny), F32)
        for x in range(rows):
            image_part = image_part + square((v_ref[x, pl.ds(0, 1), :], v_ref[x, pl.ds(nz, 1), :]))
        image_fold = image_part[:, :128]
        for h in range(1, halves):
            image_fold = image_fold + image_part[:, h * 128:(h + 1) * 128]
        reduce_start(a, [fold(totals[0]), image_fold, fold(totals[1])])
        take(early.at[pl.ds(1, ns - 1)], x_recv.at[update, 0])

        def gather_early(n, carry, early=early):
            at = pl.ds(pl.multiple_of(n * 8, 8), 8)
            early_ref[src, at, :] = early_ref[src, at, :] + early[1, at, :] + early[2, at, :] + early[3, at, :]
            return carry

        lax.fori_loop(0, 3 * zgroups, gather_early, 0, unroll=4)
        reduce_middle(a)
        add_late(right, 0)
        pass_late(right, 0, 1, right)
        add_late(left, 1)
        pass_late(left, 1, 2, left)
        totals = reduce_end(a)
        length = totals[0:1] / (object_share * totals[1:2] + totals[2:3])

        def advance(x, z, carry, length=length, last=last):
            w, d = pair(w_ref, x, z), pair(d_ref, x, z)
            put(w_ref, x, z, (w[0] + length * d[0], w[1] + length * d[1]))
            if not last:
                s, h = pair(s_ref, x, z), pair(v_ref, x, z)
                put(s_ref, x, z, (s[0] + length * h[0], s[1] + length * h[1]))
            return carry

        each_block(advance, 0)
        if last:
            for x in range(rows):
                for c in range(2):
                    at = pl.ds(c * nz, nz)
                    pltpu.make_async_copy(w_ref.at[x, at, :], w_hbm.at[x, at, :], local_sem.at[4]).start()
        for half in range(2):
            for place in (1, 2):
                take(late.at[place, half], late_took.at[update, place, half])

        def contrast(n, total, length=length, late=late, chi_next=chi_next):
            z = pl.multiple_of(n * 8, 8)
            terms = []
            half = n // (zgroups // 2)
            for c in range(6):
                at = pl.ds(c * (nz // 2) + z - half * (nz // 2), 8)
                terms.append(late_ref[src, half, at, :] + late[1, half, at, :] + late[2, half, at, :])
            parts = [
                early_ref[src, pl.ds(c * nz + z, 8), :] + length * (terms[c] + length * terms[3 + c]) for c in range(3)
            ]
            scale = 1.0 / jnp.maximum(parts[2], FLOOR_SHARE * ns)
            chi = (jnp.clip(parts[0] * scale, REAL_LOW, REAL_HIGH), jnp.clip(parts[1] * scale, 0.0, IMAG_HIGH))
            put(chi_next, src, z, chi)
            return total + square(chi)

        chi_part = lax.fori_loop(0, zgroups, contrast, zero, unroll=2)
        if not last:
            reduce_start(2, [fold(chi_part)])
        for k in (2, 1, 3):
            remote(chi_next.at[src], chi_next.at[src], x_send.at[update, 1], chi_took.at[update, k],
                   (lax.rem(src + k, ns), space)).start()
        if not last:
            reduce_middle(2)
        else:
            for k in (0, 1, 3, 2):
                x = lax.rem(src + k, ns)
                if k:
                    take(chi_next.at[0], chi_took.at[update, ns - k])
                for c in range(2):
                    at = pl.ds(c * nz, nz)
                    pltpu.make_async_copy(chi_next.at[x, at, :], chi_hbm.at[x, at, :], local_sem.at[5]).start()
        take(early.at[pl.ds(1, ns - 1)], x_send.at[update, 0])
        for half in range(2):
            for place in range(3):
                take(late.at[place, half], late_send.at[update, place, half])
        chi_ref = chi_next
    for update in range(OUTER):
        take(chi2_ref.at[pl.ds(0, ns - 1)], x_send.at[update, 1])
    take(w_ref, local_sem.at[4])
    take(chi2_ref, local_sem.at[5])


def unfold(w_ref, chi_ref, w_out, chi_out, sem):
    for n, (src_ref, dst_ref) in enumerate(((w_ref, w_out), (chi_ref, chi_out))):
        rows, nz = src_ref.shape[0], src_ref.shape[1] // 2
        for x in range(rows):
            for c in range(2):
                pltpu.make_async_copy(src_ref.at[x, pl.ds(c * nz, nz), :], dst_ref.at[c, :, x, :], sem.at[n]).start()
    pltpu.make_async_copy(w_ref, w_ref, sem.at[0]).wait()
    pltpu.make_async_copy(chi_ref, chi_ref, sem.at[1]).wait()


def on_device(ns, g1, g2, contrast, measured, positions):
    _, nz, rows, ny = contrast.shape
    cfg = (ns, g1, g2, nz, ny, rows)
    transforms = 1 + 2 * OUTER
    reductions = 2 * OUTER
    tables = decay_tables(nz, ny)
    hy = high_low(hartley(ny))
    hz = high_low(np.kron(np.eye(4), hartley(nz)))
    field = (rows, 2 * nz, ny)
    vmem = pl.BlockSpec(memory_space=pltpu.VMEM)
    anywhere = pl.BlockSpec(memory_space=pltpu.HBM)
    w, chi = pl.pallas_call(
        functools.partial(kernel, cfg),
        out_shape=(jax.ShapeDtypeStruct(field, F32), jax.ShapeDtypeStruct(field, F32)),
        in_specs=[pl.BlockSpec(memory_space=pltpu.SMEM), vmem] + [anywhere] * 4,
        out_specs=(anywhere, anywhere),
        scratch_shapes=[
            pltpu.VMEM(field, F32),
            pltpu.VMEM(tables.shape, F32),
            pltpu.VMEM(hy.shape, BF16),
            pltpu.VMEM(hz.shape, BF16),
        ] + [pltpu.VMEM(field, F32)] * 9 + [
            pltpu.VMEM((2,) + field, F32),
            pltpu.VMEM((2 * rows, ny), F32),
            pltpu.VMEM((rows, 3 * nz, ny), F32),
            pltpu.VMEM((OUTER, ns, 3 * nz, ny), F32),
            pltpu.VMEM((rows, 2, 3 * nz, ny), F32),
            pltpu.VMEM((OUTER, 3, 2, 3 * nz, ny), F32),
            pltpu.VMEM((2, g1 // 2, 4, 8, 128), F32),
            pltpu.VMEM((2, g1 // 2, 4, 8, 128), F32),
            pltpu.VMEM((2, g1 // 2, 4, 8, 128), F32),
            pltpu.VMEM((2, 2, g1 // 2, 4, 8, 128), F32),
            pltpu.VMEM((transforms, 2, g1 // 2, 4, 8, 128), F32),
            pltpu.VMEM((transforms, g1 // 2, 4, 8, 128), F32),
            pltpu.VMEM((transforms, g2, 4, 8, 128), F32),
            pltpu.VMEM((transforms, g1 // 2, 4, 8, 128), F32),
            pltpu.VMEM((transforms, g1 // 2, 4, 8, 128), F32),
            pltpu.VMEM((reductions, g1 * g2 // 4, 8, 128), F32),
            pltpu.VMEM((reductions, 4 * ns, 8, 128), F32),
            pltpu.SemaphoreType.DMA((transforms, 5)),
            pltpu.SemaphoreType.DMA((transforms, 5)),
            pltpu.SemaphoreType.DMA((reductions, 2)),
            pltpu.SemaphoreType.DMA((reductions, 2)),
            pltpu.SemaphoreType.DMA((OUTER, 2)),
            pltpu.SemaphoreType.DMA((OUTER, 2)),
            pltpu.SemaphoreType.DMA((OUTER, 3, 2)),
            pltpu.SemaphoreType.DMA((OUTER, 3, 2)),
            pltpu.SemaphoreType.DMA((OUTER, ns)),
            pltpu.SemaphoreType.DMA((6,)),
        ],
        compiler_params=pltpu.CompilerParams(
            collective_id=0, has_side_effects=True, vmem_limit_bytes=56 * 1024 * 1024
        ),
    )(positions, measured[0], contrast, tables, hy, hz)
    w, chi = pl.pallas_call(
        unfold,
        out_shape=(jax.ShapeDtypeStruct(contrast.shape, F32), jax.ShapeDtypeStruct(contrast.shape, F32)),
        in_specs=[vmem, vmem],
        out_specs=(anywhere, anywhere),
        scratch_shapes=[pltpu.SemaphoreType.DMA((2,))],
        compiler_params=pltpu.CompilerParams(vmem_limit_bytes=56 * 1024 * 1024),
    )(w, chi)
    return w[None], chi


def solution(mesh, g2=4):
    placed = (P(None, None, "space", None), P("src", None, "space", None), P("src", None))
    return jax.shard_map(
        functools.partial(on_device, mesh.shape["src"], mesh.shape["space"] // g2, g2),
        mesh=mesh,
        in_specs=placed,
        out_specs=(P("src", None, None, "space", None), P(None, None, "space", None)),
        check_vma=False,
    )
```
